32 devices in a mesh: patch: 8 (over y, x, core), grp: 4 (over z).
Axes of the slice: x: 2, y: 2, z: 4, core: 2. Of those that a mesh axis runs over, the one named last changes fastest.
Arguments:
- cells: int32 [3, 8, 4, 32, 128], P(None, 'patch', 'grp'), may hold values from 0 to 15, as said below
- offsets: float32 [3, 8, 4, 32, 128], P(None, 'patch', 'grp'), may hold values from -0.5 to 0.5
- charges: float32 [8, 4, 32, 128], P('patch', 'grp'), may hold values from -4 to 4
- masses: float32 [8, 4, 32, 128], P('patch', 'grp'), may hold values from 1 to 16
- velocity: float32 [3, 8, 4, 32, 128], P(None, 'patch', 'grp'), may hold values from -5 to 5
- task_first: int32 [8, 4, 32], P('patch', 'grp'), may hold values from 0 to 127, as said below
- task_second: int32 [8, 4, 32], P('patch', 'grp'), may hold values from 0 to 255, as said below
- task_count: int32 [8, 4], P('patch', 'grp'), may hold values from 0 to 32, as said below
- kernel_taps: float32 [6, 17], replicated, may hold values from -3 to 3
Outputs:
- displacement: float32 [3, 8, 4, 32, 128], P(None, 'patch', 'grp')
- velocities: float32 [3, 8, 4, 32, 128], P(None, 'patch', 'grp')
The draws below stay inside these ranges and needn't reach their ends.
Inputs may be any that keep to these rules, and one draw needn't show every extreme that they name: `cells`: components x, y, z lie below 8, 16, 8. `task_first`: A patch of the host's slab, written strip * 32 + place. `task_second`: slab step * 4 * 32 + strip * 32 + place of one of the 13 forward neighbours of the first patch, periodic: in the next slab any of the 9 with strip and place within one; in the same slab strip + 0 with place + 1, or strip + 1 with place within one. A pair may repeat. `task_count`: on each slab the 4 counts add up to exactly 64; every slab has one device with 32 live slots and one with none. Slots at or past the count are ignored.
All inputs are finite; a program needn't handle non-finite values.
Results may differ from the reference program's by a relative error of at most 0.000068.
Values sent between devices are 32-bit elements; how exact they have to be, the bound alone decides.
No kernel may reach another device: no remote copies, remote signals or barrier semaphores. Data moves between devices by JAX's collectives and lax.ppermute only.
A program may use at most 64 MiB of HBM per device.

```python
import math
import jax
import jax.numpy as jnp
import numpy as np
from jax import lax

ATOMS = 128
MXD = 8
MYD = 16
PZ = 8
MZ = 256
TERMS = 6
RADIUS = 8
TASK_DEV = 32
PLACES = 32
SLABS = 8
STRIPS = 4
NX = 64
NY = 64


forward_slab = np.array([1, 1, 1, 1, 1, 1, 1, 1, 1, 0, 0, 0, 0], np.int32)


forward_strip = np.array([-1, -1, -1, 0, 0, 0, 1, 1, 1, 0, 1, 1, 1], np.int32)


forward_place = np.array([-1, 0, 1, -1, 0, 1, -1, 0, 1, 1, -1, 0, 1], np.int32)


def draw_cells(key, part):
    keys = jax.random.split(jax.random.fold_in(key, 3), 3)
    shape = (SLABS, STRIPS, PLACES, ATOMS)
    along_x = jax.random.randint(keys[0], shape, 0, MXD)
    along_y = jax.random.randint(keys[1], shape, 0, MYD)
    along_z = jax.random.randint(keys[2], shape, 0, PZ)
    return jnp.stack([along_x, along_y, along_z]).astype(jnp.int32)


def draw_tasks(key):
    keys = jax.random.split(jax.random.fold_in(key, 7), 4)
    per_slab = STRIPS * PLACES
    shape = (SLABS, STRIPS, TASK_DEV)
    first = jax.random.randint(keys[0], shape, 0, per_slab)
    choose = jax.random.randint(keys[1], shape, 0, 13)
    first = first.at[:, :, 0].set(per_slab - 1)
    choose = choose.at[:, :, 0].set(4)
    first = first.at[:, :, 1].set(PLACES - 1)
    choose = choose.at[:, :, 1].set(9)
    first = first.at[:, :, 2].set(0)
    upper = jnp.asarray(forward_slab)[choose]
    strip = (first // PLACES + jnp.asarray(forward_strip)[choose]) % STRIPS
    place = (first % PLACES + jnp.asarray(forward_place)[choose]) % PLACES
    second = upper * per_slab + strip * PLACES + place
    light = jax.random.randint(keys[2], (SLABS, STRIPS // 2), 0, TASK_DEV // 2 + 1)
    light = light.at[:, 0].set(0)
    paired = jnp.stack([TASK_DEV - light, light], axis=-1).reshape(SLABS, STRIPS)
    scores = jax.random.randint(keys[3], (SLABS, STRIPS), 0, 1 << 20) * STRIPS + jnp.arange(STRIPS, dtype=jnp.int32)[None, :]
    order = jnp.argsort(scores, axis=1)
    count = jnp.take_along_axis(paired, order, axis=1)
    return (first.astype(jnp.int32), second.astype(jnp.int32), count.astype(jnp.int32))


def draw_task_first(key, part):
    return draw_tasks(key)[0]


def draw_task_second(key, part):
    return draw_tasks(key)[1]


def draw_task_count(key, part):
    return draw_tasks(key)[2]


def block_levels(own_key, shape, pieces, smallest, high):
    factor_of, own = 1.0, jax.random.fold_in(own_key, 6)
    for axis_at, shards_of in pieces:
        heights = jnp.exp(jax.random.uniform(jax.random.fold_in(own, axis_at), (shards_of,), jnp.float32, smallest / len(pieces), high / len(pieces)))
        factor_of = factor_of * jnp.repeat(heights, shape[axis_at] // shards_of).reshape([-1 if axis == axis_at else 1 for axis in range(len(shape))])
    return factor_of


def bell_draw(key, extent, spread, limit, cuts=(), kind=jnp.bfloat16):
    drawn = jax.random.normal(key, extent, jnp.float32) * spread
    if len(cuts) > 0:
        drawn = block_levels(key, extent, cuts, -0.22, 0.18) * drawn
    return jnp.clip(drawn, min=-limit, max=limit).astype(kind)


def setup_inputs(seed: int = 0) -> dict:
    splits = jax.random.split(jax.random.key(seed), 10)
    return {
        "cells": draw_cells(jax.random.fold_in(splits[9], 71), 0),
        "offsets": jnp.clip(jax.random.uniform(splits[1], (3, SLABS, STRIPS, PLACES, ATOMS), jnp.float32, -0.5, 0.5) * block_levels(splits[1], (3, SLABS, STRIPS, PLACES, ATOMS), ((1, 8), (2, 4)), -0.4, 0.0), -0.5, 0.5),
        "charges": bell_draw(splits[2], (SLABS, STRIPS, PLACES, ATOMS), 1.0, 4.0, ((0, 8), (1, 4)), jnp.float32),
        "masses": jnp.clip(jnp.exp(math.log(16.0) - 2.7725887 * jax.random.uniform(splits[3], (SLABS, STRIPS, PLACES, ATOMS), jnp.float32) ** block_levels(splits[3], (SLABS, STRIPS, PLACES, ATOMS), ((0, 8), (1, 4)), -0.2, 0.2)), 1.0, 16.0),
        "velocity": bell_draw(splits[4], (3, SLABS, STRIPS, PLACES, ATOMS), 1.0, 5.0, ((1, 8), (2, 4)), jnp.float32),
        "task_first": draw_task_first(jax.random.fold_in(splits[9], 71), 0),
        "task_second": draw_task_second(jax.random.fold_in(splits[9], 71), 0),
        "task_count": draw_task_count(jax.random.fold_in(splits[9], 71), 0),
        "kernel_taps": bell_draw(splits[8], (TERMS, 2 * RADIUS + 1), 0.5, 3.0, (), jnp.float32),
    }


cutoff_sq = 64.0
softening = 1.0
time_step = 0.5

def pair_push(left, right, shift, weight):
    sep = left[:, :3, :, None] - right[:, :3, None, :] + shift[:, :, None, None]
    dist = lax.optimization_barrier(jnp.sum(sep * sep, axis=1))
    reach = jnp.maximum(1.0 - dist / cutoff_sq, 0.0)
    soft = dist + softening
    coupling = left[:, 3, :, None] * right[:, 3, None, :] * weight[:, None, None] * reach * reach / (soft * jnp.sqrt(soft))
    return coupling[:, None] * sep

def wrap_step(delta, count):
    return (delta + 1) % count - 1

def task_geometry(task_first, task_second, task_count):
    per_slab = STRIPS * PLACES
    slab = lax.broadcasted_iota(jnp.int32, task_first.shape, 0)
    upper = task_second // per_slab
    rest = task_second % per_slab
    left_index = slab * per_slab + task_first
    right_index = (slab + upper) % SLABS * per_slab + rest
    shift = jnp.stack([-upper * MXD, wrap_step(task_first // PLACES - rest // PLACES, STRIPS) * MYD, wrap_step(task_first % PLACES - rest % PLACES, PLACES) * PZ], axis=-1).astype(jnp.float32)
    slot = lax.broadcasted_iota(jnp.int32, task_first.shape, 2)
    weight = (slot < task_count[:, :, None]).astype(jnp.float32)
    return (left_index.reshape(-1), right_index.reshape(-1), shift.reshape(-1, 3), weight.reshape(-1))

def short_force(points, charge, left_index, right_index, shift, weight):
    packed = jnp.concatenate([points, charge[:, None, :]], axis=1)

    def own_block(block):
        number = block.shape[0]
        return lax.optimization_barrier(jnp.sum(pair_push(block, block, jnp.zeros((number, 3), jnp.float32), jnp.ones((number,), jnp.float32)), axis=3))
    inner = lax.map(own_block, packed.reshape(-1, PLACES, 4, ATOMS)).reshape(-1, 3, ATOMS)

    def task_block(block):
        left, right, offset, live = block
        push = pair_push(packed[left], packed[right], offset, live)
        return (lax.optimization_barrier(jnp.sum(push, axis=3)), -lax.optimization_barrier(jnp.sum(push, axis=2)))
    on_left, on_right = lax.map(task_block, (left_index.reshape(-1, TASK_DEV), right_index.reshape(-1, TASK_DEV), shift.reshape(-1, TASK_DEV, 3), weight.reshape(-1, TASK_DEV)))
    gained = jax.ops.segment_sum(jnp.concatenate([on_left.reshape(-1, 3, ATOMS), on_right.reshape(-1, 3, ATOMS)]), jnp.concatenate([left_index, right_index]), num_segments=packed.shape[0])
    return inner + gained

def spline(frac):
    weights = (0.5 * (0.5 - frac) ** 2, 0.75 - frac * frac, 0.5 * (0.5 + frac) ** 2)
    slopes = (frac - 0.5, -2.0 * frac, 0.5 + frac)
    return (weights, slopes)

def kernel_line(kernel_taps, length):
    span = kernel_taps.shape[1]
    where = ((jnp.arange(span) - span // 2) % length).astype(jnp.int32)
    return jnp.zeros((kernel_taps.shape[0], length), jnp.float32).at[:, where].set(kernel_taps)

def mesh_force(cells, offsets, charges, kernel_taps):
    shape = charges.shape
    grid_x = lax.broadcasted_iota(jnp.int32, shape, 0) * MXD + cells[0]
    grid_y = lax.broadcasted_iota(jnp.int32, shape, 1) * MYD + cells[1]
    grid_z = lax.broadcasted_iota(jnp.int32, shape, 2) * PZ + cells[2]
    weight_x, slope_x = spline(offsets[0])
    weight_y, slope_y = spline(offsets[1])
    weight_z, slope_z = spline(offsets[2])
    mesh = jnp.zeros((NX, NY, MZ), jnp.float32)
    for step_x in range(3):
        for step_y in range(3):
            for step_z in range(3):
                mesh = mesh.at[(grid_x + step_x - 1) % NX, (grid_y + step_y - 1) % NY, (grid_z + step_z - 1) % MZ].add(charges * weight_x[step_x] * weight_y[step_y] * weight_z[step_z])
    spec_x = jnp.fft.fft(kernel_line(kernel_taps, NX), axis=1)
    spec_y = jnp.fft.fft(kernel_line(kernel_taps, NY), axis=1)
    spec_z = jnp.fft.rfft(kernel_line(kernel_taps, MZ), axis=1)
    spectrum = jnp.einsum('ta,tb,tc->abc', spec_x, spec_y, spec_z)
    potential = jnp.fft.irfftn(jnp.fft.rfftn(mesh) * spectrum, s=(NX, NY, MZ))
    grad_x = jnp.zeros(shape, jnp.float32)
    grad_y = jnp.zeros(shape, jnp.float32)
    grad_z = jnp.zeros(shape, jnp.float32)
    for step_x in range(3):
        for step_y in range(3):
            for step_z in range(3):
                value = potential[(grid_x + step_x - 1) % NX, (grid_y + step_y - 1) % NY, (grid_z + step_z - 1) % MZ]
                grad_x = grad_x + slope_x[step_x] * weight_y[step_y] * weight_z[step_z] * value
                grad_y = grad_y + weight_x[step_x] * slope_y[step_y] * weight_z[step_z] * value
                grad_z = grad_z + weight_x[step_x] * weight_y[step_y] * slope_z[step_z] * value
    return -charges[None] * jnp.stack([grad_x, grad_y, grad_z])

def to_rows(array):
    return jnp.transpose(array, (1, 2, 3, 0, 4)).reshape(-1, 3, ATOMS)

def from_rows(array):
    return jnp.transpose(array.reshape(SLABS, STRIPS, PLACES, 3, ATOMS), (3, 0, 1, 2, 4))

def reference(cells, offsets, charges, masses, velocity, task_first, task_second, task_count, kernel_taps):
    start = to_rows(cells.astype(jnp.float32) + offsets)
    charge = charges.reshape(-1, ATOMS)
    long_force = to_rows(mesh_force(cells, offsets, charges, kernel_taps))
    inverse = (1.0 / masses).reshape(-1, 1, ATOMS)
    speed = to_rows(velocity)
    left_index, right_index, shift, weight = task_geometry(task_first, task_second, task_count)
    first_force = short_force(start, charge, left_index, right_index, shift, weight)
    half = speed + time_step * inverse * (first_force + 2.0 * long_force)
    moved = start + time_step * half
    second_force = short_force(moved, charge, left_index, right_index, shift, weight)
    final = half + time_step * inverse * second_force
    displacement = time_step * (half + final)
    return (from_rows(displacement), from_rows(final))
```

```python
import functools

import jax
import jax.numpy as jnp
from jax import lax
from jax.experimental import pallas as pl
from jax.experimental.pallas import tpu as pltpu
from jax.sharding import PartitionSpec as P

MXD = 8
MYD = 16
PZ = 8
RADIUS = 8

time_step = 0.5
reach_sq = 64.0
soft_end = 65.0
push_scale = 1.0 / 4096.0

XO = MXD + 2
YO = MYD + 2
YR = 24
XW = XO + 2 * RADIUS
YE = RADIUS + 2
NE = 104
NS = 184
N2 = 40

f32 = jnp.float32
bf16 = jnp.bfloat16
i32 = jnp.int32


def split(x):
    hi = x.astype(bf16)
    lo = (x - hi.astype(f32)).astype(bf16)
    return hi, lo


def dot(a, b, dims=(((1,), (0,)), ((), ()))):
    return lax.dot_general(a, b, dims, preferred_element_type=f32)


def dot3(a, b, dims=(((1,), (0,)), ((), ()))):
    ah, al = a
    bh, bl = b
    return dot(ah, bh, dims) + (dot(al, bh, dims) + dot(ah, bl, dims))


NT = (((1,), (1,)), ((), ()))
TN = (((0,), (0,)), ((), ()))


def iota(shape, dim):
    return lax.broadcasted_iota(i32, shape, dim)


def spline(frac):
    weights = (0.5 * (0.5 - frac) ** 2, 0.75 - frac * frac, 0.5 * (0.5 + frac) ** 2)
    slopes = (frac - 0.5, -2.0 * frac, 0.5 + frac)
    return weights, slopes


def place3(rows, base, values):
    out = jnp.where(rows == base, values[0], 0.0)
    out = jnp.where(rows == base + 1, values[1], out)
    return jnp.where(rows == base + 2, values[2], out)


def pair_rows(ref, c, m):
    if c is None:
        return jnp.concatenate([ref[2 * m : 2 * m + 1, :], ref[2 * m + 1 : 2 * m + 2, :]], axis=1)
    return jnp.concatenate([ref[c, 2 * m : 2 * m + 1, :], ref[c, 2 * m + 1 : 2 * m + 2, :]], axis=1)


def pair_base_z(cz, atoms):
    second = (iota(cz.shape, 1) >= atoms).astype(i32)
    return cz + (PZ - 1) + PZ * second


def spread_kernel(cells, frac, charge, first, second, count, own, pk_lo, pk_hi, pos, lists, acc):
    places, atoms = charge.shape
    depth = places * PZ
    for c in range(3):
        start = cells[c].astype(f32) + frac[c]
        for dst, at in ((pos, 0), (pk_lo, 2 * NE), (pk_hi, 2 * NE)):
            dst[at + c * places : at + (c + 1) * places, :] = start
    q = charge[...]
    for dst, at in ((pos, 0), (pk_lo, 2 * NE), (pk_hi, 2 * NE)):
        dst[at + 3 * places : at + 4 * places, :] = q
    slots = first.shape[1]
    zero = jnp.zeros((1, atoms - slots), f32)
    block = jnp.concatenate(
        [
            jnp.concatenate([first[...].astype(f32), zero], axis=1),
            jnp.concatenate([second[...].astype(f32), zero], axis=1),
            jnp.broadcast_to(count[...].astype(f32), (1, atoms)),
            jnp.zeros((5, atoms), f32),
        ],
        axis=0,
    )
    at = 2 * NE + 4 * places
    lists[...] = block
    pk_lo[at : at + 8, :] = block
    pk_hi[at : at + 8, :] = block
    acc[...] = jnp.zeros_like(acc)
    y_rows = iota((YR, 2 * atoms), 0)
    x_rows = iota((16, 2 * atoms), 0)
    z_rows = iota((4 * PZ, 2 * atoms), 0)
    for m in range(places // 2):
        wx = place3(x_rows, pair_rows(cells, 0, m), spline(pair_rows(frac, 0, m))[0])
        wy = place3(y_rows, pair_rows(cells, 1, m), spline(pair_rows(frac, 1, m))[0])
        wz = place3(
            z_rows, pair_base_z(pair_rows(cells, 2, m), atoms), spline(pair_rows(frac, 2, m))[0]
        )
        wy = wy * pair_rows(charge, None, m)
        table = jnp.concatenate([wx[x : x + 1, :] * wy for x in range(XO)], axis=0)
        rows = pl.ds(2 * PZ * m, 4 * PZ)
        acc[rows, : XO * YR] += dot3(split(wz), split(table), NT)
    acc[depth : depth + PZ, :] += acc[0:PZ, :]
    acc[PZ : 2 * PZ, :] += acc[depth + PZ : depth + 2 * PZ, :]
    grid = jnp.transpose(acc[PZ : PZ + depth, :])
    own[...] = grid[: XO * YR, :]
    pk_lo[0 : 2 * NE, :] = jnp.zeros((2 * NE, 128), f32)
    pk_hi[0 : 2 * NE, :] = jnp.zeros((2 * NE, 128), f32)
    for x in range(XO):
        for half in range(2):
            dst = pl.ds(half * NE + x * YE, YE)
            lanes = slice(half * 128, half * 128 + 128)
            pk_lo[dst, :] = own[x * YR : x * YR + YE, lanes]
            pk_hi[dst, :] = own[x * YR + YO - YE : x * YR + YO, lanes]


def add_side(force, posr, cols, blk, r, p, places, offsets):
    off_x, off_y, off_z = offsets
    shape = (8, 128)
    xr = jnp.broadcast_to(posr[pl.ds(r, 1), :] + off_x, shape)
    yr = jnp.broadcast_to(posr[pl.ds(places + r, 1), :] + off_y, shape)
    zr = jnp.broadcast_to(posr[pl.ds(2 * places + r, 1), :] + off_z, shape)
    ax = jnp.zeros(shape, f32)
    ay = jnp.zeros(shape, f32)
    az = jnp.zeros(shape, f32)
    ix = jnp.full(shape, p, i32)
    iy, iz, iq = ix + places, ix + 2 * places, ix + 3 * places
    for k in range(16):
        col = cols[blk, 8 * k : 8 * k + 8, :]
        dx = xr - jnp.take_along_axis(col, ix, axis=1)
        dy = yr - jnp.take_along_axis(col, iy, axis=1)
        dz = zr - jnp.take_along_axis(col, iz, axis=1)
        qs = jnp.take_along_axis(col, iq, axis=1)
        soft = (dx * dx + dy * dy) + (dz * dz + 1.0)
        reach = jnp.maximum(soft_end - soft, 0.0)
        rs = lax.rsqrt(soft)
        t = reach * rs
        c = (t * t) * (rs * qs)
        ax = ax + c * dx
        ay = ay + c * dy
        az = az + c * dz
    for c, a in enumerate((ax, ay, az)):
        rows = pl.ds(pl.multiple_of((c * places + r) * 8, 8), 8)
        force[rows, :] += a


def folded_force(force, posr, places, c):
    part = force[c * places * 8 : (c + 1) * places * 8, :]
    total = jnp.sum(part.reshape(places, 8, 128), axis=1)
    return total * (posr[3 * places : 4 * places, :] * push_scale)


def add_self(force, posr, cols, places):
    def body(r, carry):
        add_side(force, posr, cols, 0, r, r, places, (0.0, 0.0, 0.0))
        return carry

    lax.fori_loop(0, places, body, 0)


def add_listed(force, posr, cols, work, places, slot_of):
    bits = places.bit_length() - 1

    def body(n, carry):
        code = work[n + 1]
        r = code & (places - 1)
        p = (code >> bits) & (places - 1)
        blk = code >> (2 * bits)
        dslab = blk // 3 - 1
        dstrip = blk % 3 - 1
        dz = ((r - p + 1) & (places - 1)) - 1
        off = (
            (-MXD * dslab).astype(f32),
            (-MYD * dstrip).astype(f32),
            (PZ * dz).astype(f32),
        )
        add_side(force, posr, cols, slot_of(blk), r, p, places, off)
        return carry

    lax.fori_loop(0, work[0], body, 0)


def wrap_step(delta, count):
    return jnp.where(delta > 1, delta - count, jnp.where(delta < -1, delta + count, delta))


def list_tasks(lists, number, below, work_near, work_far, places, strips):
    bits = places.bit_length() - 1
    per_slab = places * strips
    mine = lax.axis_index("grp")

    def code(r, dslab, strip, p):
        blk = (dslab + 1) * 3 + wrap_step(strip - mine, strips) + 1
        blk = jnp.clip(blk, 0, 8)
        return r + places * (p + places * blk)

    def each_list(h, carry):
        live = lists[h, 2, 0].astype(i32)

        def each(k, carry):
            near, far = carry
            a = lists[h, 0, k].astype(i32)
            b = lists[h, 1, k].astype(i32)
            upper = (b >= per_slab).astype(i32)
            rest = b - upper * per_slab
            a_strip, a_place = a >> bits, a & (places - 1)
            b_strip, b_place = rest >> bits, rest & (places - 1)
            if below:
                work_far[far + 1] = code(b_place, -1, a_strip, a_place)
                return near, far + upper * (b_strip == mine).astype(i32)
            left = (a_strip == mine).astype(i32)
            work_far[far + 1] = code(a_place, 1, b_strip, b_place)
            far = far + upper * left
            work_near[near + 1] = code(a_place, 0, b_strip, b_place)
            near = near + (1 - upper) * left
            work_near[near + 1] = code(b_place, 0, a_strip, a_place)
            near = near + (1 - upper) * (b_strip == mine).astype(i32)
            return near, far

        return lax.fori_loop(0, live, each, carry)

    near, far = lax.fori_loop(0, number, each_list, (jnp.int32(0), jnp.int32(0)))
    work_far[0] = far
    if not below:
        work_near[0] = near


def tap_lookup(taps, t, index):
    span = 2 * RADIUS + 1
    index = jnp.where((index >= 0) & (index < span), index, 127)
    row = jnp.broadcast_to(taps[t : t + 1, :], (8, 128))
    blocks = []
    for i in range(0, index.shape[0], 8):
        blocks.append(
            jnp.concatenate(
                [
                    jnp.take_along_axis(row, index[i : i + 8, j : j + 128], axis=1)
                    for j in range(0, index.shape[1], 128)
                ],
                axis=1,
            )
        )
    return jnp.concatenate(blocks, axis=0)


def line_table(taps, t, depth):
    half = depth // 2
    rows, lanes = iota((half, half), 0), iota((half, half), 1)
    same = tap_lookup(taps, t, lanes - rows + RADIUS)
    other = tap_lookup(taps, t, (lanes - rows + half + RADIUS) % depth)
    return jnp.concatenate(
        [jnp.concatenate([same, other], axis=1), jnp.concatenate([other, same], axis=1)], axis=0
    )


def plane_table(taps, t, x_of, y_of):
    lanes = x_of.shape[1]
    x_rows = iota((32, lanes), 0) - (RADIUS + 1)
    y_rows = iota((YR, lanes), 0) - 1
    along_x = tap_lookup(taps, t, x_rows - x_of + RADIUS)
    along_y = tap_lookup(taps, t, y_rows - y_of + RADIUS)
    return jnp.concatenate([along_x[x : x + 1, :] * along_y for x in range(XW)], axis=0)


def put_split(pair, rows, lanes, value):
    hi, lo = split(value)
    pair[0, rows, lanes] = hi
    pair[1, rows, lanes] = lo


def tables_kernel(
    taps_in, own, pos, line, edge_table, partial, force_out, taps, table, smooth, cols, force
):
    places = pos.shape[0] // 4
    depth = places * PZ
    terms = taps_in.shape[0]
    taps[...] = jnp.zeros_like(taps)
    taps[0:terms, 0 : taps_in.shape[1]] = taps_in[...]
    lane_own = iota((8, 256), 1)
    own_x = lane_own[0:1] // YR - 1
    own_y = lane_own[0:1] % YR - 1
    own_x = jnp.where(lane_own[0:1] < XO * YR, own_x, 1000)
    lane = iota((1, 256), 1)
    in_up = lane < XO * YE
    in_down = (lane >= NE) & (lane < NE + XO * YE)
    local = jnp.where(in_up, lane, lane - NE)
    edge_x = jnp.where(in_up | in_down, local // YE - 1, 1000)
    edge_y = local % YE + jnp.where(in_up, MYD - 1, -(RADIUS + 1))
    own_pair = split(jnp.concatenate([own[...], jnp.zeros((16, depth), f32)], axis=0))
    for t in range(terms):
        kz = line_table(taps, t, depth)
        kh, kl = split(kz)
        line[0, t] = kh
        line[1, t] = kl
        q = dot3(own_pair, (kh, kl))
        put_split(smooth, slice(t * 256, t * 256 + 256), slice(None), q)
        put_split(table, slice(None), slice(t * 256, t * 256 + 256), plane_table(taps, t, own_x, own_y))
        put_split(
            edge_table, slice(None), slice(t * 256, t * 256 + 256), plane_table(taps, t, edge_x, edge_y)
        )
    partial[...] = dot3((table[0], table[1]), (smooth[0], smooth[1]))
    cols[0] = jnp.transpose(pos[...])
    force[...] = jnp.zeros_like(force)
    add_self(force, pos, cols, places)
    force_out[...] = force[...]


def planes_kernel(
    *refs, number_far
):
    up, down, pos, lists = refs[:4]
    far = refs[4 : 4 + number_far]
    line, edge_table, partial = refs[4 + number_far : 7 + number_far]
    pk_lo, pk_hi, e_lo, e_hi, mid, smooth = refs[7 + number_far :]
    places = pos.shape[0] // 4
    terms = line.shape[1]
    block = jnp.concatenate(
        [
            jnp.concatenate([src[0:NE, :], src[NE : 2 * NE, :]], axis=1) for src in (up, down)
        ]
        + [jnp.zeros((256 - 2 * NE, 256), f32)],
        axis=0,
    )
    pair = split(block)
    for t in range(terms):
        q = dot3(pair, (line[0, t], line[1, t]))
        put_split(smooth, slice(t * 256, t * 256 + 256), slice(None), q)
    total = partial[...] + dot3((edge_table[0], edge_table[1]), (smooth[0], smooth[1]))
    mid[...] = total[RADIUS * YR : (RADIUS + XO) * YR, :]
    low = total[: XO * YR, :]
    high = total[2 * RADIUS * YR :, :]
    for half in range(2):
        lanes = slice(half * 128, half * 128 + 128)
        for x in range(XO):
            rows = pl.ds(half * NS + x * YO, YO)
            pk_lo[rows, :] = low[x * YR : x * YR + YO, lanes]
            pk_hi[rows, :] = high[x * YR : x * YR + YO, lanes]
        for x in range(2):
            rows = pl.ds(half * N2 + x * YO, YO)
            e_lo[rows, :] = low[x * YR : x * YR + YO, lanes]
            e_hi[rows, :] = high[(XO - 2 + x) * YR : (XO - 2 + x) * YR + YO, lanes]
        for dst, size, pad in ((pk_lo, NS, NS - XO * YO), (pk_hi, NS, NS - XO * YO), (e_lo, N2, N2 - 2 * YO), (e_hi, N2, N2 - 2 * YO)):
            dst[(half + 1) * size - pad : (half + 1) * size, :] = jnp.zeros((pad, 128), f32)
    rows = 4 * places
    for dst in (pk_lo, pk_hi):
        at = 2 * NS
        for src, begin in ((down, 2 * NE), (pos, 0), (up, 2 * NE)):
            dst[at : at + rows, :] = src[begin : begin + rows, :]
            at += rows
        for src, begin in [(lists, 0), (down, 2 * NE + rows), (up, 2 * NE + rows)] + [(r, 0) for r in far]:
            dst[at : at + 8, :] = src[begin : begin + 8, :]
            at += 8


def near_kernel(*refs, number_far, strips):
    up, down, pos, lists = refs[:4]
    far = refs[4 : 4 + number_far]
    force_in = refs[4 + number_far]
    force_out, work_near, work_far, held, cols, sem = refs[5 + number_far :]
    places = pos.shape[0] // 4
    rows = 4 * places
    sources = [lists.at[0:8], down.at[pl.ds(2 * NE + rows, 8)], up.at[pl.ds(2 * NE + rows, 8)]]
    sources += [r.at[0:8] for r in far]
    copies = [
        pltpu.make_async_copy(src, held.at[n], sem.at[n]) for n, src in enumerate(sources)
    ]
    for copy in copies:
        copy.start()
    force_out[...] = force_in[...]
    cols[0] = jnp.transpose(down[2 * NE : 2 * NE + rows, :])
    cols[1] = jnp.transpose(pos[...])
    cols[2] = jnp.transpose(up[2 * NE : 2 * NE + rows, :])
    for copy in copies:
        copy.wait()
    list_tasks(held, len(sources), False, work_near, work_far, places, strips)
    add_listed(force_out, pos, cols, work_near, places, lambda blk: blk - 3)


def sample_kernel(
    cells, frac, charge, masses, velocity, pos, mid, low, high, e_lo, e_hi, force_in, work_far,
    half_out, moved, work_below, force, held, cols, grid, turned, long, sem, *, strips
):
    places, atoms = charge.shape
    depth = places * PZ
    rows = 4 * places
    at = 2 * NS + 3 * rows
    copies = [
        pltpu.make_async_copy(low.at[pl.ds(at + 8 * n, 8)], held.at[n], sem.at[n]) for n in range(strips)
    ]
    for copy in copies:
        copy.start()
    grid[...] = jnp.zeros_like(grid)
    for x in range(XO):
        for half in range(2):
            lanes = slice(half * 128, half * 128 + 128)
            src = pl.ds(half * NS + x * YO, YO)
            value = mid[x * YR : x * YR + YO, lanes] + low[src, :] + high[src, :]
            if x < 2:
                value = value + e_lo[pl.ds(half * N2 + x * YO, YO), :]
            if x >= XO - 2:
                value = value + e_hi[pl.ds(half * N2 + (x - XO + 2) * YO, YO), :]
            grid[x * YR : x * YR + YO, lanes] = value
    body = jnp.transpose(grid[...])
    turned[PZ : PZ + depth, :] = body
    turned[0:PZ, :] = body[depth - PZ :, :]
    turned[PZ + depth : 2 * PZ + depth, :] = body[0:PZ, :]
    y_rows = iota((YR, 2 * atoms), 0)
    x_rows = iota((16, 2 * atoms), 0)
    z_rows = iota((4 * PZ, 2 * atoms), 0)
    for m in range(places // 2):
        vx, dx = spline(pair_rows(frac, 0, m))
        vy, dy = spline(pair_rows(frac, 1, m))
        vz, dz = spline(pair_rows(frac, 2, m))
        bx, by = pair_rows(cells, 0, m), pair_rows(cells, 1, m)
        bz = pair_base_z(pair_rows(cells, 2, m), atoms)
        wx, sx = place3(x_rows, bx, vx), place3(x_rows, bx, dx)
        wy, sy = place3(y_rows, by, vy), place3(y_rows, by, dy)
        both = jnp.concatenate([place3(z_rows, bz, vz), place3(z_rows, bz, dz)], axis=1)
        bh, bl = split(both)
        th, tl = split(turned[2 * PZ * m : 2 * PZ * m + 4 * PZ, :])
        sampled = dot(
            jnp.concatenate([th, th, tl], axis=0), jnp.concatenate([bh, bl, bh], axis=0), TN
        )
        shape = (YR, 2 * atoms)
        gx, gy, gz = jnp.zeros(shape, f32), jnp.zeros(shape, f32), jnp.zeros(shape, f32)
        for x in range(XO):
            plain = sampled[x * YR : (x + 1) * YR, : 2 * atoms]
            sloped = sampled[x * YR : (x + 1) * YR, 2 * atoms :]
            gx = gx + sx[x : x + 1, :] * plain
            gy = gy + wx[x : x + 1, :] * plain
            gz = gz + wx[x : x + 1, :] * sloped
        for c, value in enumerate((gx * wy, gy * sy, gz * wy)):
            line = jnp.sum(value, axis=0, keepdims=True)
            long[c, 2 * m : 2 * m + 1, :] = line[:, :atoms]
            long[c, 2 * m + 1 : 2 * m + 2, :] = line[:, atoms:]
    for n, src in enumerate((low, high)):
        for k in range(3):
            begin = 2 * NS + k * rows
            cols[3 * n + k] = jnp.transpose(src[begin : begin + rows, :])
    force[...] = force_in[...]
    add_listed(force, pos, cols, work_far, places, lambda blk: blk - 3)
    for copy in copies:
        copy.wait()
    list_tasks(held, strips, True, None, work_below, places, strips)
    add_listed(force, pos, cols, work_below, places, lambda blk: blk)
    inverse = time_step * (1.0 / masses[...])
    q = charge[...]
    for c in range(3):
        total = folded_force(force, pos, places, c) - 2.0 * q * long[c]
        half = velocity[c] + inverse * total
        half_out[c] = half
        moved[c * places : (c + 1) * places, :] = (
            pos[c * places : (c + 1) * places, :] + time_step * half
        )


def with_charge(dst, src, begin, charges, places):
    dst[0 : 3 * places, :] = src[begin : begin + 3 * places, :]
    dst[3 * places : 4 * places, :] = charges


def moved_self_kernel(moved, pos, force_out, full, cols):
    places = pos.shape[0] // 4
    with_charge(full, moved, 0, pos[3 * places : 4 * places, :], places)
    cols[0] = jnp.transpose(full[...])
    force_out[...] = jnp.zeros_like(force_out)
    add_self(force_out, full, cols, places)


def moved_near_kernel(moved, up, down, pos, up_pk, down_pk, force_in, work_near, force_out, full, cols):
    places = pos.shape[0] // 4
    rows = 4 * places
    at = 2 * NE + 3 * places
    force_out[...] = force_in[...]
    for n, (src, charges) in enumerate(
        (
            (down, down_pk[at : at + places, :]),
            (up, up_pk[at : at + places, :]),
            (moved, pos[3 * places : rows, :]),
        )
    ):
        with_charge(full, src, 0, charges, places)
        cols[(0, 2, 1)[n]] = jnp.transpose(full[...])
    add_listed(force_out, full, cols, work_near, places, lambda blk: blk - 3)


def moved_far_kernel(
    moved, low, high, pos, low_pk, high_pk, force_in, work_far, work_below, half, masses,
    shown, speed, force, full, cols
):
    places = pos.shape[0] // 4
    rows = 4 * places
    force[...] = force_in[...]
    for n, (src, pack) in enumerate(((low, low_pk), (high, high_pk))):
        for k in range(3):
            at = 2 * NS + k * rows + 3 * places
            with_charge(full, src, 3 * places * k, pack[at : at + places, :], places)
            cols[3 * n + k] = jnp.transpose(full[...])
    with_charge(full, moved, 0, pos[3 * places : rows, :], places)
    add_listed(force, full, cols, work_far, places, lambda blk: blk - 3)
    add_listed(force, full, cols, work_below, places, lambda blk: blk)
    inverse = time_step * (1.0 / masses[...])
    for c in range(3):
        before = half[c]
        after = before + inverse * folded_force(force, full, places, c)
        speed[c] = after
        shown[c] = time_step * (before + after)


def call(kernel, outs, scratch, *args, flops=0, smem=(), smem_out=(), name=None):
    vmem = pl.BlockSpec(memory_space=pltpu.VMEM)
    scalar = pl.BlockSpec(memory_space=pltpu.SMEM)
    return pl.pallas_call(
        kernel,
        out_shape=outs,
        in_specs=[scalar if n in smem else vmem for n in range(len(args))],
        out_specs=[scalar if n in smem_out else vmem for n in range(len(outs))],
        scratch_shapes=scratch,
        cost_estimate=pl.CostEstimate(flops=flops, transcendentals=0, bytes_accessed=1 << 20),
        compiler_params=pltpu.CompilerParams(vmem_limit_bytes=60 * 1024 * 1024),
        name=name,
    )(*args)


def shifted(x, axis, distance):
    size = lax.axis_size(axis)
    return lax.ppermute(x, axis, [(i, (i + distance) % size) for i in range(size)])


def local(
    cells, offsets, charges, masses, velocity, task_first, task_second, task_count, kernel_taps
):
    cells, offsets, velocity = cells[:, 0, 0], offsets[:, 0, 0], velocity[:, 0, 0]
    charges, masses = charges[0, 0], masses[0, 0]
    places, atoms = charges.shape
    depth = places * PZ
    strips = lax.axis_size("grp")
    slots = task_first.shape[2]
    terms = kernel_taps.shape[0]
    rows = 4 * places
    number_far = strips - 3
    shape = jax.ShapeDtypeStruct
    vm = pltpu.VMEM

    pack = shape((2 * NE + rows + 8, 128), f32)
    own, pk_lo, pk_hi, pos, lists = call(
        spread_kernel,
        [shape((XO * YR, depth), f32), pack, pack, shape((rows, 128), f32), shape((8, 128), f32)],
        [vm((depth + 2 * PZ, 256), f32)],
        cells, offsets, charges, task_first[0], task_second[0], task_count,
        name="spread",
    )
    up = shifted(pk_lo, "grp", -1)
    down = shifted(pk_hi, "grp", 1)
    far = [shifted(lists, "grp", d) for d in range(2, strips - 1)]

    force_shape = shape((3 * places * 8, 128), f32)
    table_shape = (2, XW * YR, terms * 256)
    line, edge_table, partial, force = call(
        tables_kernel,
        [
            shape((2, terms, depth, depth), bf16),
            shape(table_shape, bf16),
            shape((XW * YR, depth), f32),
            force_shape,
        ],
        [
            vm((8, 128), f32),
            vm(table_shape, bf16),
            vm((2, terms * 256, depth), bf16),
            vm((1, 128, 128), f32),
            vm(force_shape.shape, f32),
        ],
        kernel_taps, own, pos,
        flops=10**10, name="tables",
    )

    pack = shape((2 * NS + 3 * rows + 8 * strips, 128), f32)
    edge = shape((2 * N2, 128), f32)
    to_low, to_high, edge_low, edge_high, mid = call(
        functools.partial(planes_kernel, number_far=number_far),
        [pack, pack, edge, edge, shape((XO * YR, depth), f32)],
        [vm((2, terms * 256, depth), bf16)],
        up, down, pos, lists, *far, line, edge_table, partial,
        name="planes",
    )
    high = shifted(to_low, "patch", -1)
    low = shifted(to_high, "patch", 1)
    e_hi = shifted(edge_low, "patch", -2)
    e_lo = shifted(edge_high, "patch", 2)

    work = shape((4 * strips * slots + 8,), i32)
    force, work_near, work_far = call(
        functools.partial(near_kernel, number_far=number_far, strips=strips),
        [force_shape, work, work],
        [pltpu.SMEM((strips, 8, 128), f32), vm((3, 128, 128), f32), pltpu.SemaphoreType.DMA((strips,))],
        up, down, pos, lists, *far, force,
        flops=10**10, smem_out=(1, 2), name="near",
    )

    half, moved, work_below = call(
        functools.partial(sample_kernel, strips=strips),
        [shape((3, places, atoms), f32), shape((3 * places, 128), f32), work],
        [
            vm(force_shape.shape, f32),
            pltpu.SMEM((strips, 8, 128), f32),
            vm((6, 128, 128), f32),
            vm((XO * YR, depth), f32),
            vm((depth + 2 * PZ, XO * YR), f32),
            vm((3, places, atoms), f32),
            pltpu.SemaphoreType.DMA((strips,)),
        ],
        cells, offsets, charges, masses, velocity, pos, mid, low, high, e_lo, e_hi, force, work_far,
        smem=(12,), smem_out=(2,), name="sample",
    )

    moved_up = shifted(moved, "grp", -1)
    moved_down = shifted(moved, "grp", 1)
    force = call(
        moved_self_kernel,
        [force_shape],
        [vm((rows, 128), f32), vm((1, 128, 128), f32)],
        moved, pos,
        flops=10**10, name="moved_self",
    )[0]
    column = jnp.concatenate([moved_down, moved, moved_up], axis=0)
    moved_high = shifted(column, "patch", -1)
    moved_low = shifted(column, "patch", 1)
    force = call(
        moved_near_kernel,
        [force_shape],
        [vm((rows, 128), f32), vm((3, 128, 128), f32)],
        moved, moved_up, moved_down, pos, up, down, force, work_near,
        smem=(7,), flops=10**10, name="moved_near",
    )[0]
    shown, speed = call(
        moved_far_kernel,
        [shape((3, places, atoms), f32)] * 2,
        [vm(force_shape.shape, f32), vm((rows, 128), f32), vm((6, 128, 128), f32)],
        moved, moved_low, moved_high, pos, low, high, force, work_far, work_below, half, masses,
        smem=(7, 8), name="moved_far",
    )
    return shown[:, None, None], speed[:, None, None]


def solution(mesh):
    placed = (
        P(None, "patch", "grp", None, None),
        P(None, "patch", "grp", None, None),
        P("patch", "grp", None, None),
        P("patch", "grp", None, None),
        P(None, "patch", "grp", None, None),
        P("patch", "grp", None),
        P("patch", "grp", None),
        P("patch", "grp"),
        P(),
    )
    return jax.shard_map(
        local,
        mesh=mesh,
        in_specs=placed,
        out_specs=(P(None, "patch", "grp", None, None), P(None, "patch", "grp", None, None)),
        check_vma=False,
    )
```

```python
import functools

import jax
import jax.numpy as jnp
from jax import lax
from jax.experimental import pallas as pl
from jax.experimental.pallas import tpu as pltpu
from jax.sharding import PartitionSpec as P

MXD = 8
MYD = 16
PZ = 8
RADIUS = 8

time_step = 0.5
reach_sq = 64.0
soft_end = 65.0
push_scale = 1.0 / 4096.0

XO = MXD + 2
YO = MYD + 2
YR = 24
XW = XO + 2 * RADIUS
YE = RADIUS + 2
NE = 104
NS = 184
N2 = 40

UNROLL = 4

f32 = jnp.float32
bf16 = jnp.bfloat16
i32 = jnp.int32


def split(x):
    hi = x.astype(bf16)
    lo = (x - hi.astype(f32)).astype(bf16)
    return hi, lo


def dot(a, b, dims=(((1,), (0,)), ((), ()))):
    return lax.dot_general(a, b, dims, preferred_element_type=f32)


def dot3(a, b, dims=(((1,), (0,)), ((), ()))):
    ah, al = a
    bh, bl = b
    return dot(ah, bh, dims) + (dot(al, bh, dims) + dot(ah, bl, dims))


NT = (((1,), (1,)), ((), ()))
TN = (((0,), (0,)), ((), ()))


def iota(shape, dim):
    return lax.broadcasted_iota(i32, shape, dim)


def spline(frac):
    weights = (0.5 * (0.5 - frac) ** 2, 0.75 - frac * frac, 0.5 * (0.5 + frac) ** 2)
    slopes = (frac - 0.5, -2.0 * frac, 0.5 + frac)
    return weights, slopes


def place3(rows, base, values):
    out = jnp.where(rows == base, values[0], 0.0)
    out = jnp.where(rows == base + 1, values[1], out)
    return jnp.where(rows == base + 2, values[2], out)


def pair_rows(ref, c, m):
    if c is None:
        return jnp.concatenate([ref[2 * m : 2 * m + 1, :], ref[2 * m + 1 : 2 * m + 2, :]], axis=1)
    return jnp.concatenate([ref[c, 2 * m : 2 * m + 1, :], ref[c, 2 * m + 1 : 2 * m + 2, :]], axis=1)


def pair_base_z(cz, atoms):
    second = (iota(cz.shape, 1) >= atoms).astype(i32)
    return cz + (PZ - 1) + PZ * second


def spread_kernel(cells, frac, charge, first, second, count, own, pk_lo, pk_hi, pos, lists, acc):
    places, atoms = charge.shape
    depth = places * PZ
    for c in range(3):
        start = cells[c].astype(f32) + frac[c]
        for dst, at in ((pos, 0), (pk_lo, 2 * NE), (pk_hi, 2 * NE)):
            dst[at + c * places : at + (c + 1) * places, :] = start
    q = charge[...]
    for dst, at in ((pos, 0), (pk_lo, 2 * NE), (pk_hi, 2 * NE)):
        dst[at + 3 * places : at + 4 * places, :] = q
    slots = first.shape[1]
    zero = jnp.zeros((1, atoms - slots), f32)
    block = jnp.concatenate(
        [
            jnp.concatenate([first[...].astype(f32), zero], axis=1),
            jnp.concatenate([second[...].astype(f32), zero], axis=1),
            jnp.broadcast_to(count[...].astype(f32), (1, atoms)),
            jnp.zeros((5, atoms), f32),
        ],
        axis=0,
    )
    at = 2 * NE + 4 * places
    lists[...] = block
    pk_lo[at : at + 8, :] = block
    pk_hi[at : at + 8, :] = block
    acc[...] = jnp.zeros_like(acc)
    y_rows = iota((YR, 2 * atoms), 0)
    x_rows = iota((16, 2 * atoms), 0)
    z_rows = iota((4 * PZ, 2 * atoms), 0)
    for m in range(places // 2):
        wx = place3(x_rows, pair_rows(cells, 0, m), spline(pair_rows(frac, 0, m))[0])
        wy = place3(y_rows, pair_rows(cells, 1, m), spline(pair_rows(frac, 1, m))[0])
        wz = place3(
            z_rows, pair_base_z(pair_rows(cells, 2, m), atoms), spline(pair_rows(frac, 2, m))[0]
        )
        wy = wy * pair_rows(charge, None, m)
        table = jnp.concatenate([wx[x : x + 1, :] * wy for x in range(XO)], axis=0)
        rows = pl.ds(2 * PZ * m, 4 * PZ)
        acc[rows, : XO * YR] += dot3(split(wz), split(table), NT)
    acc[depth : depth + PZ, :] += acc[0:PZ, :]
    acc[PZ : 2 * PZ, :] += acc[depth + PZ : depth + 2 * PZ, :]
    grid = jnp.transpose(acc[PZ : PZ + depth, :])
    own[...] = grid[: XO * YR, :]
    pk_lo[0 : 2 * NE, :] = jnp.zeros((2 * NE, 128), f32)
    pk_hi[0 : 2 * NE, :] = jnp.zeros((2 * NE, 128), f32)
    for x in range(XO):
        for half in range(2):
            dst = pl.ds(half * NE + x * YE, YE)
            lanes = slice(half * 128, half * 128 + 128)
            pk_lo[dst, :] = own[x * YR : x * YR + YE, lanes]
            pk_hi[dst, :] = own[x * YR + YO - YE : x * YR + YO, lanes]


def fill_receivers(parts, posr, places):
    rows = iota((8, 128), 0)
    for c in range(3):
        base = 8 * (places + 1) * c
        constant = jnp.where(rows == c, -1.0, 0.0)
        for r in range(places + 1):
            parts[base + 8 * r : base + 8 * r + 8, :] = constant
        for g in range(0, places, 8):
            x = posr[c * places + g : c * places + g + 8, :]
            hi = x.astype(bf16).astype(f32)
            rest = x - hi
            mid = rest.astype(bf16).astype(f32)
            for n, value in enumerate((hi, mid, rest - mid)):
                parts[pl.ds(base + 8 * g + 4 + n, 8, stride=8), :] = value


def side_operands(parts, src, source, r, shifts):
    rows = iota((8, 128), 0)
    shift_x, shift_y, shift_z = shifts
    shift = jnp.where(rows == 0, shift_x, jnp.where(rows == 1, shift_y, shift_z))
    at = src[pl.ds(pl.multiple_of(8 * source, 8), 8), :]
    at = jnp.where(rows < 3, at - shift, at)
    hi = at.astype(bf16).astype(f32)
    rest = at - hi
    mid = rest.astype(bf16).astype(f32)
    low = rest - mid
    mid = pltpu.roll(mid, 4, 0)
    left = jnp.concatenate(
        [jnp.where(rows < 4, hi, mid), jnp.where(rows < 4, low, 1.0)], axis=0
    )
    top = []
    end = []
    for c in range(4):
        sign = 1.0 if c == 3 else -1.0
        top.append(jnp.where((rows & 3) == c, sign, 0.0))
        if c < 3:
            end.append(parts[pl.ds(pl.multiple_of(parts.shape[0] // 3 * c + 8 * r, 8), 8), :])
        else:
            end.append(jnp.where(rows == c, sign, 0.0))
    right = jnp.concatenate(
        [jnp.concatenate(top, axis=1), jnp.concatenate(end, axis=1)], axis=0
    )
    return jnp.transpose(left).astype(bf16), right.astype(bf16)


def side_push(force, pairs, r):
    shape = (8, 128)
    ax = jnp.zeros(shape, f32)
    ay = jnp.zeros(shape, f32)
    az = jnp.zeros(shape, f32)
    for k in range(16):
        rows = slice(8 * k, 8 * k + 8)
        dx = pairs[rows, 0:128]
        dy = pairs[rows, 128:256]
        dz = pairs[rows, 256:384]
        qs = pairs[rows, 384:512]
        soft = (dx * dx + dy * dy) + (dz * dz + 1.0)
        reach = jnp.maximum(soft_end - soft, 0.0)
        rs = lax.rsqrt(soft)
        t = reach * rs
        c = (t * t) * (rs * qs)
        ax = ax + c * dx
        ay = ay + c * dy
        az = az + c * dz
    for c, a in enumerate((ax, ay, az)):
        rows = pl.ds(pl.multiple_of((3 * r + c) * 8, 8), 8)
        force[rows, :] += a


def add_sides(force, parts, src, pairs, number, places, decode):
    def prepare(n, dst):
        r, source, shifts = decode(n)
        left, right = side_operands(parts, src, source, r, shifts)
        dst[...] = dot(left, right)

    def receiver(n):
        return jnp.where(n < number, decode(n)[0], places)

    for u, dst in enumerate(pairs):
        prepare(jnp.int32(u), dst)

    def body(m, carry):
        n = UNROLL * m
        for u, dst in enumerate(pairs):
            side_push(force, dst, receiver(n + u))
            prepare(n + UNROLL + u, dst)
        return carry

    lax.fori_loop(0, (number + UNROLL - 1) // UNROLL, body, 0)


def fill_sources(src, block, component, places):
    for c in range(4):
        rows = component(c)
        for g in range(0, places, 8):
            at = (block * places + g) * 8 + c
            src[pl.ds(at, 8, stride=8), :] = rows[g : g + 8, :]


def rows_of(ref, begin, places):
    return lambda c: ref[begin + c * places : begin + (c + 1) * places, :]


def moved_rows(ref, begin, charges, at, places):
    return lambda c: (
        charges[at + 3 * places : at + 4 * places, :]
        if c == 3
        else ref[begin + c * places : begin + (c + 1) * places, :]
    )


def folded_force(force, posr, places):
    part = force[0 : 24 * places, :].reshape(places, 3, 8, 128)
    total = jnp.sum(part, axis=2)
    scale = posr[3 * places : 4 * places, :] * push_scale
    return [total[:, c, :] * scale for c in range(3)]


def add_self(force, parts, src, pairs, places):
    def decode(n):
        n = jnp.minimum(n, places - 1)
        return n, n, (0.0, 0.0, 0.0)

    add_sides(force, parts, src, pairs, places, places, decode)


def add_listed(force, parts, src, pairs, work, places, first_block):
    bits = places.bit_length() - 1

    def decode(n):
        code = work[n + 1]
        r = code & (places - 1)
        p = (code >> bits) & (places - 1)
        blk = code >> (2 * bits)
        dslab = blk // 3 - 1
        dstrip = blk % 3 - 1
        dz = ((r - p + 1) & (places - 1)) - 1
        shifts = (
            (-MXD * dslab).astype(f32),
            (-MYD * dstrip).astype(f32),
            (PZ * dz).astype(f32),
        )
        source = jnp.maximum(blk - first_block, 0) * places + p
        return r, source, shifts

    @pl.when(work[0] > 0)
    def _():
        add_sides(force, parts, src, pairs, work[0], places, decode)


def wrap_step(delta, count):
    return jnp.where(delta > 1, delta - count, jnp.where(delta < -1, delta + count, delta))


def list_tasks(lists, number, below, work_near, work_far, places, strips):
    bits = places.bit_length() - 1
    per_slab = places * strips
    mine = lax.axis_index("grp")

    def code(r, dslab, strip, p):
        blk = (dslab + 1) * 3 + wrap_step(strip - mine, strips) + 1
        blk = jnp.clip(blk, 0, 8)
        return r + places * (p + places * blk)

    def each_list(h, carry):
        live = lists[h, 2, 0].astype(i32)

        def each(k, carry):
            near, far = carry
            a = lists[h, 0, k].astype(i32)
            b = lists[h, 1, k].astype(i32)
            upper = (b >= per_slab).astype(i32)
            rest = b - upper * per_slab
            a_strip, a_place = a >> bits, a & (places - 1)
            b_strip, b_place = rest >> bits, rest & (places - 1)
            if below:
                work_far[far + 1] = code(b_place, -1, a_strip, a_place)
                return near, far + upper * (b_strip == mine).astype(i32)
            left = (a_strip == mine).astype(i32)
            work_far[far + 1] = code(a_place, 1, b_strip, b_place)
            far = far + upper * left
            work_near[near + 1] = code(a_place, 0, b_strip, b_place)
            near = near + (1 - upper) * left
            work_near[near + 1] = code(b_place, 0, a_strip, a_place)
            near = near + (1 - upper) * (b_strip == mine).astype(i32)
            return near, far

        return lax.fori_loop(0, live, each, carry)

    near, far = lax.fori_loop(0, number, each_list, (jnp.int32(0), jnp.int32(0)))
    for work, number in ((work_far, far),) + (() if below else ((work_near, near),)):
        work[0] = number
        for n in range(UNROLL * 2):
            work[number + 1 + n] = jnp.int32(0)


def tap_lookup(taps, t, index):
    span = 2 * RADIUS + 1
    index = jnp.where((index >= 0) & (index < span), index, 127)
    row = jnp.broadcast_to(taps[t : t + 1, :], (8, 128))
    blocks = []
    for i in range(0, index.shape[0], 8):
        blocks.append(
            jnp.concatenate(
                [
                    jnp.take_along_axis(row, index[i : i + 8, j : j + 128], axis=1)
                    for j in range(0, index.shape[1], 128)
                ],
                axis=1,
            )
        )
    return jnp.concatenate(blocks, axis=0)


def line_table(taps, t, depth):
    half = depth // 2
    rows, lanes = iota((half, half), 0), iota((half, half), 1)
    same = tap_lookup(taps, t, lanes - rows + RADIUS)
    other = tap_lookup(taps, t, (lanes - rows + half + RADIUS) % depth)
    return jnp.concatenate(
        [jnp.concatenate([same, other], axis=1), jnp.concatenate([other, same], axis=1)], axis=0
    )


def plane_table(taps, t, x_of, y_of):
    lanes = x_of.shape[1]
    x_rows = iota((32, lanes), 0) - (RADIUS + 1)
    y_rows = iota((YR, lanes), 0) - 1
    along_x = tap_lookup(taps, t, x_rows - x_of + RADIUS)
    along_y = tap_lookup(taps, t, y_rows - y_of + RADIUS)
    return jnp.concatenate([along_x[x : x + 1, :] * along_y for x in range(XW)], axis=0)


def put_split(pair, rows, lanes, value):
    hi, lo = split(value)
    pair[0, rows, lanes] = hi
    pair[1, rows, lanes] = lo


def tables_kernel(
    taps_in, own, pos, line, edge_table, partial, force_out, taps, table, smooth, src, parts, *pairs
):
    places = pos.shape[0] // 4
    depth = places * PZ
    terms = taps_in.shape[0]
    taps[...] = jnp.zeros_like(taps)
    taps[0:terms, 0 : taps_in.shape[1]] = taps_in[...]
    lane_own = iota((8, 256), 1)
    own_x = lane_own[0:1] // YR - 1
    own_y = lane_own[0:1] % YR - 1
    own_x = jnp.where(lane_own[0:1] < XO * YR, own_x, 1000)
    lane = iota((1, 256), 1)
    in_up = lane < XO * YE
    in_down = (lane >= NE) & (lane < NE + XO * YE)
    local = jnp.where(in_up, lane, lane - NE)
    edge_x = jnp.where(in_up | in_down, local // YE - 1, 1000)
    edge_y = local % YE + jnp.where(in_up, MYD - 1, -(RADIUS + 1))
    own_pair = split(jnp.concatenate([own[...], jnp.zeros((16, depth), f32)], axis=0))
    for t in range(terms):
        kz = line_table(taps, t, depth)
        kh, kl = split(kz)
        line[0, t] = kh
        line[1, t] = kl
        q = dot3(own_pair, (kh, kl))
        put_split(smooth, slice(t * 256, t * 256 + 256), slice(None), q)
        put_split(table, slice(None), slice(t * 256, t * 256 + 256), plane_table(taps, t, own_x, own_y))
        put_split(
            edge_table, slice(None), slice(t * 256, t * 256 + 256), plane_table(taps, t, edge_x, edge_y)
        )
    partial[...] = dot3((table[0], table[1]), (smooth[0], smooth[1]))
    fill_sources(src, 0, rows_of(pos, 0, places), places)
    fill_receivers(parts, pos, places)
    force_out[...] = jnp.zeros_like(force_out)
    add_self(force_out, parts, src, pairs, places)


def planes_kernel(
    *refs, number_far
):
    up, down, pos, lists = refs[:4]
    far = refs[4 : 4 + number_far]
    line, edge_table, partial = refs[4 + number_far : 7 + number_far]
    pk_lo, pk_hi, e_lo, e_hi, mid, smooth = refs[7 + number_far :]
    places = pos.shape[0] // 4
    terms = line.shape[1]
    block = jnp.concatenate(
        [
            jnp.concatenate([src[0:NE, :], src[NE : 2 * NE, :]], axis=1) for src in (up, down)
        ]
        + [jnp.zeros((256 - 2 * NE, 256), f32)],
        axis=0,
    )
    pair = split(block)
    for t in range(terms):
        q = dot3(pair, (line[0, t], line[1, t]))
        put_split(smooth, slice(t * 256, t * 256 + 256), slice(None), q)
    total = partial[...] + dot3((edge_table[0], edge_table[1]), (smooth[0], smooth[1]))
    mid[...] = total[RADIUS * YR : (RADIUS + XO) * YR, :]
    low = total[: XO * YR, :]
    high = total[2 * RADIUS * YR :, :]
    for half in range(2):
        lanes = slice(half * 128, half * 128 + 128)
        for x in range(XO):
            rows = pl.ds(half * NS + x * YO, YO)
            pk_lo[rows, :] = low[x * YR : x * YR + YO, lanes]
            pk_hi[rows, :] = high[x * YR : x * YR + YO, lanes]
        for x in range(2):
            rows = pl.ds(half * N2 + x * YO, YO)
            e_lo[rows, :] = low[x * YR : x * YR + YO, lanes]
            e_hi[rows, :] = high[(XO - 2 + x) * YR : (XO - 2 + x) * YR + YO, lanes]
        for dst, size, pad in ((pk_lo, NS, NS - XO * YO), (pk_hi, NS, NS - XO * YO), (e_lo, N2, N2 - 2 * YO), (e_hi, N2, N2 - 2 * YO)):
            dst[(half + 1) * size - pad : (half + 1) * size, :] = jnp.zeros((pad, 128), f32)
    rows = 4 * places
    for dst in (pk_lo, pk_hi):
        at = 2 * NS
        for src, begin in ((down, 2 * NE), (pos, 0), (up, 2 * NE)):
            dst[at : at + rows, :] = src[begin : begin + rows, :]
            at += rows
        for src, begin in [(lists, 0), (down, 2 * NE + rows), (up, 2 * NE + rows)] + [(r, 0) for r in far]:
            dst[at : at + 8, :] = src[begin : begin + 8, :]
            at += 8


def near_kernel(*refs, number_far, strips):
    up, down, pos, lists = refs[:4]
    far = refs[4 : 4 + number_far]
    force_in = refs[4 + number_far]
    force_out, work_near, work_far, held, src, parts, *pairs, sem = refs[5 + number_far :]
    places = pos.shape[0] // 4
    rows = 4 * places
    sources = [lists.at[0:8], down.at[pl.ds(2 * NE + rows, 8)], up.at[pl.ds(2 * NE + rows, 8)]]
    sources += [r.at[0:8] for r in far]
    copies = [
        pltpu.make_async_copy(src, held.at[n], sem.at[n]) for n, src in enumerate(sources)
    ]
    for copy in copies:
        copy.start()
    force_out[...] = force_in[...]
    blocks = [rows_of(down, 2 * NE, places), rows_of(pos, 0, places), rows_of(up, 2 * NE, places)]
    for n, block in enumerate(blocks):
        fill_sources(src, n, block, places)
    fill_receivers(parts, pos, places)
    for copy in copies:
        copy.wait()
    list_tasks(held, len(sources), False, work_near, work_far, places, strips)
    add_listed(force_out, parts, src, pairs, work_near, places, 3)


def sample_kernel(
    cells, frac, charge, masses, velocity, pos, mid, low, high, e_lo, e_hi, force_in, work_far,
    half_out, moved, work_below, force, held, src, grid, turned, long, sem, parts, *pairs, strips
):
    places, atoms = charge.shape
    depth = places * PZ
    rows = 4 * places
    at = 2 * NS + 3 * rows
    copies = [
        pltpu.make_async_copy(low.at[pl.ds(at + 8 * n, 8)], held.at[n], sem.at[n]) for n in range(strips)
    ]
    for copy in copies:
        copy.start()
    grid[...] = jnp.zeros_like(grid)
    for x in range(XO):
        for half in range(2):
            lanes = slice(half * 128, half * 128 + 128)
            at_x = pl.ds(half * NS + x * YO, YO)
            value = mid[x * YR : x * YR + YO, lanes] + low[at_x, :] + high[at_x, :]
            if x < 2:
                value = value + e_lo[pl.ds(half * N2 + x * YO, YO), :]
            if x >= XO - 2:
                value = value + e_hi[pl.ds(half * N2 + (x - XO + 2) * YO, YO), :]
            grid[x * YR : x * YR + YO, lanes] = value
    body = jnp.transpose(grid[...])
    turned[PZ : PZ + depth, :] = body
    turned[0:PZ, :] = body[depth - PZ :, :]
    turned[PZ + depth : 2 * PZ + depth, :] = body[0:PZ, :]
    y_rows = iota((YR, 2 * atoms), 0)
    x_rows = iota((16, 2 * atoms), 0)
    z_rows = iota((4 * PZ, 2 * atoms), 0)
    for m in range(places // 2):
        vx, dx = spline(pair_rows(frac, 0, m))
        vy, dy = spline(pair_rows(frac, 1, m))
        vz, dz = spline(pair_rows(frac, 2, m))
        bx, by = pair_rows(cells, 0, m), pair_rows(cells, 1, m)
        bz = pair_base_z(pair_rows(cells, 2, m), atoms)
        wx, sx = place3(x_rows, bx, vx), place3(x_rows, bx, dx)
        wy, sy = place3(y_rows, by, vy), place3(y_rows, by, dy)
        both = jnp.concatenate([place3(z_rows, bz, vz), place3(z_rows, bz, dz)], axis=1)
        bh, bl = split(both)
        th, tl = split(turned[2 * PZ * m : 2 * PZ * m + 4 * PZ, :])
        sampled = dot(
            jnp.concatenate([th, th, tl], axis=0), jnp.concatenate([bh, bl, bh], axis=0), TN
        )
        shape = (YR, 2 * atoms)
        gx, gy, gz = jnp.zeros(shape, f32), jnp.zeros(shape, f32), jnp.zeros(shape, f32)
        for x in range(XO):
            plain = sampled[x * YR : (x + 1) * YR, : 2 * atoms]
            sloped = sampled[x * YR : (x + 1) * YR, 2 * atoms :]
            gx = gx + sx[x : x + 1, :] * plain
            gy = gy + wx[x : x + 1, :] * plain
            gz = gz + wx[x : x + 1, :] * sloped
        for c, value in enumerate((gx * wy, gy * sy, gz * wy)):
            line = jnp.sum(value, axis=0, keepdims=True)
            long[c, 2 * m : 2 * m + 1, :] = line[:, :atoms]
            long[c, 2 * m + 1 : 2 * m + 2, :] = line[:, atoms:]
    for n in range(6):
        fill_sources(src, n, rows_of((low, high)[n // 3], 2 * NS + n % 3 * rows, places), places)
    fill_receivers(parts, pos, places)
    force[...] = force_in[...]
    add_listed(force, parts, src, pairs, work_far, places, 3)
    for copy in copies:
        copy.wait()
    list_tasks(held, strips, True, None, work_below, places, strips)
    add_listed(force, parts, src, pairs, work_below, places, 0)
    inverse = time_step * (1.0 / masses[...])
    q = charge[...]
    short = folded_force(force, pos, places)
    for c in range(3):
        total = short[c] - 2.0 * q * long[c]
        half = velocity[c] + inverse * total
        half_out[c] = half
        moved[c * places : (c + 1) * places, :] = (
            pos[c * places : (c + 1) * places, :] + time_step * half
        )


def moved_self_kernel(moved, pos, force_out, src, parts, *pairs):
    places = pos.shape[0] // 4
    fill_sources(src, 0, moved_rows(moved, 0, pos, 0, places), places)
    fill_receivers(parts, moved, places)
    force_out[...] = jnp.zeros_like(force_out)
    add_self(force_out, parts, src, pairs, places)


def moved_near_kernel(
    moved, up, down, pos, up_pk, down_pk, force_in, work_near, force_out, src, parts, *pairs
):
    places = pos.shape[0] // 4
    force_out[...] = force_in[...]
    blocks = [
        moved_rows(down, 0, down_pk, 2 * NE, places),
        moved_rows(moved, 0, pos, 0, places),
        moved_rows(up, 0, up_pk, 2 * NE, places),
    ]
    for n, block in enumerate(blocks):
        fill_sources(src, n, block, places)
    fill_receivers(parts, moved, places)
    add_listed(force_out, parts, src, pairs, work_near, places, 3)


def moved_far_kernel(
    moved, low, high, pos, low_pk, high_pk, force_in, work_far, work_below, half, masses,
    shown, speed, force, src, parts, *pairs
):
    places = pos.shape[0] // 4
    rows = 4 * places
    force[...] = force_in[...]
    for n in range(6):
        part, pack = ((low, low_pk), (high, high_pk))[n // 3]
        k = n % 3
        block = moved_rows(part, 3 * places * k, pack, 2 * NS + k * rows, places)
        fill_sources(src, n, block, places)
    fill_receivers(parts, moved, places)
    add_listed(force, parts, src, pairs, work_far, places, 3)
    add_listed(force, parts, src, pairs, work_below, places, 0)
    short = folded_force(force, pos, places)
    inverse = time_step * (1.0 / masses[...])
    for c in range(3):
        before = half[c]
        after = before + inverse * short[c]
        speed[c] = after
        shown[c] = time_step * (before + after)


def call(kernel, outs, scratch, *args, flops=0, smem=(), smem_out=(), name=None):
    vmem = pl.BlockSpec(memory_space=pltpu.VMEM)
    scalar = pl.BlockSpec(memory_space=pltpu.SMEM)
    return pl.pallas_call(
        kernel,
        out_shape=outs,
        in_specs=[scalar if n in smem else vmem for n in range(len(args))],
        out_specs=[scalar if n in smem_out else vmem for n in range(len(outs))],
        scratch_shapes=scratch,
        cost_estimate=pl.CostEstimate(flops=flops, transcendentals=0, bytes_accessed=1 << 20),
        compiler_params=pltpu.CompilerParams(vmem_limit_bytes=20 * 1024 * 1024),
        name=name,
    )(*args)


def shifted(x, axis, distance):
    size = lax.axis_size(axis)
    return lax.ppermute(x, axis, [(i, (i + distance) % size) for i in range(size)])


def local(
    cells, offsets, charges, masses, velocity, task_first, task_second, task_count, kernel_taps
):
    cells, offsets, velocity = cells[:, 0, 0], offsets[:, 0, 0], velocity[:, 0, 0]
    charges, masses = charges[0, 0], masses[0, 0]
    places, atoms = charges.shape
    depth = places * PZ
    strips = lax.axis_size("grp")
    slots = task_first.shape[2]
    terms = kernel_taps.shape[0]
    rows = 4 * places
    number_far = strips - 3
    shape = jax.ShapeDtypeStruct
    vm = pltpu.VMEM

    pack = shape((2 * NE + rows + 8, 128), f32)
    own, pk_lo, pk_hi, pos, lists = call(
        spread_kernel,
        [shape((XO * YR, depth), f32), pack, pack, shape((rows, 128), f32), shape((8, 128), f32)],
        [vm((depth + 2 * PZ, 256), f32)],
        cells, offsets, charges, task_first[0], task_second[0], task_count,
        name="spread",
    )
    up = shifted(pk_lo, "grp", -1)
    down = shifted(pk_hi, "grp", 1)
    far = [shifted(lists, "grp", d) for d in range(2, strips - 1)]

    force_shape = shape((3 * (places + 1) * 8, 128), f32)
    pairs = [vm((24 * (places + 1), 128), f32)] + [vm((128, 512), f32)] * UNROLL

    def sources(blocks):
        return vm((blocks * places * 8, 128), f32)

    table_shape = (2, XW * YR, terms * 256)
    line, edge_table, partial, force = call(
        tables_kernel,
        [
            shape((2, terms, depth, depth), bf16),
            shape(table_shape, bf16),
            shape((XW * YR, depth), f32),
            force_shape,
        ],
        [
            vm((8, 128), f32),
            vm(table_shape, bf16),
            vm((2, terms * 256, depth), bf16),
            sources(1),
            *pairs,
        ],
        kernel_taps, own, pos,
        flops=10**10, name="tables",
    )

    pack = shape((2 * NS + 3 * rows + 8 * strips, 128), f32)
    edge = shape((2 * N2, 128), f32)
    to_low, to_high, edge_low, edge_high, mid = call(
        functools.partial(planes_kernel, number_far=number_far),
        [pack, pack, edge, edge, shape((XO * YR, depth), f32)],
        [vm((2, terms * 256, depth), bf16)],
        up, down, pos, lists, *far, line, edge_table, partial,
        name="planes",
    )
    high = shifted(to_low, "patch", -1)
    low = shifted(to_high, "patch", 1)
    e_hi = shifted(edge_low, "patch", -2)
    e_lo = shifted(edge_high, "patch", 2)

    work = shape((4 * strips * slots + 16,), i32)
    force, work_near, work_far = call(
        functools.partial(near_kernel, number_far=number_far, strips=strips),
        [force_shape, work, work],
        [pltpu.SMEM((strips, 8, 128), f32), sources(3), *pairs, pltpu.SemaphoreType.DMA((strips,))],
        up, down, pos, lists, *far, force,
        flops=10**10, smem_out=(1, 2), name="near",
    )

    half, moved, work_below = call(
        functools.partial(sample_kernel, strips=strips),
        [shape((3, places, atoms), f32), shape((3 * places, 128), f32), work],
        [
            vm(force_shape.shape, f32),
            pltpu.SMEM((strips, 8, 128), f32),
            sources(6),
            vm((XO * YR, depth), f32),
            vm((depth + 2 * PZ, XO * YR), f32),
            vm((3, places, atoms), f32),
            pltpu.SemaphoreType.DMA((strips,)),
            *pairs,
        ],
        cells, offsets, charges, masses, velocity, pos, mid, low, high, e_lo, e_hi, force, work_far,
        smem=(12,), smem_out=(2,), name="sample",
    )

    moved_up = shifted(moved, "grp", -1)
    moved_down = shifted(moved, "grp", 1)
    force = call(
        moved_self_kernel,
        [force_shape],
        [sources(1), *pairs],
        moved, pos,
        flops=10**10, name="moved_self",
    )[0]
    column = jnp.concatenate([moved_down, moved, moved_up], axis=0)
    moved_high = shifted(column, "patch", -1)
    moved_low = shifted(column, "patch", 1)
    force = call(
        moved_near_kernel,
        [force_shape],
        [sources(3), *pairs],
        moved, moved_up, moved_down, pos, up, down, force, work_near,
        smem=(7,), flops=10**10, name="moved_near",
    )[0]
    shown, speed = call(
        moved_far_kernel,
        [shape((3, places, atoms), f32)] * 2,
        [vm(force_shape.shape, f32), sources(6), *pairs],
        moved, moved_low, moved_high, pos, low, high, force, work_far, work_below, half, masses,
        smem=(7, 8), name="moved_far",
    )
    return shown[:, None, None], speed[:, None, None]


def solution(mesh):
    placed = (
        P(None, "patch", "grp", None, None),
        P(None, "patch", "grp", None, None),
        P("patch", "grp", None, None),
        P("patch", "grp", None, None),
        P(None, "patch", "grp", None, None),
        P("patch", "grp", None),
        P("patch", "grp", None),
        P("patch", "grp"),
        P(),
    )
    return jax.shard_map(
        local,
        mesh=mesh,
        in_specs=placed,
        out_specs=(P(None, "patch", "grp", None, None), P(None, "patch", "grp", None, None)),
        check_vma=False,
    )
```

```python
import functools

import jax
import jax.numpy as jnp
from jax import lax
from jax.experimental import pallas as pl
from jax.experimental.pallas import tpu as pltpu
from jax.sharding import PartitionSpec as P

MXD = 8
MYD = 16
PZ = 8
RADIUS = 8

time_step = 0.5
reach_sq = 64.0
soft_end = 65.0
push_scale = 1.0 / 4096.0

XO = MXD + 2
YO = MYD + 2
YR = 24
XW = XO + 2 * RADIUS
YE = RADIUS + 2
NE = 104
NS = 184
N2 = 40

UNROLL = 4


f32 = jnp.float32
bf16 = jnp.bfloat16
i32 = jnp.int32


def split(x):
    hi = x.astype(bf16)
    lo = (x - hi.astype(f32)).astype(bf16)
    return hi, lo


def dot(a, b, dims=(((1,), (0,)), ((), ()))):
    return lax.dot_general(a, b, dims, preferred_element_type=f32)


def dot3(a, b, dims=(((1,), (0,)), ((), ()))):
    ah, al = a
    bh, bl = b
    return dot(ah, bh, dims) + (dot(al, bh, dims) + dot(ah, bl, dims))


NT = (((1,), (1,)), ((), ()))
TN = (((0,), (0,)), ((), ()))


def iota(shape, dim):
    return lax.broadcasted_iota(i32, shape, dim)


def spline(frac):
    weights = (0.5 * (0.5 - frac) ** 2, 0.75 - frac * frac, 0.5 * (0.5 + frac) ** 2)
    slopes = (frac - 0.5, -2.0 * frac, 0.5 + frac)
    return weights, slopes


def place3(rows, base, values):
    out = jnp.where(rows == base, values[0], 0.0)
    out = jnp.where(rows == base + 1, values[1], out)
    return jnp.where(rows == base + 2, values[2], out)


def pair_rows(ref, c, m):
    if c is None:
        return jnp.concatenate([ref[2 * m : 2 * m + 1, :], ref[2 * m + 1 : 2 * m + 2, :]], axis=1)
    return jnp.concatenate([ref[c, 2 * m : 2 * m + 1, :], ref[c, 2 * m + 1 : 2 * m + 2, :]], axis=1)


def pair_base_z(cz, atoms):
    second = (iota(cz.shape, 1) >= atoms).astype(i32)
    return cz + (PZ - 1) + PZ * second


def list_block(first, second, count, places, strips, lanes):
    bits = places.bit_length() - 1
    slots = first.shape[1]
    live = iota((1, slots), 1) < count
    upper = (second >= places * strips).astype(i32)
    rest = second - upper * (places * strips)
    dead = jnp.full((1, lanes - slots), -1.0, f32)
    rows = [
        jnp.where(live, first >> bits, -1),
        first & (places - 1),
        jnp.where(live, rest >> bits, -1),
        rest & (places - 1),
        upper,
    ]
    rows = [jnp.concatenate([row.astype(f32), dead], axis=1) for row in rows]
    return jnp.concatenate(rows + [jnp.zeros((3, lanes), f32)], axis=0)


def spread_kernel(*refs, strips):
    sources, count, outs, scratch = refs[:6], refs[6], refs[7:13], refs[13:]
    own, pk_lo, pk_hi, pos, lists, taps_out = outs
    cells, frac, charge, first, second, taps, acc, sem = scratch
    copies = [
        pltpu.make_async_copy(src, dst, sem.at[n])
        for n, (src, dst) in enumerate(zip(sources, scratch[:6]))
    ]
    for copy in copies:
        copy.start()
    acc[...] = jnp.zeros_like(acc)
    pk_lo[0 : 2 * NE, :] = jnp.zeros((2 * NE, 128), f32)
    pk_hi[0 : 2 * NE, :] = jnp.zeros((2 * NE, 128), f32)
    for copy in copies:
        copy.wait()
    places, atoms = charge.shape
    depth = places * PZ
    for c in range(3):
        start = cells[c].astype(f32) + frac[c]
        for dst, at in ((pos, 0), (pk_lo, 2 * NE), (pk_hi, 2 * NE)):
            dst[at + c * places : at + (c + 1) * places, :] = start
    taps_out[...] = jnp.zeros_like(taps_out)
    taps_out[0 : taps.shape[0], 0 : taps.shape[1]] = taps[...]
    q = charge[...]
    for dst, at in ((pos, 0), (pk_lo, 2 * NE), (pk_hi, 2 * NE)):
        dst[at + 3 * places : at + 4 * places, :] = q
    block = list_block(first[...], second[...], count[0, 0], places, strips, atoms)
    at = 2 * NE + 4 * places
    lists[...] = block
    pk_lo[at : at + 8, :] = block
    pk_hi[at : at + 8, :] = block
    y_rows = iota((YR, 2 * atoms), 0)
    x_rows = iota((16, 2 * atoms), 0)
    z_rows = iota((4 * PZ, 2 * atoms), 0)
    for m in range(places // 2):
        wx = place3(x_rows, pair_rows(cells, 0, m), spline(pair_rows(frac, 0, m))[0])
        wy = place3(y_rows, pair_rows(cells, 1, m), spline(pair_rows(frac, 1, m))[0])
        wz = place3(
            z_rows, pair_base_z(pair_rows(cells, 2, m), atoms), spline(pair_rows(frac, 2, m))[0]
        )
        wy = wy * pair_rows(charge, None, m)
        table = jnp.concatenate([wx[x : x + 1, :] * wy for x in range(XO)], axis=0)
        rows = pl.ds(2 * PZ * m, 4 * PZ)
        acc[rows, : XO * YR] += dot3(split(wz), split(table), NT)
    acc[depth : depth + PZ, :] += acc[0:PZ, :]
    acc[PZ : 2 * PZ, :] += acc[depth + PZ : depth + 2 * PZ, :]
    grid = jnp.transpose(acc[PZ : PZ + depth, :])
    own[...] = grid[: XO * YR, :]
    for x in range(XO):
        for half in range(2):
            dst = pl.ds(half * NE + x * YE, YE)
            lanes = slice(half * 128, half * 128 + 128)
            pk_lo[dst, :] = own[x * YR : x * YR + YE, lanes]
            pk_hi[dst, :] = own[x * YR + YO - YE : x * YR + YO, lanes]


def fill_receivers(parts, posr, places):
    rows = iota((8, 128), 0)
    for c in range(3):
        base = 8 * (places + 1) * c
        constant = jnp.where(rows == c, -1.0, 0.0)
        for r in range(places + 1):
            parts[base + 8 * r : base + 8 * r + 8, :] = constant
        for g in range(0, places, 8):
            x = posr[c * places + g : c * places + g + 8, :]
            hi = x.astype(bf16).astype(f32)
            rest = x - hi
            mid = rest.astype(bf16).astype(f32)
            for n, value in enumerate((hi, mid, rest - mid)):
                parts[pl.ds(base + 8 * g + 4 + n, 8, stride=8), :] = value


def side_operands(parts, src, source, r, shifts):
    rows = iota((8, 128), 0)
    shift_x, shift_y, shift_z = shifts
    shift = jnp.where(rows == 0, shift_x, jnp.where(rows == 1, shift_y, shift_z))
    at = src[pl.ds(pl.multiple_of(8 * source, 8), 8), :]
    at = jnp.where(rows < 3, at - shift, at)
    hi = at.astype(bf16).astype(f32)
    rest = at - hi
    mid = rest.astype(bf16).astype(f32)
    low = rest - mid
    mid = pltpu.roll(mid, 4, 0)
    left = jnp.concatenate(
        [jnp.where(rows < 4, hi, mid), jnp.where(rows < 4, low, 1.0)], axis=0
    )
    top = []
    end = []
    for c in range(4):
        sign = 1.0 if c == 3 else -1.0
        top.append(jnp.where((rows & 3) == c, sign, 0.0))
        if c < 3:
            end.append(parts[pl.ds(pl.multiple_of(parts.shape[0] // 3 * c + 8 * r, 8), 8), :])
        else:
            end.append(jnp.where(rows == c, sign, 0.0))
    right = jnp.concatenate(
        [jnp.concatenate(top, axis=1), jnp.concatenate(end, axis=1)], axis=0
    )
    return jnp.transpose(left).astype(bf16), right.astype(bf16)


def side_push(force, pairs, r):
    shape = (8, 128)
    ax = jnp.zeros(shape, f32)
    ay = jnp.zeros(shape, f32)
    az = jnp.zeros(shape, f32)
    for k in range(16):
        rows = slice(8 * k, 8 * k + 8)
        dx = pairs[rows, 0:128]
        dy = pairs[rows, 128:256]
        dz = pairs[rows, 256:384]
        qs = pairs[rows, 384:512]
        soft = (dx * dx + dy * dy) + (dz * dz + 1.0)
        reach = jnp.maximum(soft_end - soft, 0.0)
        rs = lax.rsqrt(soft)
        t = reach * rs
        c = (t * t) * (rs * qs)
        ax = ax + c * dx
        ay = ay + c * dy
        az = az + c * dz
    for c, a in enumerate((ax, ay, az)):
        rows = pl.ds(pl.multiple_of((3 * r + c) * 8, 8), 8)
        force[rows, :] += a


def add_sides(force, parts, src, pairs, number, places, decode):
    def prepare(n, dst):
        r, source, shifts = decode(n)
        left, right = side_operands(parts, src, source, r, shifts)
        dst[...] = dot(left, right)

    def receiver(n):
        return jnp.where(n < number, decode(n)[0], places)

    for u, dst in enumerate(pairs):
        prepare(jnp.int32(u), dst)

    def body(m, carry):
        n = UNROLL * m
        for u, dst in enumerate(pairs):
            side_push(force, dst, receiver(n + u))
            prepare(n + UNROLL + u, dst)
        return carry

    lax.fori_loop(0, (number + UNROLL - 1) // UNROLL, body, 0)


def fill_sources(src, block, component, places):
    for c in range(4):
        rows = component(c)
        for g in range(0, places, 8):
            at = (block * places + g) * 8 + c
            src[pl.ds(at, 8, stride=8), :] = rows[g : g + 8, :]


def rows_of(ref, begin, places):
    return lambda c: ref[begin + c * places : begin + (c + 1) * places, :]


def moved_rows(ref, begin, charges, at, places):
    return lambda c: (
        charges[at + 3 * places : at + 4 * places, :]
        if c == 3
        else ref[begin + c * places : begin + (c + 1) * places, :]
    )


def folded_force(force, posr, places):
    part = force[0 : 24 * places, :].reshape(places, 3, 8, 128)
    total = jnp.sum(part, axis=2)
    scale = posr[3 * places : 4 * places, :] * push_scale
    return [total[:, c, :] * scale for c in range(3)]


def add_self(force, parts, src, pairs, places):
    def decode(n):
        n = jnp.minimum(n, places - 1)
        return n, n, (0.0, 0.0, 0.0)

    add_sides(force, parts, src, pairs, places, places, decode)


def add_listed(force, parts, src, pairs, work, places, across):
    bits = places.bit_length() - 1

    def decode(n):
        code = work[0, n]
        r = code & (places - 1)
        source = code >> bits
        p = source & (places - 1)
        strip = source >> bits
        slab = jnp.int32(0)
        if across:
            slab = jnp.where(strip >= 3, 1, -1)
            strip = jnp.where(strip >= 3, strip - 3, strip)
        dz = ((r - p + 1) & (places - 1)) - 1
        shifts = (
            (-MXD * slab).astype(f32),
            (-MYD * (strip - 1)).astype(f32),
            (PZ * dz).astype(f32),
        )
        return r, source, shifts

    add_sides(force, parts, src, pairs, work[1, 0], places, decode)


def wrap_step(delta, count):
    return jnp.where(delta > 1, delta - count, jnp.where(delta < -1, delta + count, delta))


def join_lists(blocks, slots, strips):
    lane = iota((8, 128), 1)
    group = 128 // slots
    parts = []
    for g in range(0, strips, group):
        joined = blocks[g]
        for n in range(1, group):
            block = pltpu.roll(blocks[g + n], n * slots, 1) if g + n < strips else -1.0
            joined = jnp.where(lane < n * slots, joined, block)
        parts.append(joined)
    return parts


def compact(work, mask, source, receiver, places):
    size = mask.shape[1]
    wide = work.shape[1]
    ones = jnp.where(mask, 1.0, 0.0)
    before = jnp.where(iota((size, size), 0) < iota((size, size), 1), 1.0, 0.0).astype(bf16)
    rank = dot(jnp.broadcast_to(ones, (8, size)).astype(bf16), before)[0:1].astype(i32)
    rank = jnp.where(mask, rank, -1)
    chosen = jnp.where(iota((wide, size), 0) == rank, 1.0, 0.0).astype(bf16)
    rows = iota((8, size), 0)
    values = jnp.where(rows == 0, jnp.where(mask, source, 0.0), jnp.where(rows == 1, receiver, 0.0))
    got = dot(values.astype(bf16), chosen, NT)
    code = (got[0:1] * places + got[1:2]).astype(i32)
    number = jnp.sum(ones, axis=1, keepdims=True).astype(i32)
    rows = iota((8, wide), 0)
    work[...] = jnp.where(rows == 0, code, jnp.broadcast_to(number, (8, wide)))


def list_near(work, tables, places, strips):
    t = jnp.concatenate(tables, axis=1)
    mine = lax.axis_index("grp").astype(f32)
    a, pa, b, pb, upper = (t[n : n + 1] for n in range(5))
    left = (a == mine) & (upper == 0.0)
    right = (b == mine) & (upper == 0.0)
    both = (
        jnp.concatenate([jnp.where(left, 1.0, 0.0), jnp.where(right, 1.0, 0.0)], axis=1) > 0.5,
        jnp.concatenate(
            [
                (wrap_step(b - mine, strips) + 1.0) * places + pb,
                (wrap_step(a - mine, strips) + 1.0) * places + pa,
            ],
            axis=1,
        ),
        jnp.concatenate([pa, pb], axis=1),
    )
    compact(work, *both, places)


def list_across(work, tables, tables_below, places, strips):
    t, u = jnp.concatenate(tables, axis=1), jnp.concatenate(tables_below, axis=1)
    mine = lax.axis_index("grp").astype(f32)
    left = (t[0:1] == mine) & (t[4:5] == 1.0)
    right = (u[2:3] == mine) & (u[4:5] == 1.0)
    both = (
        jnp.concatenate([jnp.where(left, 1.0, 0.0), jnp.where(right, 1.0, 0.0)], axis=1) > 0.5,
        jnp.concatenate(
            [
                (wrap_step(t[2:3] - mine, strips) + 4.0) * places + t[3:4],
                (wrap_step(u[0:1] - mine, strips) + 1.0) * places + u[1:2],
            ],
            axis=1,
        ),
        jnp.concatenate([t[1:2], u[3:4]], axis=1),
    )
    compact(work, *both, places)


def tables_of(column, places):
    begin = 12 * places
    return [column[at : at + 8, :] for at in range(begin, column.shape[0], 8)]


def column_kernel(*refs, number_far, strips, slots):
    up, down, pos, lists = refs[:4]
    far = refs[4 : 4 + number_far]
    column = refs[-1]
    rows = pos.shape[0]
    for n, (src, begin) in enumerate(((down, 2 * NE), (pos, 0), (up, 2 * NE))):
        column[n * rows : (n + 1) * rows, :] = src[begin : begin + rows, :]
    at = 2 * NE + rows
    blocks = [lists[...], down[at : at + 8, :], up[at : at + 8, :]] + [r[...] for r in far]
    for n, table in enumerate(join_lists(blocks, slots, strips)):
        column[3 * rows + 8 * n : 3 * rows + 8 * n + 8, :] = table


def tap_lookup(taps, t, index):
    span = 2 * RADIUS + 1
    index = jnp.where((index >= 0) & (index < span), index, 127)
    row = jnp.broadcast_to(taps[t : t + 1, :], (8, 128))
    blocks = []
    for i in range(0, index.shape[0], 8):
        blocks.append(
            jnp.concatenate(
                [
                    jnp.take_along_axis(row, index[i : i + 8, j : j + 128], axis=1)
                    for j in range(0, index.shape[1], 128)
                ],
                axis=1,
            )
        )
    return jnp.concatenate(blocks, axis=0)


def line_table(taps, t, depth):
    half = depth // 2
    rows, lanes = iota((half, half), 0), iota((half, half), 1)
    same = tap_lookup(taps, t, lanes - rows + RADIUS)
    other = tap_lookup(taps, t, (lanes - rows + half + RADIUS) % depth)
    return jnp.concatenate(
        [jnp.concatenate([same, other], axis=1), jnp.concatenate([other, same], axis=1)], axis=0
    )


def plane_table(taps, t, x_of, y_of):
    lanes = x_of.shape[1]
    x_rows = iota((32, lanes), 0) - (RADIUS + 1)
    y_rows = iota((YR, lanes), 0) - 1
    along_x = tap_lookup(taps, t, x_rows - x_of + RADIUS)
    along_y = tap_lookup(taps, t, y_rows - y_of + RADIUS)
    return jnp.concatenate([along_x[x : x + 1, :] * along_y for x in range(XW)], axis=0)


def put_split(pair, rows, lanes, value):
    hi, lo = split(value)
    pair[0, rows, lanes] = hi
    pair[1, rows, lanes] = lo


def tables_kernel(
    taps, own, pos, line, edge_table, partial, force_out, table, smooth, src, parts, *pairs
):
    places = pos.shape[0] // 4
    depth = places * PZ
    terms = line.shape[1]
    lane_own = iota((8, 256), 1)
    own_x = lane_own[0:1] // YR - 1
    own_y = lane_own[0:1] % YR - 1
    own_x = jnp.where(lane_own[0:1] < XO * YR, own_x, 1000)
    lane = iota((1, 256), 1)
    in_up = lane < XO * YE
    in_down = (lane >= NE) & (lane < NE + XO * YE)
    local = jnp.where(in_up, lane, lane - NE)
    edge_x = jnp.where(in_up | in_down, local // YE - 1, 1000)
    edge_y = local % YE + jnp.where(in_up, MYD - 1, -(RADIUS + 1))
    own_pair = split(jnp.concatenate([own[...], jnp.zeros((16, depth), f32)], axis=0))
    for t in range(terms):
        kz = line_table(taps, t, depth)
        kh, kl = split(kz)
        line[0, t] = kh
        line[1, t] = kl
        q = dot3(own_pair, (kh, kl))
        put_split(smooth, slice(t * 256, t * 256 + 256), slice(None), q)
        put_split(table, slice(None), slice(t * 256, t * 256 + 256), plane_table(taps, t, own_x, own_y))
        put_split(
            edge_table, slice(None), slice(t * 256, t * 256 + 256), plane_table(taps, t, edge_x, edge_y)
        )
    partial[...] = dot3((table[0], table[1]), (smooth[0], smooth[1]))
    fill_sources(src, 0, rows_of(pos, 0, places), places)
    fill_receivers(parts, pos, places)
    force_out[...] = jnp.zeros_like(force_out)
    add_self(force_out, parts, src, pairs, places)


def planes_kernel(up, down, line, edge_table, partial, pk_lo, pk_hi, e_lo, e_hi, mid, smooth):
    terms = line.shape[1]
    block = jnp.concatenate(
        [
            jnp.concatenate([src[0:NE, :], src[NE : 2 * NE, :]], axis=1) for src in (up, down)
        ]
        + [jnp.zeros((256 - 2 * NE, 256), f32)],
        axis=0,
    )
    pair = split(block)
    for t in range(terms):
        q = dot3(pair, (line[0, t], line[1, t]))
        put_split(smooth, slice(t * 256, t * 256 + 256), slice(None), q)
    total = partial[...] + dot3((edge_table[0], edge_table[1]), (smooth[0], smooth[1]))
    mid[...] = total[RADIUS * YR : (RADIUS + XO) * YR, :]
    low = total[: XO * YR, :]
    high = total[2 * RADIUS * YR :, :]
    for half in range(2):
        lanes = slice(half * 128, half * 128 + 128)
        for x in range(XO):
            rows = pl.ds(half * NS + x * YO, YO)
            pk_lo[rows, :] = low[x * YR : x * YR + YO, lanes]
            pk_hi[rows, :] = high[x * YR : x * YR + YO, lanes]
        for x in range(2):
            rows = pl.ds(half * N2 + x * YO, YO)
            e_lo[rows, :] = low[x * YR : x * YR + YO, lanes]
            e_hi[rows, :] = high[(XO - 2 + x) * YR : (XO - 2 + x) * YR + YO, lanes]
        for dst, size, pad in ((pk_lo, NS, NS - XO * YO), (pk_hi, NS, NS - XO * YO), (e_lo, N2, N2 - 2 * YO), (e_hi, N2, N2 - 2 * YO)):
            dst[(half + 1) * size - pad : (half + 1) * size, :] = jnp.zeros((pad, 128), f32)


def near_kernel(column, pos, force_in, force_out, work_out, work, src, sem, parts, *pairs, strips):
    places = pos.shape[0] // 4
    rows = 4 * places
    list_near(work_out, tables_of(column, places), places, strips)
    copy = pltpu.make_async_copy(work_out, work, sem)
    copy.start()
    force_out[...] = force_in[...]
    for n in range(3):
        fill_sources(src, n, rows_of(column, n * rows, places), places)
    fill_receivers(parts, pos, places)
    copy.wait()
    add_listed(force_out, parts, src, pairs, work, places, False)


def sample_kernel(
    cells, frac, charge, masses, velocity, pos, mid, low, high, e_lo, e_hi, column, below, above, force_in,
    half_out, moved, work_out, force, work, src, grid, turned, long, sem, parts, *pairs, strips
):
    places, atoms = charge.shape
    depth = places * PZ
    rows = 4 * places
    list_across(work_out, tables_of(column, places), tables_of(below, places), places, strips)
    copy = pltpu.make_async_copy(work_out, work, sem)
    copy.start()
    grid[...] = jnp.zeros_like(grid)
    for x in range(XO):
        for half in range(2):
            lanes = slice(half * 128, half * 128 + 128)
            at_x = pl.ds(half * NS + x * YO, YO)
            value = mid[x * YR : x * YR + YO, lanes] + low[at_x, :] + high[at_x, :]
            if x < 2:
                value = value + e_lo[pl.ds(half * N2 + x * YO, YO), :]
            if x >= XO - 2:
                value = value + e_hi[pl.ds(half * N2 + (x - XO + 2) * YO, YO), :]
            grid[x * YR : x * YR + YO, lanes] = value
    body = jnp.transpose(grid[...])
    turned[PZ : PZ + depth, :] = body
    turned[0:PZ, :] = body[depth - PZ :, :]
    turned[PZ + depth : 2 * PZ + depth, :] = body[0:PZ, :]
    y_rows = iota((YR, 2 * atoms), 0)
    x_rows = iota((16, 2 * atoms), 0)
    z_rows = iota((4 * PZ, 2 * atoms), 0)
    for m in range(places // 2):
        vx, dx = spline(pair_rows(frac, 0, m))
        vy, dy = spline(pair_rows(frac, 1, m))
        vz, dz = spline(pair_rows(frac, 2, m))
        bx, by = pair_rows(cells, 0, m), pair_rows(cells, 1, m)
        bz = pair_base_z(pair_rows(cells, 2, m), atoms)
        wx, sx = place3(x_rows, bx, vx), place3(x_rows, bx, dx)
        wy, sy = place3(y_rows, by, vy), place3(y_rows, by, dy)
        both = jnp.concatenate([place3(z_rows, bz, vz), place3(z_rows, bz, dz)], axis=1)
        bh, bl = split(both)
        th, tl = split(turned[2 * PZ * m : 2 * PZ * m + 4 * PZ, :])
        sampled = dot(
            jnp.concatenate([th, th, tl], axis=0), jnp.concatenate([bh, bl, bh], axis=0), TN
        )
        shape = (YR, 2 * atoms)
        gx, gy, gz = jnp.zeros(shape, f32), jnp.zeros(shape, f32), jnp.zeros(shape, f32)
        for x in range(XO):
            plain = sampled[x * YR : (x + 1) * YR, : 2 * atoms]
            sloped = sampled[x * YR : (x + 1) * YR, 2 * atoms :]
            gx = gx + sx[x : x + 1, :] * plain
            gy = gy + wx[x : x + 1, :] * plain
            gz = gz + wx[x : x + 1, :] * sloped
        for c, value in enumerate((gx * wy, gy * sy, gz * wy)):
            line = jnp.sum(value, axis=0, keepdims=True)
            long[c, 2 * m : 2 * m + 1, :] = line[:, :atoms]
            long[c, 2 * m + 1 : 2 * m + 2, :] = line[:, atoms:]
    for n in range(6):
        fill_sources(src, n, rows_of((below, above)[n // 3], n % 3 * rows, places), places)
    fill_receivers(parts, pos, places)
    force[...] = force_in[...]
    copy.wait()
    add_listed(force, parts, src, pairs, work, places, True)
    inverse = time_step * (1.0 / masses[...])
    q = charge[...]
    short = folded_force(force, pos, places)
    for c in range(3):
        total = short[c] - 2.0 * q * long[c]
        half = velocity[c] + inverse * total
        half_out[c] = half
        moved[c * places : (c + 1) * places, :] = (
            pos[c * places : (c + 1) * places, :] + time_step * half
        )


def moved_self_kernel(moved, pos, force_out, src, parts, *pairs):
    places = pos.shape[0] // 4
    fill_sources(src, 0, moved_rows(moved, 0, pos, 0, places), places)
    fill_receivers(parts, moved, places)
    force_out[...] = jnp.zeros_like(force_out)
    add_self(force_out, parts, src, pairs, places)


def moved_near_kernel(moved, column, charged, force_in, work, force_out, src, parts, *pairs):
    places = moved.shape[0] // 3
    force_out[...] = force_in[...]
    for n in range(3):
        block = moved_rows(column, 3 * places * n, charged, 4 * places * n, places)
        fill_sources(src, n, block, places)
    fill_receivers(parts, moved, places)
    add_listed(force_out, parts, src, pairs, work, places, False)


def moved_far_kernel(
    moved, low, high, pos, below, above, force_in, work, half, masses,
    shown, speed, force, src, parts, *pairs
):
    places = pos.shape[0] // 4
    force[...] = force_in[...]
    for n in range(6):
        part, charged = ((low, below), (high, above))[n // 3]
        k = n % 3
        fill_sources(src, n, moved_rows(part, 3 * places * k, charged, 4 * places * k, places), places)
    fill_receivers(parts, moved, places)
    add_listed(force, parts, src, pairs, work, places, True)
    short = folded_force(force, pos, places)
    inverse = time_step * (1.0 / masses[...])
    for c in range(3):
        before = half[c]
        after = before + inverse * short[c]
        speed[c] = after
        shown[c] = time_step * (before + after)


def call(kernel, outs, scratch, *args, flops=0, smem=(), hbm=(), name=None):
    def space(n):
        return pltpu.SMEM if n in smem else pltpu.HBM if n in hbm else pltpu.VMEM

    return pl.pallas_call(
        kernel,
        out_shape=outs,
        in_specs=[pl.BlockSpec(memory_space=space(n)) for n in range(len(args))],
        out_specs=[pl.BlockSpec(memory_space=pltpu.VMEM)] * len(outs),
        scratch_shapes=scratch,
        cost_estimate=pl.CostEstimate(flops=flops, transcendentals=0, bytes_accessed=1 << 20),
        compiler_params=pltpu.CompilerParams(vmem_limit_bytes=20 * 1024 * 1024),
        name=name,
    )(*args)


def shifted(x, axis, distance):
    size = lax.axis_size(axis)
    return lax.ppermute(x, axis, [(i, (i + distance) % size) for i in range(size)])


def local(
    cells, offsets, charges, masses, velocity, task_first, task_second, task_count, kernel_taps
):
    cells, offsets, velocity = cells[:, 0, 0], offsets[:, 0, 0], velocity[:, 0, 0]
    charges, masses = charges[0, 0], masses[0, 0]
    places, atoms = charges.shape
    depth = places * PZ
    strips = lax.axis_size("grp")
    slots = task_first.shape[2]
    terms = kernel_taps.shape[0]
    rows = 4 * places
    number_far = strips - 3
    shape = jax.ShapeDtypeStruct
    vm = pltpu.VMEM
    dma = pltpu.SemaphoreType.DMA

    inputs = tuple(
        pltpu.with_memory_space_constraint(x, pltpu.HBM)
        for x in (cells, offsets, charges, task_first[0], task_second[0], kernel_taps)
    )
    pack = shape((2 * NE + rows + 8, 128), f32)
    own, pk_lo, pk_hi, pos, lists, taps = call(
        functools.partial(spread_kernel, strips=strips),
        [shape((XO * YR, depth), f32), pack, pack, shape((rows, 128), f32)] + [shape((8, 128), f32)] * 2,
        [vm(x.shape, x.dtype) for x in inputs] + [vm((depth + 2 * PZ, 256), f32), dma((6,))],
        *inputs, task_count,
        hbm=range(6), smem=(6,), name="spread",
    )
    up = shifted(pk_lo, "grp", -1)
    down = shifted(pk_hi, "grp", 1)
    far = [shifted(lists, "grp", d) for d in range(2, strips - 1)]
    up, down, *far = lax.optimization_barrier((up, down, *far))

    force_shape = shape((3 * (places + 1) * 8, 128), f32)
    pairs = [vm((24 * (places + 1), 128), f32)] + [vm((128, 512), f32)] * UNROLL

    def sources(blocks):
        return vm((blocks * places * 8, 128), f32)

    table_shape = (2, XW * YR, terms * 256)
    line, edge_table, partial, force = call(
        tables_kernel,
        [
            shape((2, terms, depth, depth), bf16),
            shape(table_shape, bf16),
            shape((XW * YR, depth), f32),
            force_shape,
        ],
        [vm(table_shape, bf16), vm((2, terms * 256, depth), bf16), sources(1), *pairs],
        taps, own, pos,
        flops=10**10, name="tables",
    )

    tables = -(-strips * slots // 128)
    column = call(
        functools.partial(column_kernel, number_far=number_far, strips=strips, slots=slots),
        [shape((3 * rows + 8 * tables, 128), f32)],
        [],
        up, down, pos, lists, *far,
        name="column",
    )[0]
    above = shifted(column, "patch", -1)
    below = shifted(column, "patch", 1)

    up, column = lax.optimization_barrier((up, column))
    pack = shape((2 * NS, 128), f32)
    edge = shape((2 * N2, 128), f32)
    to_low, to_high, edge_low, edge_high, mid = call(
        planes_kernel,
        [pack, pack, edge, edge, shape((XO * YR, depth), f32)],
        [vm((2, terms * 256, depth), bf16)],
        up, down, line, edge_table, partial,
        name="planes",
    )
    high = shifted(to_low, "patch", -1)
    low = shifted(to_high, "patch", 1)
    e_hi = shifted(edge_low, "patch", -2)
    e_lo = shifted(edge_high, "patch", 2)

    work = (8, 2 * 128 * tables + 128)
    force, work_near = call(
        functools.partial(near_kernel, strips=strips),
        [force_shape, shape(work, i32)],
        [pltpu.SMEM(work, i32), sources(3), dma, *pairs],
        column, pos, force,
        flops=10**10, name="near",
    )

    half, moved, work_across = call(
        functools.partial(sample_kernel, strips=strips),
        [shape((3, places, atoms), f32), shape((3 * places, 128), f32), shape(work, i32)],
        [
            vm(force_shape.shape, f32),
            pltpu.SMEM(work, i32),
            sources(6),
            vm((XO * YR, depth), f32),
            vm((depth + 2 * PZ, XO * YR), f32),
            vm((3, places, atoms), f32),
            dma,
            *pairs,
        ],
        cells, offsets, charges, masses, velocity, pos, mid, low, high, e_lo, e_hi, column, below, above, force,
        name="sample",
    )

    moved_up = shifted(moved, "grp", -1)
    moved_down = shifted(moved, "grp", 1)
    force = call(
        moved_self_kernel,
        [force_shape],
        [sources(1), *pairs],
        moved, pos,
        flops=10**10, name="moved_self",
    )[0]
    moved_column = jnp.concatenate([moved_down, moved, moved_up], axis=0)
    moved_high = shifted(moved_column, "patch", -1)
    moved_low = shifted(moved_column, "patch", 1)
    force = call(
        moved_near_kernel,
        [force_shape],
        [sources(3), *pairs],
        moved, moved_column, column, force, work_near,
        smem=(4,), flops=10**10, name="moved_near",
    )[0]
    shown, speed = call(
        moved_far_kernel,
        [shape((3, places, atoms), f32)] * 2,
        [vm(force_shape.shape, f32), sources(6), *pairs],
        moved, moved_low, moved_high, pos, below, above, force, work_across, half, masses,
        smem=(7,), name="moved_far",
    )
    return shown[:, None, None], speed[:, None, None]


def solution(mesh):
    placed = (
        P(None, "patch", "grp", None, None),
        P(None, "patch", "grp", None, None),
        P("patch", "grp", None, None),
        P("patch", "grp", None, None),
        P(None, "patch", "grp", None, None),
        P("patch", "grp", None),
        P("patch", "grp", None),
        P("patch", "grp"),
        P(),
    )
    return jax.shard_map(
        local,
        mesh=mesh,
        in_specs=placed,
        out_specs=(P(None, "patch", "grp", None, None), P(None, "patch", "grp", None, None)),
        check_vma=False,
    )
```

```python
import functools

import jax
import jax.numpy as jnp
from jax import lax
from jax.experimental import pallas as pl
from jax.experimental.pallas import tpu as pltpu
from jax.sharding import PartitionSpec as P


MXD = 8
MYD = 16
PZ = 8
RADIUS = 8

time_step = 0.5
soft_end = 65.0
push_scale = 1.0 / 4096.0

XO = MXD + 2
YO = MYD + 2
YR = 24
XW = XO + 2 * RADIUS
YE = RADIUS + 2
NE = 104
NS = 184
N2 = 40

UNROLL = 8


f32 = jnp.float32
bf16 = jnp.bfloat16
i32 = jnp.int32


def split(x):
    hi = x.astype(bf16)
    lo = (x - hi.astype(f32)).astype(bf16)
    return hi, lo


def dot(a, b, dims=(((1,), (0,)), ((), ()))):
    return lax.dot_general(a, b, dims, preferred_element_type=f32)


def dot3(a, b, dims=(((1,), (0,)), ((), ()))):
    ah, al = a
    bh, bl = b
    return dot(ah, bh, dims) + (dot(al, bh, dims) + dot(ah, bl, dims))


NT = (((1,), (1,)), ((), ()))
TN = (((0,), (0,)), ((), ()))


def iota(shape, dim):
    return lax.broadcasted_iota(i32, shape, dim)


def spline(frac):
    weights = (0.5 * (0.5 - frac) ** 2, 0.75 - frac * frac, 0.5 * (0.5 + frac) ** 2)
    slopes = (frac - 0.5, -2.0 * frac, 0.5 + frac)
    return weights, slopes


def place3(rows, base, values):
    out = jnp.where(rows == base, values[0], 0.0)
    out = jnp.where(rows == base + 1, values[1], out)
    return jnp.where(rows == base + 2, values[2], out)


def pair_rows(ref, c, m):
    if c is None:
        return jnp.concatenate([ref[2 * m : 2 * m + 1, :], ref[2 * m + 1 : 2 * m + 2, :]], axis=1)
    return jnp.concatenate([ref[c, 2 * m : 2 * m + 1, :], ref[c, 2 * m + 1 : 2 * m + 2, :]], axis=1)


def pair_base_z(cz, atoms):
    second = (iota(cz.shape, 1) >= atoms).astype(i32)
    return cz + (PZ - 1) + PZ * second


def list_block(first, second, count, places, strips, lanes):
    bits = places.bit_length() - 1
    slots = first.shape[1]
    live = iota((1, slots), 1) < count
    upper = (second >= places * strips).astype(i32)
    rest = second - upper * (places * strips)
    dead = jnp.full((1, lanes - slots), -1.0, f32)
    rows = [
        jnp.where(live, first >> bits, -1),
        first & (places - 1),
        jnp.where(live, rest >> bits, -1),
        rest & (places - 1),
        upper,
    ]
    rows = [jnp.concatenate([row.astype(f32), dead], axis=1) for row in rows]
    return jnp.concatenate(rows + [jnp.zeros((3, lanes), f32)], axis=0)


def spread_kernel(*refs, strips):
    sources, count, outs, scratch = refs[:6], refs[6], refs[7:13], refs[13:]
    own, pk_lo, pk_hi, pos, lists, taps_out = outs
    cells, frac, charge, first, second, taps, acc, sem = scratch
    copies = [
        pltpu.make_async_copy(src, dst, sem.at[n])
        for n, (src, dst) in enumerate(zip(sources, scratch[:6]))
    ]
    for copy in copies:
        copy.start()
    acc[...] = jnp.zeros_like(acc)
    pk_lo[0 : 2 * NE, :] = jnp.zeros((2 * NE, 128), f32)
    pk_hi[0 : 2 * NE, :] = jnp.zeros((2 * NE, 128), f32)
    for copy in copies:
        copy.wait()
    places, atoms = charge.shape
    depth = places * PZ
    for c in range(3):
        start = cells[c].astype(f32) + frac[c]
        for dst, at in ((pos, 0), (pk_lo, 2 * NE), (pk_hi, 2 * NE)):
            dst[at + c * places : at + (c + 1) * places, :] = start
    taps_out[...] = jnp.zeros_like(taps_out)
    taps_out[0 : taps.shape[0], 0 : taps.shape[1]] = taps[...]
    q = charge[...]
    for dst, at in ((pos, 0), (pk_lo, 2 * NE), (pk_hi, 2 * NE)):
        dst[at + 3 * places : at + 4 * places, :] = q
    block = list_block(first[...], second[...], count[0, 0], places, strips, atoms)
    at = 2 * NE + 4 * places
    lists[...] = block
    pk_lo[at : at + 8, :] = block
    pk_hi[at : at + 8, :] = block
    y_rows = iota((YR, 2 * atoms), 0)
    x_rows = iota((16, 2 * atoms), 0)
    z_rows = iota((4 * PZ, 2 * atoms), 0)
    for m in range(places // 2):
        wx = place3(x_rows, pair_rows(cells, 0, m), spline(pair_rows(frac, 0, m))[0])
        wy = place3(y_rows, pair_rows(cells, 1, m), spline(pair_rows(frac, 1, m))[0])
        wz = place3(
            z_rows, pair_base_z(pair_rows(cells, 2, m), atoms), spline(pair_rows(frac, 2, m))[0]
        )
        wy = wy * pair_rows(charge, None, m)
        table = jnp.concatenate([wx[x : x + 1, :] * wy for x in range(XO)], axis=0)
        rows = pl.ds(2 * PZ * m, 4 * PZ)
        acc[rows, : XO * YR] += dot3(split(wz), split(table), NT)
    acc[depth : depth + PZ, :] += acc[0:PZ, :]
    acc[PZ : 2 * PZ, :] += acc[depth + PZ : depth + 2 * PZ, :]
    grid = jnp.transpose(acc[PZ : PZ + depth, :])
    own[...] = grid[: XO * YR, :]
    for x in range(XO):
        for half in range(2):
            dst = pl.ds(half * NE + x * YE, YE)
            lanes = slice(half * 128, half * 128 + 128)
            pk_lo[dst, :] = own[x * YR : x * YR + YE, lanes]
            pk_hi[dst, :] = own[x * YR + YO - YE : x * YR + YO, lanes]


def fill_receivers(parts, posr, places):
    rows = iota((8, 128), 0)
    for c in range(3):
        base = 8 * (places + 1) * c
        constant = jnp.where(rows == c, -1.0, 0.0)
        for r in range(places + 1):
            parts[base + 8 * r : base + 8 * r + 8, :] = constant
        for g in range(0, places, 8):
            x = posr[c * places + g : c * places + g + 8, :]
            hi = x.astype(bf16).astype(f32)
            rest = x - hi
            mid = rest.astype(bf16).astype(f32)
            for n, value in enumerate((hi, mid, rest - mid)):
                parts[pl.ds(base + 8 * g + 4 + n, 8, stride=8), :] = value


def side_operands(parts, src, source, r, shifts):
    rows = iota((8, 128), 0)
    shift_x, shift_y, shift_z = shifts
    shift = jnp.where(rows == 0, shift_x, jnp.where(rows == 1, shift_y, shift_z))
    at = src[pl.ds(pl.multiple_of(8 * source, 8), 8), :]
    at = jnp.where(rows < 3, at - shift, at)
    hi = at.astype(bf16).astype(f32)
    rest = at - hi
    mid = rest.astype(bf16).astype(f32)
    low = rest - mid
    mid = pltpu.roll(mid, 4, 0)
    left = jnp.concatenate(
        [jnp.where(rows < 4, hi, mid), jnp.where(rows < 4, low, 1.0)], axis=0
    )
    top = []
    end = []
    for c in range(4):
        sign = 1.0 if c == 3 else -1.0
        top.append(jnp.where((rows & 3) == c, sign, 0.0))
        if c < 3:
            end.append(parts[pl.ds(pl.multiple_of(parts.shape[0] // 3 * c + 8 * r, 8), 8), :])
        else:
            end.append(jnp.where(rows == c, sign, 0.0))
    right = jnp.concatenate(
        [jnp.concatenate(top, axis=1), jnp.concatenate(end, axis=1)], axis=0
    )
    return jnp.transpose(left).astype(bf16), right.astype(bf16)


def side_push(force, pairs, r):
    shape = (8, 128)
    ax = jnp.zeros(shape, f32)
    ay = jnp.zeros(shape, f32)
    az = jnp.zeros(shape, f32)
    for k in range(16):
        rows = slice(8 * k, 8 * k + 8)
        dx = pairs[rows, 0:128]
        dy = pairs[rows, 128:256]
        dz = pairs[rows, 256:384]
        qs = pairs[rows, 384:512]
        soft = (dx * dx + dy * dy) + (dz * dz + 1.0)
        reach = jnp.maximum(soft_end - soft, 0.0)
        rs = lax.rsqrt(soft)
        t = reach * rs
        c = (t * t) * (rs * qs)
        ax = ax + c * dx
        ay = ay + c * dy
        az = az + c * dz
    for c, a in enumerate((ax, ay, az)):
        rows = pl.ds(pl.multiple_of((3 * r + c) * 8, 8), 8)
        force[rows, :] += a


def add_sides(force, parts, src, pairs, number, places, decode):
    def prepare(n, dst):
        r, source, shifts = decode(n)
        left, right = side_operands(parts, src, source, r, shifts)
        dst[...] = dot(left, right)

    def receiver(n):
        return jnp.where(n < number, decode(n)[0], places)

    for u, dst in enumerate(pairs):
        prepare(jnp.int32(u), dst)

    def body(m, carry):
        n = UNROLL * m
        for u, dst in enumerate(pairs):
            side_push(force, dst, receiver(n + u))
            prepare(n + UNROLL + u, dst)
        return carry

    lax.fori_loop(0, (number + UNROLL - 1) // UNROLL, body, 0)


def fill_sources(src, block, component, places):
    for c in range(4):
        rows = component(c)
        for g in range(0, places, 8):
            at = (block * places + g) * 8 + c
            src[pl.ds(at, 8, stride=8), :] = rows[g : g + 8, :]


def rows_of(ref, begin, places):
    return lambda c: ref[begin + c * places : begin + (c + 1) * places, :]


def moved_rows(ref, begin, charges, at, places):
    return lambda c: (
        charges[at + 3 * places : at + 4 * places, :]
        if c == 3
        else ref[begin + c * places : begin + (c + 1) * places, :]
    )


def folded_force(force, posr, places):
    part = force[0 : 24 * places, :].reshape(places, 3, 8, 128)
    total = jnp.sum(part, axis=2)
    scale = posr[3 * places : 4 * places, :] * push_scale
    return [total[:, c, :] * scale for c in range(3)]


def add_self(force, parts, src, pairs, places):
    def decode(n):
        n = jnp.minimum(n, places - 1)
        return n, n, (0.0, 0.0, 0.0)

    add_sides(force, parts, src, pairs, places, places, decode)


def add_listed(force, parts, src, pairs, work, places, across, begin, end):
    bits = places.bit_length() - 1

    def decode(n):
        code = work[0, begin + n]
        r = code & (places - 1)
        source = code >> bits
        p = source & (places - 1)
        strip = source >> bits
        slab = jnp.int32(0)
        if across:
            slab = jnp.where(strip >= 3, 1, -1)
            strip = jnp.where(strip >= 3, strip - 3, strip)
        dz = ((r - p + 1) & (places - 1)) - 1
        shifts = (
            (-MXD * slab).astype(f32),
            (-MYD * (strip - 1)).astype(f32),
            (PZ * dz).astype(f32),
        )
        return r, source, shifts

    add_sides(force, parts, src, pairs, end - begin, places, decode)


def wrap_step(delta, count):
    return jnp.where(delta > 1, delta - count, jnp.where(delta < -1, delta + count, delta))


def join_lists(blocks, slots, strips):
    lane = iota((8, 128), 1)
    group = 128 // slots
    parts = []
    for g in range(0, strips, group):
        joined = blocks[g]
        for n in range(1, group):
            block = pltpu.roll(blocks[g + n], n * slots, 1) if g + n < strips else -1.0
            joined = jnp.where(lane < n * slots, joined, block)
        parts.append(joined)
    return parts


def compact(work, mask, early, source, receiver, places):
    size = mask.shape[1]
    wide = work.shape[1]
    first = jnp.where(mask & early, 1.0, 0.0)
    rest = jnp.where(mask, 1.0, 0.0) - first
    rows = iota((8, size), 0)
    before = jnp.where(iota((size, size), 0) < iota((size, size), 1), 1.0, 0.0).astype(bf16)
    rank = dot(jnp.where(rows == 0, first, rest).astype(bf16), before)
    firsts = jnp.sum(first, axis=1, keepdims=True)
    number = firsts + jnp.sum(rest, axis=1, keepdims=True)
    rank = jnp.where(first > 0.5, rank[0:1], firsts + rank[1:2]).astype(i32)
    rank = jnp.where(mask, rank, -1)
    chosen = jnp.where(iota((wide, size), 0) == rank, 1.0, 0.0).astype(bf16)
    values = jnp.where(rows == 0, jnp.where(mask, source, 0.0), jnp.where(rows == 1, receiver, 0.0))
    got = dot(values.astype(bf16), chosen, NT)
    code = (got[0:1] * places + got[1:2]).astype(i32)
    rows = iota((8, wide), 0)
    counts = jnp.where(rows == 1, number.astype(i32), firsts.astype(i32))
    work[...] = jnp.where(rows == 0, code, counts)


def list_near(work, tables, places, strips):
    t = jnp.concatenate(tables, axis=1)
    mine = lax.axis_index("grp").astype(f32)
    a, pa, b, pb, upper = (t[n : n + 1] for n in range(5))
    left = (a == mine) & (upper == 0.0)
    right = (b == mine) & (upper == 0.0)
    mask = jnp.concatenate([jnp.where(left, 1.0, 0.0), jnp.where(right, 1.0, 0.0)], axis=1) > 0.5
    both = (
        mask,
        mask,
        jnp.concatenate(
            [
                (wrap_step(b - mine, strips) + 1.0) * places + pb,
                (wrap_step(a - mine, strips) + 1.0) * places + pa,
            ],
            axis=1,
        ),
        jnp.concatenate([pa, pb], axis=1),
    )
    compact(work, *both, places)


def list_across(work, tables, tables_below, places, strips):
    t, u = jnp.concatenate(tables, axis=1), jnp.concatenate(tables_below, axis=1)
    mine = lax.axis_index("grp").astype(f32)
    left = (t[0:1] == mine) & (t[4:5] == 1.0)
    right = (u[2:3] == mine) & (u[4:5] == 1.0)
    both = (
        jnp.concatenate([jnp.where(left, 1.0, 0.0), jnp.where(right, 1.0, 0.0)], axis=1) > 0.5,
        jnp.concatenate([t[2:3], u[0:1]], axis=1) == mine,
        jnp.concatenate(
            [
                (wrap_step(t[2:3] - mine, strips) + 4.0) * places + t[3:4],
                (wrap_step(u[0:1] - mine, strips) + 1.0) * places + u[1:2],
            ],
            axis=1,
        ),
        jnp.concatenate([t[1:2], u[3:4]], axis=1),
    )
    compact(work, *both, places)


def tables_of(column, places):
    begin = 12 * places
    return [column[at : at + 8, :] for at in range(begin, column.shape[0], 8)]


def column_kernel(*refs, number_far, strips, slots):
    up, down, pos, lists = refs[:4]
    far = refs[4 : 4 + number_far]
    column = refs[-1]
    rows = pos.shape[0]
    for n, (src, begin) in enumerate(((down, 2 * NE), (pos, 0), (up, 2 * NE))):
        column[n * rows : (n + 1) * rows, :] = src[begin : begin + rows, :]
    at = 2 * NE + rows
    blocks = [lists[...], down[at : at + 8, :], up[at : at + 8, :]] + [r[...] for r in far]
    for n, table in enumerate(join_lists(blocks, slots, strips)):
        column[3 * rows + 8 * n : 3 * rows + 8 * n + 8, :] = table


def tap_lookup(taps, t, index):
    span = 2 * RADIUS + 1
    index = jnp.where((index >= 0) & (index < span), index, 127)
    row = jnp.broadcast_to(taps[t : t + 1, :], (8, 128))
    blocks = []
    for i in range(0, index.shape[0], 8):
        blocks.append(
            jnp.concatenate(
                [
                    jnp.take_along_axis(row, index[i : i + 8, j : j + 128], axis=1)
                    for j in range(0, index.shape[1], 128)
                ],
                axis=1,
            )
        )
    return jnp.concatenate(blocks, axis=0)


def line_table(taps, t, depth):
    half = depth // 2
    rows, lanes = iota((half, half), 0), iota((half, half), 1)
    same = tap_lookup(taps, t, lanes - rows + RADIUS)
    other = tap_lookup(taps, t, (lanes - rows + half + RADIUS) % depth)
    return jnp.concatenate(
        [jnp.concatenate([same, other], axis=1), jnp.concatenate([other, same], axis=1)], axis=0
    )


def plane_table(taps, t, x_of, y_of):
    lanes = x_of.shape[1]
    x_rows = iota((32, lanes), 0) - (RADIUS + 1)
    y_rows = iota((YR, lanes), 0) - 1
    along_x = tap_lookup(taps, t, x_rows - x_of + RADIUS)
    along_y = tap_lookup(taps, t, y_rows - y_of + RADIUS)
    return jnp.concatenate([along_x[x : x + 1, :] * along_y for x in range(XW)], axis=0)


def put_split(pair, rows, lanes, value):
    hi, lo = split(value)
    pair[0, rows, lanes] = hi
    pair[1, rows, lanes] = lo


def tables_kernel(
    taps, own, pos, line, edge_table, partial, force_out, parts, table, smooth, src, *pairs
):
    places = pos.shape[0] // 4
    depth = places * PZ
    terms = line.shape[1]
    lane_own = iota((8, 256), 1)
    own_x = lane_own[0:1] // YR - 1
    own_y = lane_own[0:1] % YR - 1
    own_x = jnp.where(lane_own[0:1] < XO * YR, own_x, 1000)
    lane = iota((1, 256), 1)
    in_up = lane < XO * YE
    in_down = (lane >= NE) & (lane < NE + XO * YE)
    local = jnp.where(in_up, lane, lane - NE)
    edge_x = jnp.where(in_up | in_down, local // YE - 1, 1000)
    edge_y = local % YE + jnp.where(in_up, MYD - 1, -(RADIUS + 1))
    own_pair = split(jnp.concatenate([own[...], jnp.zeros((16, depth), f32)], axis=0))
    for t in range(terms):
        kz = line_table(taps, t, depth)
        kh, kl = split(kz)
        line[0, t] = kh
        line[1, t] = kl
        q = dot3(own_pair, (kh, kl))
        put_split(smooth, slice(t * 256, t * 256 + 256), slice(None), q)
        put_split(table, slice(None), slice(t * 256, t * 256 + 256), plane_table(taps, t, own_x, own_y))
        put_split(
            edge_table, slice(None), slice(t * 256, t * 256 + 256), plane_table(taps, t, edge_x, edge_y)
        )
    partial[...] = dot3((table[0], table[1]), (smooth[0], smooth[1]))
    fill_sources(src, 0, rows_of(pos, 0, places), places)
    fill_receivers(parts, pos, places)
    force_out[...] = jnp.zeros_like(force_out)
    add_self(force_out, parts, src, pairs, places)


def planes_kernel(up, down, line, edge_table, partial, pk_lo, pk_hi, e_lo, e_hi, mid, smooth):
    terms = line.shape[1]
    block = jnp.concatenate(
        [
            jnp.concatenate([src[0:NE, :], src[NE : 2 * NE, :]], axis=1) for src in (up, down)
        ]
        + [jnp.zeros((256 - 2 * NE, 256), f32)],
        axis=0,
    )
    pair = split(block)
    for t in range(terms):
        q = dot3(pair, (line[0, t], line[1, t]))
        put_split(smooth, slice(t * 256, t * 256 + 256), slice(None), q)
    total = partial[...] + dot3((edge_table[0], edge_table[1]), (smooth[0], smooth[1]))
    mid[...] = total[RADIUS * YR : (RADIUS + XO) * YR, :]
    low = total[: XO * YR, :]
    high = total[2 * RADIUS * YR :, :]
    for half in range(2):
        lanes = slice(half * 128, half * 128 + 128)
        for x in range(XO):
            rows = pl.ds(half * NS + x * YO, YO)
            pk_lo[rows, :] = low[x * YR : x * YR + YO, lanes]
            pk_hi[rows, :] = high[x * YR : x * YR + YO, lanes]
        for x in range(2):
            rows = pl.ds(half * N2 + x * YO, YO)
            e_lo[rows, :] = low[x * YR : x * YR + YO, lanes]
            e_hi[rows, :] = high[(XO - 2 + x) * YR : (XO - 2 + x) * YR + YO, lanes]
        for dst, size, pad in ((pk_lo, NS, NS - XO * YO), (pk_hi, NS, NS - XO * YO), (e_lo, N2, N2 - 2 * YO), (e_hi, N2, N2 - 2 * YO)):
            dst[(half + 1) * size - pad : (half + 1) * size, :] = jnp.zeros((pad, 128), f32)


def near_kernel(column, pos, force_in, parts, force_out, work_out, work, src, sem, *pairs, strips):
    places = pos.shape[0] // 4
    rows = 4 * places
    list_near(work_out, tables_of(column, places), places, strips)
    copy = pltpu.make_async_copy(work_out, work, sem)
    copy.start()
    force_out[...] = force_in[...]
    for n in range(3):
        fill_sources(src, n, rows_of(column, n * rows, places), places)
    copy.wait()
    add_listed(force_out, parts, src, pairs, work, places, False, 0, work[1, 0])


def sample_kernel(cells, frac, charge, mid, low, high, e_lo, e_hi, long, grid, turned):
    places, atoms = charge.shape
    depth = places * PZ
    grid[...] = jnp.zeros_like(grid)
    for x in range(XO):
        for half in range(2):
            lanes = slice(half * 128, half * 128 + 128)
            at_x = pl.ds(half * NS + x * YO, YO)
            value = mid[x * YR : x * YR + YO, lanes] + low[at_x, :] + high[at_x, :]
            if x < 2:
                value = value + e_lo[pl.ds(half * N2 + x * YO, YO), :]
            if x >= XO - 2:
                value = value + e_hi[pl.ds(half * N2 + (x - XO + 2) * YO, YO), :]
            grid[x * YR : x * YR + YO, lanes] = value
    body = jnp.transpose(grid[...])
    turned[PZ : PZ + depth, :] = body
    turned[0:PZ, :] = body[depth - PZ :, :]
    turned[PZ + depth : 2 * PZ + depth, :] = body[0:PZ, :]
    y_rows = iota((YR, 2 * atoms), 0)
    x_rows = iota((16, 2 * atoms), 0)
    z_rows = iota((4 * PZ, 2 * atoms), 0)
    for m in range(places // 2):
        vx, dx = spline(pair_rows(frac, 0, m))
        vy, dy = spline(pair_rows(frac, 1, m))
        vz, dz = spline(pair_rows(frac, 2, m))
        bx, by = pair_rows(cells, 0, m), pair_rows(cells, 1, m)
        bz = pair_base_z(pair_rows(cells, 2, m), atoms)
        wx, sx = place3(x_rows, bx, vx), place3(x_rows, bx, dx)
        wy, sy = place3(y_rows, by, vy), place3(y_rows, by, dy)
        both = jnp.concatenate([place3(z_rows, bz, vz), place3(z_rows, bz, dz)], axis=1)
        bh, bl = split(both)
        th, tl = split(turned[2 * PZ * m : 2 * PZ * m + 4 * PZ, :])
        sampled = dot(
            jnp.concatenate([th, th, tl], axis=0), jnp.concatenate([bh, bl, bh], axis=0), TN
        )
        shape = (YR, 2 * atoms)
        gx, gy, gz = jnp.zeros(shape, f32), jnp.zeros(shape, f32), jnp.zeros(shape, f32)
        for x in range(XO):
            plain = sampled[x * YR : (x + 1) * YR, : 2 * atoms]
            sloped = sampled[x * YR : (x + 1) * YR, 2 * atoms :]
            gx = gx + sx[x : x + 1, :] * plain
            gy = gy + wx[x : x + 1, :] * plain
            gz = gz + wx[x : x + 1, :] * sloped
        for c, value in enumerate((gx * wy, gy * sy, gz * wy)):
            line = jnp.sum(value, axis=0, keepdims=True)
            long[c, 2 * m : 2 * m + 1, :] = line[:, :atoms]
            long[c, 2 * m + 1 : 2 * m + 2, :] = line[:, atoms:]


def far_kernel(
    charge, masses, velocity, pos, long, column, below, above, force_in, parts,
    half_out, moved, work_out, force, work, src, sem, *pairs, strips
):
    places = charge.shape[0]
    rows = 4 * places
    list_across(work_out, tables_of(column, places), tables_of(below, places), places, strips)
    copy = pltpu.make_async_copy(work_out, work, sem)
    copy.start()
    for n in range(6):
        fill_sources(src, n, rows_of((below, above)[n // 3], n % 3 * rows, places), places)
    force[...] = force_in[...]
    copy.wait()
    add_listed(force, parts, src, pairs, work, places, True, 0, work[1, 0])
    inverse = time_step * (1.0 / masses[...])
    q = charge[...]
    short = folded_force(force, pos, places)
    for c in range(3):
        total = short[c] - 2.0 * q * long[c]
        half = velocity[c] + inverse * total
        half_out[c] = half
        moved[c * places : (c + 1) * places, :] = (
            pos[c * places : (c + 1) * places, :] + time_step * half
        )


def moved_self_kernel(moved, pos, force_out, parts, src, *pairs):
    places = pos.shape[0] // 4
    fill_sources(src, 0, moved_rows(moved, 0, pos, 0, places), places)
    fill_receivers(parts, moved, places)
    force_out[...] = jnp.zeros_like(force_out)
    add_self(force_out, parts, src, pairs, places)


def moved_near_kernel(
    moved, below_strip, above_strip, low, high, charged, below, above, force_in, parts, work, work_across,
    force_out, src, src_across, *pairs
):
    places = moved.shape[0] // 3
    force_out[...] = force_in[...]
    for n, part in enumerate((below_strip, moved, above_strip)):
        fill_sources(src, n, moved_rows(part, 0, charged, 4 * places * n, places), places)
    for n, part, charges in ((1, low, below), (4, high, above)):
        fill_sources(src_across, n, moved_rows(part, 0, charges, 4 * places, places), places)
    add_listed(force_out, parts, src, pairs, work, places, False, 0, work[1, 0])
    add_listed(force_out, parts, src_across, pairs, work_across, places, True, 0, work_across[2, 0])


def moved_far_kernel(
    low, high, pos, below, above, force_in, parts, work, half, masses,
    shown, speed, force, src, *pairs
):
    places = pos.shape[0] // 4
    force[...] = force_in[...]
    for n in range(2):
        part, charged = ((low, below), (high, above))[n]
        for k in range(2):
            block = moved_rows(part, 3 * places * k, charged, 8 * places * k, places)
            fill_sources(src, 3 * n + 2 * k, block, places)
    add_listed(force, parts, src, pairs, work, places, True, work[2, 0], work[1, 0])
    short = folded_force(force, pos, places)
    inverse = time_step * (1.0 / masses[...])
    for c in range(3):
        before = half[c]
        after = before + inverse * short[c]
        speed[c] = after
        shown[c] = time_step * (before + after)


def call(kernel, outs, scratch, *args, flops=0, smem=(), hbm=()):
    def space(n):
        return pltpu.SMEM if n in smem else pltpu.HBM if n in hbm else pltpu.VMEM

    return pl.pallas_call(
        kernel,
        out_shape=outs,
        in_specs=[pl.BlockSpec(memory_space=space(n)) for n in range(len(args))],
        out_specs=[pl.BlockSpec(memory_space=pltpu.VMEM)] * len(outs),
        scratch_shapes=scratch,
        cost_estimate=pl.CostEstimate(flops=flops, transcendentals=0, bytes_accessed=1 << 20),
        compiler_params=pltpu.CompilerParams(vmem_limit_bytes=20 * 1024 * 1024),
    )(*args)


def shifted(x, axis, distance):
    size = lax.axis_size(axis)
    return lax.ppermute(x, axis, [(i, (i + distance) % size) for i in range(size)])


def step(
    cells, offsets, charges, masses, velocity, task_first, task_second, task_count, kernel_taps
):
    cells, offsets, velocity = cells[:, 0, 0], offsets[:, 0, 0], velocity[:, 0, 0]
    charges, masses = charges[0, 0], masses[0, 0]
    places, atoms = charges.shape
    depth = places * PZ
    strips = lax.axis_size("grp")
    slots = task_first.shape[2]
    terms = kernel_taps.shape[0]
    rows = 4 * places
    number_far = strips - 3
    shape = jax.ShapeDtypeStruct
    vm = pltpu.VMEM
    dma = pltpu.SemaphoreType.DMA

    inputs = tuple(
        pltpu.with_memory_space_constraint(x, pltpu.HBM)
        for x in (cells, offsets, charges, task_first[0], task_second[0], kernel_taps)
    )
    pack = shape((2 * NE + rows + 8, 128), f32)
    own, pk_lo, pk_hi, pos, lists, taps = call(
        functools.partial(spread_kernel, strips=strips),
        [shape((XO * YR, depth), f32), pack, pack, shape((rows, 128), f32)] + [shape((8, 128), f32)] * 2,
        [vm(x.shape, x.dtype) for x in inputs] + [vm((depth + 2 * PZ, 256), f32), dma((6,))],
        *inputs, task_count,
        hbm=range(6), smem=(6,),
    )
    up = shifted(pk_lo, "grp", -1)
    down = shifted(pk_hi, "grp", 1)
    far = [shifted(lists, "grp", d) for d in range(2, strips - 1)]
    up, down, *far = lax.optimization_barrier((up, down, *far))

    force_shape = shape((3 * (places + 1) * 8, 128), f32)
    part_shape = shape((24 * (places + 1), 128), f32)
    pairs = [vm((128, 512), f32)] * UNROLL

    def sources(blocks):
        return vm((blocks * places * 8, 128), f32)

    table_shape = (2, XW * YR, terms * 256)
    line, edge_table, partial, force, parts = call(
        tables_kernel,
        [
            shape((2, terms, depth, depth), bf16),
            shape(table_shape, bf16),
            shape((XW * YR, depth), f32),
            force_shape,
            part_shape,
        ],
        [vm(table_shape, bf16), vm((2, terms * 256, depth), bf16), sources(1), *pairs],
        taps, own, pos,
        flops=10**10,
    )

    pack = shape((2 * NS, 128), f32)
    edge = shape((2 * N2, 128), f32)
    to_low, to_high, edge_low, edge_high, mid = call(
        planes_kernel,
        [pack, pack, edge, edge, shape((XO * YR, depth), f32)],
        [vm((2, terms * 256, depth), bf16)],
        up, down, line, edge_table, partial,
    )
    high = shifted(to_low, "patch", -1)
    low = shifted(to_high, "patch", 1)
    e_hi = shifted(edge_low, "patch", -2)
    e_lo = shifted(edge_high, "patch", 2)

    tables = -(-strips * slots // 128)
    up, mid = lax.optimization_barrier((up, mid))
    column = call(
        functools.partial(column_kernel, number_far=number_far, strips=strips, slots=slots),
        [shape((3 * rows + 8 * tables, 128), f32)],
        [],
        up, down, pos, lists, *far,
    )[0]
    above = shifted(column, "patch", -1)
    below = shifted(column, "patch", 1)

    work = (8, 2 * 128 * tables + 128)
    force, work_near = call(
        functools.partial(near_kernel, strips=strips),
        [force_shape, shape(work, i32)],
        [pltpu.SMEM(work, i32), sources(3), dma, *pairs],
        column, pos, force, parts,
        flops=10**10,
    )

    long = call(
        sample_kernel,
        [shape((3, places, atoms), f32)],
        [vm((XO * YR, depth), f32), vm((depth + 2 * PZ, XO * YR), f32)],
        cells, offsets, charges, mid, low, high, e_lo, e_hi,
    )[0]
    half, moved, work_across = call(
        functools.partial(far_kernel, strips=strips),
        [shape((3, places, atoms), f32), shape((3 * places, 128), f32), shape(work, i32)],
        [vm(force_shape.shape, f32), pltpu.SMEM(work, i32), sources(6), dma, *pairs],
        charges, masses, velocity, pos, long, column, below, above, force, parts,
    )

    moved_up = shifted(moved, "grp", -1)
    moved_down = shifted(moved, "grp", 1)
    own_high = shifted(moved, "patch", -1)
    own_low = shifted(moved, "patch", 1)
    force, parts = call(
        moved_self_kernel,
        [force_shape, part_shape],
        [sources(1), *pairs],
        moved, pos,
        flops=10**10,
    )
    beside = jnp.concatenate([moved_down, moved_up], axis=0)
    moved_high = shifted(beside, "patch", -1)
    moved_low = shifted(beside, "patch", 1)
    force = call(
        moved_near_kernel,
        [force_shape],
        [sources(3), sources(6), *pairs],
        moved, moved_down, moved_up, own_low, own_high, column, below, above, force, parts, work_near, work_across,
        smem=(10, 11), flops=10**10,
    )[0]
    shown, speed = call(
        moved_far_kernel,
        [shape((3, places, atoms), f32)] * 2,
        [vm(force_shape.shape, f32), sources(6), *pairs],
        moved_low, moved_high, pos, below, above, force, parts, work_across, half, masses,
        smem=(7,),
    )
    return shown[:, None, None], speed[:, None, None]


def solution(mesh):
    placed = (
        P(None, "patch", "grp", None, None),
        P(None, "patch", "grp", None, None),
        P("patch", "grp", None, None),
        P("patch", "grp", None, None),
        P(None, "patch", "grp", None, None),
        P("patch", "grp", None),
        P("patch", "grp", None),
        P("patch", "grp"),
        P(),
    )
    return jax.shard_map(
        step,
        mesh=mesh,
        in_specs=placed,
        out_specs=(P(None, "patch", "grp", None, None), P(None, "patch", "grp", None, None)),
        check_vma=False,
    )
```

```python
import functools

import jax
import jax.numpy as jnp
from jax import lax
from jax.experimental import pallas as pl
from jax.experimental.pallas import tpu as pltpu
from jax.sharding import PartitionSpec as P


MXD = 8
MYD = 16
PZ = 8
RADIUS = 8

time_step = 0.5
soft_end = 65.0
push_scale = 1.0 / 4096.0

XO = MXD + 2
YO = MYD + 2
YR = 24
XW = XO + 2 * RADIUS
YE = RADIUS + 2
NE = 104
NS = 184
N2 = 40

UNROLL = 8


f32 = jnp.float32
bf16 = jnp.bfloat16
i32 = jnp.int32


def split(x):
    hi = x.astype(bf16)
    lo = (x - hi.astype(f32)).astype(bf16)
    return hi, lo


def dot(a, b, dims=(((1,), (0,)), ((), ()))):
    return lax.dot_general(a, b, dims, preferred_element_type=f32)


def dot3(a, b, dims=(((1,), (0,)), ((), ()))):
    ah, al = a
    bh, bl = b
    return dot(ah, bh, dims) + (dot(al, bh, dims) + dot(ah, bl, dims))


NT = (((1,), (1,)), ((), ()))
TN = (((0,), (0,)), ((), ()))


def iota(shape, dim):
    return lax.broadcasted_iota(i32, shape, dim)


def spline(frac):
    weights = (0.5 * (0.5 - frac) ** 2, 0.75 - frac * frac, 0.5 * (0.5 + frac) ** 2)
    slopes = (frac - 0.5, -2.0 * frac, 0.5 + frac)
    return weights, slopes


def place3(rows, base, values):
    out = jnp.where(rows == base, values[0], 0.0)
    out = jnp.where(rows == base + 1, values[1], out)
    return jnp.where(rows == base + 2, values[2], out)


def pair_rows(ref, c, m):
    if c is None:
        return jnp.concatenate([ref[2 * m : 2 * m + 1, :], ref[2 * m + 1 : 2 * m + 2, :]], axis=1)
    return jnp.concatenate([ref[c, 2 * m : 2 * m + 1, :], ref[c, 2 * m + 1 : 2 * m + 2, :]], axis=1)


def fill_spline(store, frac, c, slopes):
    places = frac.shape[1]
    weights, derivs = spline(frac[c])
    for n, value in enumerate(weights + derivs if slopes else weights):
        at = (6 * c + n) * places
        store[at : at + places, :] = value


def pair_values(store, places, c, m, first):
    out = []
    for n in range(first, first + 3):
        at = (6 * c + n) * places + 2 * m
        out.append(jnp.concatenate([store[at : at + 1, :], store[at + 1 : at + 2, :]], axis=1))
    return out


def pair_base_z(cz, atoms):
    second = (iota(cz.shape, 1) >= atoms).astype(i32)
    return cz + (PZ - 1) + PZ * second


def list_block(first, second, count, places, strips, lanes):
    bits = places.bit_length() - 1
    slots = first.shape[1]
    live = iota((1, slots), 1) < count
    upper = (second >= places * strips).astype(i32)
    rest = second - upper * (places * strips)
    dead = jnp.full((1, lanes - slots), -1.0, f32)
    rows = [
        jnp.where(live, first >> bits, -1),
        first & (places - 1),
        jnp.where(live, rest >> bits, -1),
        rest & (places - 1),
        upper,
    ]
    rows = [jnp.concatenate([row.astype(f32), dead], axis=1) for row in rows]
    return jnp.concatenate(rows + [jnp.zeros((3, lanes), f32)], axis=0)


def spread_kernel(*refs, strips):
    sources, count, outs, scratch = refs[:6], refs[6], refs[7:13], refs[13:]
    own, pk_lo, pk_hi, pos, lists, taps_out = outs
    cells, frac, charge, first, second, taps, acc, sem, store = scratch
    copies = [
        pltpu.make_async_copy(src, dst, sem.at[n])
        for n, (src, dst) in enumerate(zip(sources, scratch[:6]))
    ]
    for copy in copies:
        copy.start()
    acc[...] = jnp.zeros_like(acc)
    pk_lo[0 : 2 * NE, :] = jnp.zeros((2 * NE, 128), f32)
    pk_hi[0 : 2 * NE, :] = jnp.zeros((2 * NE, 128), f32)
    for copy in copies:
        copy.wait()
    places, atoms = charge.shape
    depth = places * PZ
    for c in range(3):
        start = cells[c].astype(f32) + frac[c]
        for dst, at in ((pos, 0), (pk_lo, 2 * NE), (pk_hi, 2 * NE)):
            dst[at + c * places : at + (c + 1) * places, :] = start
    taps_out[...] = jnp.zeros_like(taps_out)
    taps_out[0 : taps.shape[0], 0 : taps.shape[1]] = taps[...]
    q = charge[...]
    for dst, at in ((pos, 0), (pk_lo, 2 * NE), (pk_hi, 2 * NE)):
        dst[at + 3 * places : at + 4 * places, :] = q
    block = list_block(first[...], second[...], count[0, 0], places, strips, atoms)
    at = 2 * NE + 4 * places
    lists[...] = block
    pk_lo[at : at + 8, :] = block
    pk_hi[at : at + 8, :] = block
    for c in range(3):
        fill_spline(store, frac, c, False)
    y_rows = iota((YR, 2 * atoms), 0)
    x_rows = iota((16, 2 * atoms), 0)
    z_rows = iota((4 * PZ, 2 * atoms), 0)
    for m in range(places // 2):
        wx = place3(x_rows, pair_rows(cells, 0, m), pair_values(store, places, 0, m, 0))
        wy = place3(y_rows, pair_rows(cells, 1, m), pair_values(store, places, 1, m, 0))
        bz = pair_base_z(pair_rows(cells, 2, m), atoms)
        wz = place3(z_rows, bz, pair_values(store, places, 2, m, 0))
        wy = wy * pair_rows(charge, None, m)
        table = jnp.concatenate([wx[x : x + 1, :] * wy for x in range(XO)], axis=0)
        rows = pl.ds(2 * PZ * m, 4 * PZ)
        wh, wl = split(wz)
        th, tl = split(table)
        acc[rows, : XO * YR] += dot(
            jnp.concatenate([wh, wl, wh], axis=1), jnp.concatenate([th, th, tl], axis=1), NT
        )
    acc[depth : depth + PZ, :] += acc[0:PZ, :]
    acc[PZ : 2 * PZ, :] += acc[depth + PZ : depth + 2 * PZ, :]
    grid = jnp.transpose(acc[PZ : PZ + depth, :])
    own[...] = grid[: XO * YR, :]
    for x in range(XO):
        for half in range(2):
            dst = pl.ds(half * NE + x * YE, YE)
            lanes = slice(half * 128, half * 128 + 128)
            pk_lo[dst, :] = own[x * YR : x * YR + YE, lanes]
            pk_hi[dst, :] = own[x * YR + YO - YE : x * YR + YO, lanes]


def fill_receivers(parts, posr, places):
    rows = iota((8, 128), 0)
    for c in range(3):
        base = 8 * (places + 1) * c
        constant = jnp.where(rows == c, -1.0, 0.0)
        for r in range(places + 1):
            parts[base + 8 * r : base + 8 * r + 8, :] = constant
        for g in range(0, places, 8):
            x = posr[c * places + g : c * places + g + 8, :]
            hi = x.astype(bf16).astype(f32)
            rest = x - hi
            mid = rest.astype(bf16).astype(f32)
            for n, value in enumerate((hi, mid, rest - mid)):
                parts[pl.ds(base + 8 * g + 4 + n, 8, stride=8), :] = value


def side_operands(parts, src, source, r, shifts):
    rows = iota((8, 128), 0)
    shift_x, shift_y, shift_z = shifts
    shift = jnp.where(rows == 0, shift_x, jnp.where(rows == 1, shift_y, shift_z))
    at = src[pl.ds(pl.multiple_of(8 * source, 8), 8), :]
    at = jnp.where(rows < 3, at - shift, at)
    hi = at.astype(bf16).astype(f32)
    rest = at - hi
    mid = rest.astype(bf16).astype(f32)
    low = rest - mid
    mid = pltpu.roll(mid, 4, 0)
    left = jnp.concatenate(
        [jnp.where(rows < 4, hi, mid), jnp.where(rows < 4, low, 1.0)], axis=0
    )
    top = []
    end = []
    for c in range(4):
        sign = 1.0 if c == 3 else -1.0
        top.append(jnp.where((rows & 3) == c, sign, 0.0))
        if c < 3:
            end.append(parts[pl.ds(pl.multiple_of(parts.shape[0] // 3 * c + 8 * r, 8), 8), :])
        else:
            end.append(jnp.where(rows == c, sign, 0.0))
    right = jnp.concatenate(
        [jnp.concatenate(top, axis=1), jnp.concatenate(end, axis=1)], axis=0
    )
    return jnp.transpose(left).astype(bf16), right.astype(bf16)


def side_push(force, pairs, r):
    shape = (8, 128)
    ax = jnp.zeros(shape, f32)
    ay = jnp.zeros(shape, f32)
    az = jnp.zeros(shape, f32)
    for k in range(16):
        rows = slice(8 * k, 8 * k + 8)
        dx = pairs[rows, 0:128]
        dy = pairs[rows, 128:256]
        dz = pairs[rows, 256:384]
        qs = pairs[rows, 384:512]
        soft = (dx * dx + dy * dy) + (dz * dz + 1.0)
        reach = jnp.maximum(soft_end - soft, 0.0)
        rs = lax.rsqrt(soft)
        t = reach * rs
        c = (t * t) * (rs * qs)
        ax = ax + c * dx
        ay = ay + c * dy
        az = az + c * dz
    for c, a in enumerate((ax, ay, az)):
        rows = pl.ds(pl.multiple_of((3 * r + c) * 8, 8), 8)
        force[rows, :] += a


def add_sides(force, parts, src, pairs, number, places, decode):
    def prepare(n, dst):
        r, source, shifts = decode(n)
        left, right = side_operands(parts, src, source, r, shifts)
        dst[...] = dot(left, right)

    def receiver(n):
        return jnp.where(n < number, decode(n)[0], places)

    def body(m, carry):
        n = UNROLL * m
        for u, dst in enumerate(pairs):
            prepare(n + u, dst)
        for u, dst in enumerate(pairs):
            side_push(force, dst, receiver(n + u))
        return carry

    lax.fori_loop(0, (number + UNROLL - 1) // UNROLL, body, 0)


def fill_sources(src, block, component, places):
    for c in range(4):
        rows = component(c)
        for g in range(0, places, 8):
            at = (block * places + g) * 8 + c
            src[pl.ds(at, 8, stride=8), :] = rows[g : g + 8, :]


def rows_of(ref, begin, places):
    return lambda c: ref[begin + c * places : begin + (c + 1) * places, :]


def moved_rows(ref, begin, charges, at, places):
    return lambda c: (
        charges[at + 3 * places : at + 4 * places, :]
        if c == 3
        else ref[begin + c * places : begin + (c + 1) * places, :]
    )


def folded_force(force, posr, places):
    part = force[0 : 24 * places, :].reshape(places, 3, 8, 128)
    total = jnp.sum(part, axis=2)
    scale = posr[3 * places : 4 * places, :] * push_scale
    return [total[:, c, :] * scale for c in range(3)]


def add_self(force, parts, src, pairs, places):
    def decode(n):
        n = jnp.minimum(n, places - 1)
        return n, n, (0.0, 0.0, 0.0)

    add_sides(force, parts, src, pairs, places, places, decode)


def add_listed(force, parts, src, pairs, work, places, across, begin, end):
    bits = places.bit_length() - 1

    def decode(n):
        code = work[0, begin + n]
        r = code & (places - 1)
        source = code >> bits
        p = source & (places - 1)
        strip = source >> bits
        slab = jnp.int32(0)
        if across:
            slab = jnp.where(strip >= 3, 1, -1)
            strip = jnp.where(strip >= 3, strip - 3, strip)
        dz = ((r - p + 1) & (places - 1)) - 1
        shifts = (
            (-MXD * slab).astype(f32),
            (-MYD * (strip - 1)).astype(f32),
            (PZ * dz).astype(f32),
        )
        return r, source, shifts

    add_sides(force, parts, src, pairs, end - begin, places, decode)


def wrap_step(delta, count):
    return jnp.where(delta > 1, delta - count, jnp.where(delta < -1, delta + count, delta))


def join_lists(blocks, slots, strips):
    lane = iota((8, 128), 1)
    group = 128 // slots
    parts = []
    for g in range(0, strips, group):
        joined = blocks[g]
        for n in range(1, group):
            block = pltpu.roll(blocks[g + n], n * slots, 1) if g + n < strips else -1.0
            joined = jnp.where(lane < n * slots, joined, block)
        parts.append(joined)
    return parts


def compact(work, mask, early, source, receiver, places):
    size = mask.shape[1]
    wide = work.shape[1]
    first = jnp.where(mask & early, 1.0, 0.0)
    rest = jnp.where(mask, 1.0, 0.0) - first
    rows = iota((8, size), 0)
    before = jnp.where(iota((size, size), 0) < iota((size, size), 1), 1.0, 0.0).astype(bf16)
    rank = dot(jnp.where(rows == 0, first, rest).astype(bf16), before)
    firsts = jnp.sum(first, axis=1, keepdims=True)
    number = firsts + jnp.sum(rest, axis=1, keepdims=True)
    rank = jnp.where(first > 0.5, rank[0:1], firsts + rank[1:2]).astype(i32)
    rank = jnp.where(mask, rank, -1)
    chosen = jnp.where(iota((wide, size), 0) == rank, 1.0, 0.0).astype(bf16)
    values = jnp.where(rows == 0, jnp.where(mask, source, 0.0), jnp.where(rows == 1, receiver, 0.0))
    got = dot(values.astype(bf16), chosen, NT)
    code = (got[0:1] * places + got[1:2]).astype(i32)
    rows = iota((8, wide), 0)
    counts = jnp.where(rows == 1, number.astype(i32), firsts.astype(i32))
    work[...] = jnp.where(rows == 0, code, counts)


def list_near(work, tables, places, strips):
    t = jnp.concatenate(tables, axis=1)
    mine = lax.axis_index("grp").astype(f32)
    a, pa, b, pb, upper = (t[n : n + 1] for n in range(5))
    left = (a == mine) & (upper == 0.0)
    right = (b == mine) & (upper == 0.0)
    mask = jnp.concatenate([jnp.where(left, 1.0, 0.0), jnp.where(right, 1.0, 0.0)], axis=1) > 0.5
    both = (
        mask,
        mask,
        jnp.concatenate(
            [
                (wrap_step(b - mine, strips) + 1.0) * places + pb,
                (wrap_step(a - mine, strips) + 1.0) * places + pa,
            ],
            axis=1,
        ),
        jnp.concatenate([pa, pb], axis=1),
    )
    compact(work, *both, places)


def list_across(work, tables, tables_below, places, strips):
    t, u = jnp.concatenate(tables, axis=1), jnp.concatenate(tables_below, axis=1)
    mine = lax.axis_index("grp").astype(f32)
    left = (t[0:1] == mine) & (t[4:5] == 1.0)
    right = (u[2:3] == mine) & (u[4:5] == 1.0)
    both = (
        jnp.concatenate([jnp.where(left, 1.0, 0.0), jnp.where(right, 1.0, 0.0)], axis=1) > 0.5,
        jnp.concatenate([t[2:3], u[0:1]], axis=1) == mine,
        jnp.concatenate(
            [
                (wrap_step(t[2:3] - mine, strips) + 4.0) * places + t[3:4],
                (wrap_step(u[0:1] - mine, strips) + 1.0) * places + u[1:2],
            ],
            axis=1,
        ),
        jnp.concatenate([t[1:2], u[3:4]], axis=1),
    )
    compact(work, *both, places)


def tables_of(column, places):
    begin = 12 * places
    return [column[at : at + 8, :] for at in range(begin, column.shape[0], 8)]


def column_kernel(*refs, number_far, strips, slots):
    up, down, pos, lists = refs[:4]
    far = refs[4 : 4 + number_far]
    column = refs[-1]
    rows = pos.shape[0]
    for n, (src, begin) in enumerate(((down, 2 * NE), (pos, 0), (up, 2 * NE))):
        column[n * rows : (n + 1) * rows, :] = src[begin : begin + rows, :]
    at = 2 * NE + rows
    blocks = [lists[...], down[at : at + 8, :], up[at : at + 8, :]] + [r[...] for r in far]
    for n, table in enumerate(join_lists(blocks, slots, strips)):
        column[3 * rows + 8 * n : 3 * rows + 8 * n + 8, :] = table


def tap_lookup(taps, t, index):
    span = 2 * RADIUS + 1
    index = jnp.where((index >= 0) & (index < span), index, 127)
    row = jnp.broadcast_to(taps[t : t + 1, :], (8, 128))
    blocks = []
    for i in range(0, index.shape[0], 8):
        blocks.append(
            jnp.concatenate(
                [
                    jnp.take_along_axis(row, index[i : i + 8, j : j + 128], axis=1)
                    for j in range(0, index.shape[1], 128)
                ],
                axis=1,
            )
        )
    return jnp.concatenate(blocks, axis=0)


def line_table(taps, t, depth):
    half = depth // 2
    rows, lanes = iota((half, half), 0), iota((half, half), 1)
    same = tap_lookup(taps, t, lanes - rows + RADIUS)
    other = tap_lookup(taps, t, (lanes - rows + half + RADIUS) % depth)
    return jnp.concatenate(
        [jnp.concatenate([same, other], axis=1), jnp.concatenate([other, same], axis=1)], axis=0
    )


def plane_table(taps, t, x_of, y_of):
    lanes = x_of.shape[1]
    x_rows = iota((32, lanes), 0) - (RADIUS + 1)
    y_rows = iota((YR, lanes), 0) - 1
    along_x = tap_lookup(taps, t, x_rows - x_of + RADIUS)
    along_y = tap_lookup(taps, t, y_rows - y_of + RADIUS)
    return jnp.concatenate([along_x[x : x + 1, :] * along_y for x in range(XW)], axis=0)


def put_split(pair, rows, lanes, value):
    hi, lo = split(value)
    pair[0, rows, lanes] = hi
    pair[1, rows, lanes] = lo


def tables_kernel(
    taps, own, pos, line, edge_table, partial, force_out, parts, table, smooth, src, *pairs
):
    places = pos.shape[0] // 4
    depth = places * PZ
    terms = line.shape[1]
    lane_own = iota((8, 256), 1)
    own_x = lane_own[0:1] // YR - 1
    own_y = lane_own[0:1] % YR - 1
    own_x = jnp.where(lane_own[0:1] < XO * YR, own_x, 1000)
    lane = iota((1, 256), 1)
    in_up = lane < XO * YE
    in_down = (lane >= NE) & (lane < NE + XO * YE)
    local = jnp.where(in_up, lane, lane - NE)
    edge_x = jnp.where(in_up | in_down, local // YE - 1, 1000)
    edge_y = local % YE + jnp.where(in_up, MYD - 1, -(RADIUS + 1))
    own_pair = split(jnp.concatenate([own[...], jnp.zeros((16, depth), f32)], axis=0))
    for t in range(terms):
        kz = line_table(taps, t, depth)
        kh, kl = split(kz)
        line[0, t] = kh
        line[1, t] = kl
        q = dot3(own_pair, (kh, kl))
        put_split(smooth, slice(t * 256, t * 256 + 256), slice(None), q)
        put_split(table, slice(None), slice(t * 256, t * 256 + 256), plane_table(taps, t, own_x, own_y))
        put_split(
            edge_table, slice(None), slice(t * 256, t * 256 + 256), plane_table(taps, t, edge_x, edge_y)
        )
    partial[...] = dot3((table[0], table[1]), (smooth[0], smooth[1]))
    fill_sources(src, 0, rows_of(pos, 0, places), places)
    fill_receivers(parts, pos, places)
    force_out[...] = jnp.zeros_like(force_out)
    add_self(force_out, parts, src, pairs, places)


def planes_kernel(up, down, line, edge_table, partial, pk_lo, pk_hi, e_lo, e_hi, mid, smooth):
    terms = line.shape[1]
    block = jnp.concatenate(
        [jnp.concatenate([src[0:NE, :], src[NE : 2 * NE, :]], axis=1) for src in (up, down)], axis=0
    )
    pair = split(block)
    for t in range(terms):
        q = dot3(pair, (line[0, t], line[1, t]))
        put_split(smooth, slice(t * 256, t * 256 + 2 * NE), slice(None), q)
        for n in range(2):
            smooth[n, t * 256 + 2 * NE : t * 256 + 256, :] = jnp.zeros((256 - 2 * NE, q.shape[1]), bf16)
    total = partial[...] + dot3((edge_table[0], edge_table[1]), (smooth[0], smooth[1]))
    mid[...] = total[RADIUS * YR : (RADIUS + XO) * YR, :]
    low = total[: XO * YR, :]
    high = total[2 * RADIUS * YR :, :]
    for half in range(2):
        lanes = slice(half * 128, half * 128 + 128)
        for x in range(XO):
            rows = pl.ds(half * NS + x * YO, YO)
            pk_lo[rows, :] = low[x * YR : x * YR + YO, lanes]
            pk_hi[rows, :] = high[x * YR : x * YR + YO, lanes]
        for x in range(2):
            rows = pl.ds(half * N2 + x * YO, YO)
            e_lo[rows, :] = low[x * YR : x * YR + YO, lanes]
            e_hi[rows, :] = high[(XO - 2 + x) * YR : (XO - 2 + x) * YR + YO, lanes]
        for dst, size, pad in ((pk_lo, NS, NS - XO * YO), (pk_hi, NS, NS - XO * YO), (e_lo, N2, N2 - 2 * YO), (e_hi, N2, N2 - 2 * YO)):
            dst[(half + 1) * size - pad : (half + 1) * size, :] = jnp.zeros((pad, 128), f32)


def near_kernel(column, pos, force_in, parts, force_out, work_out, work, src, sem, *pairs, strips):
    places = pos.shape[0] // 4
    rows = 4 * places
    list_near(work_out, tables_of(column, places), places, strips)
    copy = pltpu.make_async_copy(work_out, work, sem)
    copy.start()
    force_out[...] = force_in[...]
    for n in range(3):
        fill_sources(src, n, rows_of(column, n * rows, places), places)
    copy.wait()
    add_listed(force_out, parts, src, pairs, work, places, False, 0, work[1, 0])


def sample_kernel(
    cells, frac, charge, masses, velocity, pos, force, mid, low, high, e_lo, e_hi,
    half_out, moved, long, grid, turned, store
):
    places, atoms = charge.shape
    depth = places * PZ
    for c in range(3):
        fill_spline(store, frac, c, True)
    grid[...] = jnp.zeros_like(grid)
    for x in range(XO):
        for half in range(2):
            lanes = slice(half * 128, half * 128 + 128)
            at_x = pl.ds(half * NS + x * YO, YO)
            value = mid[x * YR : x * YR + YO, lanes] + low[at_x, :] + high[at_x, :]
            if x < 2:
                value = value + e_lo[pl.ds(half * N2 + x * YO, YO), :]
            if x >= XO - 2:
                value = value + e_hi[pl.ds(half * N2 + (x - XO + 2) * YO, YO), :]
            grid[x * YR : x * YR + YO, lanes] = value
    body = jnp.transpose(grid[...])
    turned[PZ : PZ + depth, :] = body
    turned[0:PZ, :] = body[depth - PZ :, :]
    turned[PZ + depth : 2 * PZ + depth, :] = body[0:PZ, :]
    y_rows = iota((YR, 2 * atoms), 0)
    x_rows = iota((16, 2 * atoms), 0)
    z_rows = iota((4 * PZ, 2 * atoms), 0)
    for m in range(places // 2):
        vx, dx = pair_values(store, places, 0, m, 0), pair_values(store, places, 0, m, 3)
        vy, dy = pair_values(store, places, 1, m, 0), pair_values(store, places, 1, m, 3)
        vz, dz = pair_values(store, places, 2, m, 0), pair_values(store, places, 2, m, 3)
        bx, by = pair_rows(cells, 0, m), pair_rows(cells, 1, m)
        bz = pair_base_z(pair_rows(cells, 2, m), atoms)
        wx, sx = place3(x_rows, bx, vx), place3(x_rows, bx, dx)
        wy, sy = place3(y_rows, by, vy), place3(y_rows, by, dy)
        both = jnp.concatenate([place3(z_rows, bz, vz), place3(z_rows, bz, dz)], axis=1)
        bh, bl = split(both)
        th, tl = split(turned[2 * PZ * m : 2 * PZ * m + 4 * PZ, :])
        sampled = dot(
            jnp.concatenate([th, th, tl], axis=0), jnp.concatenate([bh, bl, bh], axis=0), TN
        )
        shape = (YR, 2 * atoms)
        gx, gy, gz = jnp.zeros(shape, f32), jnp.zeros(shape, f32), jnp.zeros(shape, f32)
        for x in range(XO):
            plain = sampled[x * YR : (x + 1) * YR, : 2 * atoms]
            sloped = sampled[x * YR : (x + 1) * YR, 2 * atoms :]
            gx = gx + sx[x : x + 1, :] * plain
            gy = gy + wx[x : x + 1, :] * plain
            gz = gz + wx[x : x + 1, :] * sloped
        for c, value in enumerate((gx * wy, gy * sy, gz * wy)):
            line = jnp.sum(value, axis=0, keepdims=True)
            long[c, 2 * m : 2 * m + 1, :] = line[:, :atoms]
            long[c, 2 * m + 1 : 2 * m + 2, :] = line[:, atoms:]
    inverse = time_step * (1.0 / masses[...])
    q = charge[...]
    short = folded_force(force, pos, places)
    for c in range(3):
        total = short[c] - 2.0 * q * long[c]
        half = velocity[c] + inverse * total
        half_out[c] = half
        moved[c * places : (c + 1) * places, :] = (
            pos[c * places : (c + 1) * places, :] + time_step * half
        )


def far_kernel(
    column, below, above, force_in, parts, force, work_out, work, src, sem, *pairs, strips, places
):
    rows = 4 * places
    list_across(work_out, tables_of(column, places), tables_of(below, places), places, strips)
    copy = pltpu.make_async_copy(work_out, work, sem)
    copy.start()
    for n in range(6):
        fill_sources(src, n, rows_of((below, above)[n // 3], n % 3 * rows, places), places)
    force[...] = force_in[...]
    copy.wait()
    add_listed(force, parts, src, pairs, work, places, True, 0, work[1, 0])


def moved_self_kernel(moved, pos, force_out, parts, src, *pairs):
    places = pos.shape[0] // 4
    fill_sources(src, 0, moved_rows(moved, 0, pos, 0, places), places)
    fill_receivers(parts, moved, places)
    force_out[...] = jnp.zeros_like(force_out)
    add_self(force_out, parts, src, pairs, places)


def moved_near_kernel(
    moved, below_strip, above_strip, low, high, charged, below, above, force_in, parts, work, work_across,
    force_out, src, src_across, *pairs
):
    places = moved.shape[0] // 3
    force_out[...] = force_in[...]
    for n, part in enumerate((below_strip, moved, above_strip)):
        fill_sources(src, n, moved_rows(part, 0, charged, 4 * places * n, places), places)
    for n, part, charges in ((1, low, below), (4, high, above)):
        fill_sources(src_across, n, moved_rows(part, 0, charges, 4 * places, places), places)
    add_listed(force_out, parts, src, pairs, work, places, False, 0, work[1, 0])
    add_listed(force_out, parts, src_across, pairs, work_across, places, True, 0, work_across[2, 0])


def moved_far_kernel(
    low, high, pos, below, above, force_in, parts, work, half, masses,
    shown, speed, force, src, *pairs
):
    places = pos.shape[0] // 4
    force[...] = force_in[...]
    for n in range(2):
        part, charged = ((low, below), (high, above))[n]
        for k in range(2):
            block = moved_rows(part, 3 * places * k, charged, 8 * places * k, places)
            fill_sources(src, 3 * n + 2 * k, block, places)
    add_listed(force, parts, src, pairs, work, places, True, work[2, 0], work[1, 0])
    short = folded_force(force, pos, places)
    inverse = time_step * (1.0 / masses[...])
    for c in range(3):
        before = half[c]
        after = before + inverse * short[c]
        speed[c] = after
        shown[c] = time_step * (before + after)


def call(kernel, outs, scratch, *args, flops=0, smem=(), hbm=()):
    def space(n):
        return pltpu.SMEM if n in smem else pltpu.HBM if n in hbm else pltpu.VMEM

    return pl.pallas_call(
        kernel,
        out_shape=outs,
        in_specs=[pl.BlockSpec(memory_space=space(n)) for n in range(len(args))],
        out_specs=[pl.BlockSpec(memory_space=pltpu.VMEM)] * len(outs),
        scratch_shapes=scratch,
        cost_estimate=pl.CostEstimate(flops=flops, transcendentals=0, bytes_accessed=1 << 20),
        compiler_params=pltpu.CompilerParams(vmem_limit_bytes=20 * 1024 * 1024),
    )(*args)


def shifted(x, axis, distance):
    size = lax.axis_size(axis)
    return lax.ppermute(x, axis, [(i, (i + distance) % size) for i in range(size)])


def step(
    cells, offsets, charges, masses, velocity, task_first, task_second, task_count, kernel_taps
):
    cells, offsets, velocity = cells[:, 0, 0], offsets[:, 0, 0], velocity[:, 0, 0]
    charges, masses = charges[0, 0], masses[0, 0]
    places, atoms = charges.shape
    depth = places * PZ
    strips = lax.axis_size("grp")
    slots = task_first.shape[2]
    terms = kernel_taps.shape[0]
    rows = 4 * places
    number_far = strips - 3
    shape = jax.ShapeDtypeStruct
    vm = pltpu.VMEM
    dma = pltpu.SemaphoreType.DMA

    inputs = tuple(
        pltpu.with_memory_space_constraint(x, pltpu.HBM)
        for x in (cells, offsets, charges, task_first[0], task_second[0], kernel_taps)
    )
    pack = shape((2 * NE + rows + 8, 128), f32)
    store = vm((18 * places, atoms), f32)
    own, pk_lo, pk_hi, pos, lists, taps = call(
        functools.partial(spread_kernel, strips=strips),
        [shape((XO * YR, depth), f32), pack, pack, shape((rows, 128), f32)] + [shape((8, 128), f32)] * 2,
        [vm(x.shape, x.dtype) for x in inputs] + [vm((depth + 2 * PZ, 256), f32), dma((6,)), store],
        *inputs, task_count,
        hbm=range(6), smem=(6,),
    )
    up = shifted(pk_lo, "grp", -1)
    down = shifted(pk_hi, "grp", 1)
    far = [shifted(lists, "grp", d) for d in range(2, strips - 1)]

    force_shape = shape((3 * (places + 1) * 8, 128), f32)
    part_shape = shape((24 * (places + 1), 128), f32)
    pairs = [vm((128, 512), f32)] * UNROLL

    def sources(blocks):
        return vm((blocks * places * 8, 128), f32)

    table_shape = (2, XW * YR, terms * 256)
    line, edge_table, partial, force, parts = call(
        tables_kernel,
        [
            shape((2, terms, depth, depth), bf16),
            shape(table_shape, bf16),
            shape((XW * YR, depth), f32),
            force_shape,
            part_shape,
        ],
        [vm(table_shape, bf16), vm((2, terms * 256, depth), bf16), sources(1), *pairs],
        taps, own, pos,
        flops=10**10,
    )

    tables = -(-strips * slots // 128)
    column = call(
        functools.partial(column_kernel, number_far=number_far, strips=strips, slots=slots),
        [shape((3 * rows + 8 * tables, 128), f32)],
        [],
        up, down, pos, lists, *far,
    )[0]
    above = shifted(column, "patch", -1)
    below = shifted(column, "patch", 1)

    up, column = lax.optimization_barrier((up, column))
    pack = shape((2 * NS, 128), f32)
    edge = shape((2 * N2, 128), f32)
    to_low, to_high, edge_low, edge_high, mid = call(
        planes_kernel,
        [pack, pack, edge, edge, shape((XO * YR, depth), f32)],
        [vm((2, terms * 256, depth), bf16)],
        up, down, line, edge_table, partial,
    )
    high = shifted(to_low, "patch", -1)
    low = shifted(to_high, "patch", 1)
    e_hi = shifted(edge_low, "patch", -2)
    e_lo = shifted(edge_high, "patch", 2)

    work = (8, 2 * 128 * tables + 128)
    force, work_near = call(
        functools.partial(near_kernel, strips=strips),
        [force_shape, shape(work, i32)],
        [pltpu.SMEM(work, i32), sources(3), dma, *pairs],
        column, pos, force, parts,
        flops=10**10,
    )

    force, work_across = call(
        functools.partial(far_kernel, strips=strips, places=places),
        [force_shape, shape(work, i32)],
        [pltpu.SMEM(work, i32), sources(6), dma, *pairs],
        column, below, above, force, parts,
        flops=10**10,
    )
    half, moved = call(
        sample_kernel,
        [shape((3, places, atoms), f32), shape((3 * places, 128), f32)],
        [
            vm((3, places, atoms), f32),
            vm((XO * YR, depth), f32),
            vm((depth + 2 * PZ, XO * YR), f32),
            store,
        ],
        cells, offsets, charges, masses, velocity, pos, force, mid, low, high, e_lo, e_hi,
    )

    moved_up = shifted(moved, "grp", -1)
    moved_down = shifted(moved, "grp", 1)
    own_high = shifted(moved, "patch", -1)
    own_low = shifted(moved, "patch", 1)
    force, parts = call(
        moved_self_kernel,
        [force_shape, part_shape],
        [sources(1), *pairs],
        moved, pos,
        flops=10**10,
    )
    beside = jnp.concatenate([moved_down, moved_up], axis=0)
    moved_high = shifted(beside, "patch", -1)
    moved_low = shifted(beside, "patch", 1)
    force = call(
        moved_near_kernel,
        [force_shape],
        [sources(3), sources(6), *pairs],
        moved, moved_down, moved_up, own_low, own_high, column, below, above, force, parts, work_near, work_across,
        smem=(10, 11), flops=10**10,
    )[0]
    shown, speed = call(
        moved_far_kernel,
        [shape((3, places, atoms), f32)] * 2,
        [vm(force_shape.shape, f32), sources(6), *pairs],
        moved_low, moved_high, pos, below, above, force, parts, work_across, half, masses,
        smem=(7,),
    )
    return shown[:, None, None], speed[:, None, None]


def solution(mesh):
    placed = (
        P(None, "patch", "grp", None, None),
        P(None, "patch", "grp", None, None),
        P("patch", "grp", None, None),
        P("patch", "grp", None, None),
        P(None, "patch", "grp", None, None),
        P("patch", "grp", None),
        P("patch", "grp", None),
        P("patch", "grp"),
        P(),
    )
    return jax.shard_map(
        step,
        mesh=mesh,
        in_specs=placed,
        out_specs=(P(None, "patch", "grp", None, None), P(None, "patch", "grp", None, None)),
        check_vma=False,
    )
```

```python
import functools

import jax
import jax.numpy as jnp
from jax import lax
from jax.experimental import pallas as pl
from jax.experimental.pallas import tpu as pltpu
from jax.sharding import PartitionSpec as P


MXD = 8
MYD = 16
PZ = 8
RADIUS = 8

time_step = 0.5
soft_end = 65.0
push_scale = 1.0 / 4096.0

XO = MXD + 2
YO = MYD + 2
YR = 24
XW = XO + 2 * RADIUS
YE = RADIUS + 2
NE = 104
NS = 184
N2 = 40

UNROLL = 8


f32 = jnp.float32
bf16 = jnp.bfloat16
i32 = jnp.int32


def split(x):
    hi = x.astype(bf16)
    lo = (x - hi.astype(f32)).astype(bf16)
    return hi, lo


def dot(a, b, dims=(((1,), (0,)), ((), ()))):
    return lax.dot_general(a, b, dims, preferred_element_type=f32)


def dot3(a, b, dims=(((1,), (0,)), ((), ()))):
    ah, al = a
    bh, bl = b
    return dot(ah, bh, dims) + (dot(al, bh, dims) + dot(ah, bl, dims))


NT = (((1,), (1,)), ((), ()))
TN = (((0,), (0,)), ((), ()))


def iota(shape, dim):
    return lax.broadcasted_iota(i32, shape, dim)


def spline(frac):
    weights = (0.5 * (0.5 - frac) ** 2, 0.75 - frac * frac, 0.5 * (0.5 + frac) ** 2)
    slopes = (frac - 0.5, -2.0 * frac, 0.5 + frac)
    return weights, slopes


def place3(rows, base, values):
    out = jnp.where(rows == base, values[0], 0.0)
    out = jnp.where(rows == base + 1, values[1], out)
    return jnp.where(rows == base + 2, values[2], out)


def pair_rows(ref, c, m):
    if c is None:
        return jnp.concatenate([ref[2 * m : 2 * m + 1, :], ref[2 * m + 1 : 2 * m + 2, :]], axis=1)
    return jnp.concatenate([ref[c, 2 * m : 2 * m + 1, :], ref[c, 2 * m + 1 : 2 * m + 2, :]], axis=1)


def fill_spline(store, frac, c, slopes):
    places = frac.shape[1]
    weights, derivs = spline(frac[c])
    for n, value in enumerate(weights + derivs if slopes else weights):
        at = (6 * c + n) * places
        store[at : at + places, :] = value


def pair_values(store, places, c, m, first):
    out = []
    for n in range(first, first + 3):
        at = (6 * c + n) * places + 2 * m
        out.append(jnp.concatenate([store[at : at + 1, :], store[at + 1 : at + 2, :]], axis=1))
    return out


def pair_base_z(cz, atoms):
    second = (iota(cz.shape, 1) >= atoms).astype(i32)
    return cz + (PZ - 1) + PZ * second


def list_block(first, second, count, places, strips, lanes):
    bits = places.bit_length() - 1
    slots = first.shape[1]
    live = iota((1, slots), 1) < count
    upper = (second >= places * strips).astype(i32)
    rest = second - upper * (places * strips)
    dead = jnp.full((1, lanes - slots), -1.0, f32)
    rows = [
        jnp.where(live, first >> bits, -1),
        first & (places - 1),
        jnp.where(live, rest >> bits, -1),
        rest & (places - 1),
        upper,
    ]
    rows = [jnp.concatenate([row.astype(f32), dead], axis=1) for row in rows]
    return jnp.concatenate(rows + [jnp.zeros((3, lanes), f32)], axis=0)


def spread_kernel(*refs, strips):
    sources, count, outs, scratch = refs[:6], refs[6], refs[7:13], refs[13:]
    own, pk_lo, pk_hi, pos, lists, taps_out = outs
    cells, frac, charge, first, second, taps, acc, sem, store = scratch
    copies = [
        pltpu.make_async_copy(src, dst, sem.at[n])
        for n, (src, dst) in enumerate(zip(sources, scratch[:6]))
    ]
    for copy in copies:
        copy.start()
    acc[...] = jnp.zeros_like(acc)
    pk_lo[0 : 2 * NE, :] = jnp.zeros((2 * NE, 128), f32)
    pk_hi[0 : 2 * NE, :] = jnp.zeros((2 * NE, 128), f32)
    for copy in copies:
        copy.wait()
    places, atoms = charge.shape
    depth = places * PZ
    for c in range(3):
        start = cells[c].astype(f32) + frac[c]
        for dst, at in ((pos, 0), (pk_lo, 2 * NE), (pk_hi, 2 * NE)):
            dst[at + c * places : at + (c + 1) * places, :] = start
    taps_out[...] = jnp.zeros_like(taps_out)
    taps_out[0 : taps.shape[0], 0 : taps.shape[1]] = taps[...]
    q = charge[...]
    for dst, at in ((pos, 0), (pk_lo, 2 * NE), (pk_hi, 2 * NE)):
        dst[at + 3 * places : at + 4 * places, :] = q
    block = list_block(first[...], second[...], count[0, 0], places, strips, atoms)
    at = 2 * NE + 4 * places
    lists[...] = block
    pk_lo[at : at + 8, :] = block
    pk_hi[at : at + 8, :] = block
    for c in range(3):
        fill_spline(store, frac, c, False)
    y_rows = iota((YR, 2 * atoms), 0)
    x_rows = iota((16, 2 * atoms), 0)
    z_rows = iota((4 * PZ, 2 * atoms), 0)
    for m in range(places // 2):
        wx = place3(x_rows, pair_rows(cells, 0, m), pair_values(store, places, 0, m, 0))
        wy = place3(y_rows, pair_rows(cells, 1, m), pair_values(store, places, 1, m, 0))
        bz = pair_base_z(pair_rows(cells, 2, m), atoms)
        wz = place3(z_rows, bz, pair_values(store, places, 2, m, 0))
        wy = wy * pair_rows(charge, None, m)
        table = jnp.concatenate([wx[x : x + 1, :] * wy for x in range(XO)], axis=0)
        rows = pl.ds(2 * PZ * m, 4 * PZ)
        wh, wl = split(wz)
        th, tl = split(table)
        acc[rows, : XO * YR] += dot(
            jnp.concatenate([wh, wl, wh], axis=1), jnp.concatenate([th, th, tl], axis=1), NT
        )
    acc[depth : depth + PZ, :] += acc[0:PZ, :]
    acc[PZ : 2 * PZ, :] += acc[depth + PZ : depth + 2 * PZ, :]
    grid = jnp.transpose(acc[PZ : PZ + depth, :])
    own[...] = grid[: XO * YR, :]
    for x in range(XO):
        for half in range(2):
            dst = pl.ds(half * NE + x * YE, YE)
            lanes = slice(half * 128, half * 128 + 128)
            pk_lo[dst, :] = own[x * YR : x * YR + YE, lanes]
            pk_hi[dst, :] = own[x * YR + YO - YE : x * YR + YO, lanes]


def fill_receivers(parts, posr, places):
    rows = iota((8, 128), 0)
    for c in range(3):
        base = 8 * (places + 1) * c
        constant = jnp.where(rows == c, -1.0, 0.0)
        for r in range(places + 1):
            parts[base + 8 * r : base + 8 * r + 8, :] = constant
        for g in range(0, places, 8):
            x = posr[c * places + g : c * places + g + 8, :]
            hi = x.astype(bf16).astype(f32)
            rest = x - hi
            mid = rest.astype(bf16).astype(f32)
            for n, value in enumerate((hi, mid, rest - mid)):
                parts[pl.ds(base + 8 * g + 4 + n, 8, stride=8), :] = value


def side_operands(parts, src, source, r, shifts):
    rows = iota((8, 128), 0)
    shift_x, shift_y, shift_z = shifts
    shift = jnp.where(rows == 0, shift_x, jnp.where(rows == 1, shift_y, shift_z))
    at = src[pl.ds(pl.multiple_of(8 * source, 8), 8), :]
    at = jnp.where(rows < 3, at - shift, at)
    hi = at.astype(bf16).astype(f32)
    rest = at - hi
    mid = rest.astype(bf16).astype(f32)
    low = rest - mid
    mid = pltpu.roll(mid, 4, 0)
    left = jnp.concatenate(
        [jnp.where(rows < 4, hi, mid), jnp.where(rows < 4, low, 1.0)], axis=0
    )
    top = []
    end = []
    for c in range(4):
        sign = 1.0 if c == 3 else -1.0
        top.append(jnp.where((rows & 3) == c, sign, 0.0))
        if c < 3:
            end.append(parts[pl.ds(pl.multiple_of(parts.shape[0] // 3 * c + 8 * r, 8), 8), :])
        else:
            end.append(jnp.where(rows == c, sign, 0.0))
    right = jnp.concatenate(
        [jnp.concatenate(top, axis=1), jnp.concatenate(end, axis=1)], axis=0
    )
    return jnp.transpose(left).astype(bf16), right.astype(bf16)


def side_push(force, pairs, r):
    shape = (8, 128)
    ax = jnp.zeros(shape, f32)
    ay = jnp.zeros(shape, f32)
    az = jnp.zeros(shape, f32)
    for k in range(16):
        rows = slice(8 * k, 8 * k + 8)
        dx = pairs[rows, 0:128]
        dy = pairs[rows, 128:256]
        dz = pairs[rows, 256:384]
        qs = pairs[rows, 384:512]
        soft = (dx * dx + dy * dy) + (dz * dz + 1.0)
        reach = jnp.maximum(soft_end - soft, 0.0)
        rs = lax.rsqrt(soft)
        t = reach * rs
        c = (t * t) * (rs * qs)
        ax = ax + c * dx
        ay = ay + c * dy
        az = az + c * dz
    for c, a in enumerate((ax, ay, az)):
        rows = pl.ds(pl.multiple_of((3 * r + c) * 8, 8), 8)
        force[rows, :] += a


def add_sides(force, parts, src, pairs, number, places, decode):
    def prepare(n, dst):
        r, source, shifts = decode(n)
        left, right = side_operands(parts, src, source, r, shifts)
        dst[...] = dot(left, right)

    def receiver(n):
        return jnp.where(n < number, decode(n)[0], places)

    def body(m, carry):
        n = len(pairs) * m
        for u, dst in enumerate(pairs):
            prepare(n + u, dst)
        for u, dst in enumerate(pairs):
            side_push(force, dst, receiver(n + u))
        return carry

    lax.fori_loop(0, (number + len(pairs) - 1) // len(pairs), body, 0)


def fill_sources(src, block, component, places):
    for c in range(4):
        rows = component(c)
        for g in range(0, places, 8):
            at = (block * places + g) * 8 + c
            src[pl.ds(at, 8, stride=8), :] = rows[g : g + 8, :]


def rows_of(ref, begin, places):
    return lambda c: ref[begin + c * places : begin + (c + 1) * places, :]


def moved_rows(ref, begin, charges, at, places):
    return lambda c: (
        charges[at + 3 * places : at + 4 * places, :]
        if c == 3
        else ref[begin + c * places : begin + (c + 1) * places, :]
    )


def folded_force(force, posr, places):
    part = force[0 : 24 * places, :].reshape(places, 3, 8, 128)
    total = jnp.sum(part, axis=2)
    scale = posr[3 * places : 4 * places, :] * push_scale
    return [total[:, c, :] * scale for c in range(3)]


def add_self(force, parts, src, pairs, places):
    def decode(n):
        n = jnp.minimum(n, places - 1)
        return n, n, (0.0, 0.0, 0.0)

    add_sides(force, parts, src, pairs, places, places, decode)


def add_listed(force, parts, src, pairs, work, places, across, begin, end):
    bits = places.bit_length() - 1

    def decode(n):
        code = work[0, begin + n]
        r = code & (places - 1)
        source = code >> bits
        p = source & (places - 1)
        strip = source >> bits
        slab = jnp.int32(0)
        if across:
            slab = jnp.where(strip >= 3, 1, -1)
            strip = jnp.where(strip >= 3, strip - 3, strip)
        dz = ((r - p + 1) & (places - 1)) - 1
        shifts = (
            (-MXD * slab).astype(f32),
            (-MYD * (strip - 1)).astype(f32),
            (PZ * dz).astype(f32),
        )
        return r, source, shifts

    add_sides(force, parts, src, pairs, end - begin, places, decode)


def wrap_step(delta, count):
    return jnp.where(delta > 1, delta - count, jnp.where(delta < -1, delta + count, delta))


def join_lists(blocks, slots, strips):
    lane = iota((8, 128), 1)
    group = 128 // slots
    parts = []
    for g in range(0, strips, group):
        joined = blocks[g]
        for n in range(1, group):
            block = pltpu.roll(blocks[g + n], n * slots, 1) if g + n < strips else -1.0
            joined = jnp.where(lane < n * slots, joined, block)
        parts.append(joined)
    return parts


def compact(work, mask, early, source, receiver, places):
    size = mask.shape[1]
    wide = work.shape[1]
    first = jnp.where(mask & early, 1.0, 0.0)
    rest = jnp.where(mask, 1.0, 0.0) - first
    rows = iota((8, size), 0)
    before = jnp.where(iota((size, size), 0) < iota((size, size), 1), 1.0, 0.0).astype(bf16)
    rank = dot(jnp.where(rows == 0, first, rest).astype(bf16), before)
    firsts = jnp.sum(first, axis=1, keepdims=True)
    number = firsts + jnp.sum(rest, axis=1, keepdims=True)
    rank = jnp.where(first > 0.5, rank[0:1], firsts + rank[1:2]).astype(i32)
    rank = jnp.where(mask, rank, -1)
    chosen = jnp.where(iota((wide, size), 0) == rank, 1.0, 0.0).astype(bf16)
    values = jnp.where(rows == 0, jnp.where(mask, source, 0.0), jnp.where(rows == 1, receiver, 0.0))
    got = dot(values.astype(bf16), chosen, NT)
    code = (got[0:1] * places + got[1:2]).astype(i32)
    rows = iota((8, wide), 0)
    counts = jnp.where(rows == 1, number.astype(i32), firsts.astype(i32))
    work[...] = jnp.where(rows == 0, code, counts)


def list_near(work, tables, places, strips):
    t = jnp.concatenate(tables, axis=1)
    mine = lax.axis_index("grp").astype(f32)
    a, pa, b, pb, upper = (t[n : n + 1] for n in range(5))
    left = (a == mine) & (upper == 0.0)
    right = (b == mine) & (upper == 0.0)
    mask = jnp.concatenate([jnp.where(left, 1.0, 0.0), jnp.where(right, 1.0, 0.0)], axis=1) > 0.5
    both = (
        mask,
        mask,
        jnp.concatenate(
            [
                (wrap_step(b - mine, strips) + 1.0) * places + pb,
                (wrap_step(a - mine, strips) + 1.0) * places + pa,
            ],
            axis=1,
        ),
        jnp.concatenate([pa, pb], axis=1),
    )
    compact(work, *both, places)


def list_across(work, tables, tables_below, places, strips):
    t, u = jnp.concatenate(tables, axis=1), jnp.concatenate(tables_below, axis=1)
    mine = lax.axis_index("grp").astype(f32)
    left = (t[0:1] == mine) & (t[4:5] == 1.0)
    right = (u[2:3] == mine) & (u[4:5] == 1.0)
    both = (
        jnp.concatenate([jnp.where(left, 1.0, 0.0), jnp.where(right, 1.0, 0.0)], axis=1) > 0.5,
        jnp.concatenate([t[2:3], u[0:1]], axis=1) == mine,
        jnp.concatenate(
            [
                (wrap_step(t[2:3] - mine, strips) + 4.0) * places + t[3:4],
                (wrap_step(u[0:1] - mine, strips) + 1.0) * places + u[1:2],
            ],
            axis=1,
        ),
        jnp.concatenate([t[1:2], u[3:4]], axis=1),
    )
    compact(work, *both, places)


def tables_of(column, places):
    begin = 12 * places
    return [column[at : at + 8, :] for at in range(begin, column.shape[0], 8)]


def column_kernel(*refs, number_far, strips, slots):
    up, down, pos, lists = refs[:4]
    far = refs[4 : 4 + number_far]
    column = refs[-1]
    rows = pos.shape[0]
    for n, (src, begin) in enumerate(((down, 2 * NE), (pos, 0), (up, 2 * NE))):
        column[n * rows : (n + 1) * rows, :] = src[begin : begin + rows, :]
    at = 2 * NE + rows
    blocks = [lists[...], down[at : at + 8, :], up[at : at + 8, :]] + [r[...] for r in far]
    for n, table in enumerate(join_lists(blocks, slots, strips)):
        column[3 * rows + 8 * n : 3 * rows + 8 * n + 8, :] = table


def tap_lookup(taps, t, index):
    span = 2 * RADIUS + 1
    index = jnp.where((index >= 0) & (index < span), index, 127)
    row = jnp.broadcast_to(taps[t : t + 1, :], (8, 128))
    blocks = []
    for i in range(0, index.shape[0], 8):
        blocks.append(
            jnp.concatenate(
                [
                    jnp.take_along_axis(row, index[i : i + 8, j : j + 128], axis=1)
                    for j in range(0, index.shape[1], 128)
                ],
                axis=1,
            )
        )
    return jnp.concatenate(blocks, axis=0)


def line_table(taps, t, depth):
    half = depth // 2
    rows, lanes = iota((half, half), 0), iota((half, half), 1)
    same = tap_lookup(taps, t, lanes - rows + RADIUS)
    other = tap_lookup(taps, t, (lanes - rows + half + RADIUS) % depth)
    return jnp.concatenate(
        [jnp.concatenate([same, other], axis=1), jnp.concatenate([other, same], axis=1)], axis=0
    )


def plane_table(taps, t, x_of, y_of):
    lanes = x_of.shape[1]
    x_rows = iota((32, lanes), 0) - (RADIUS + 1)
    y_rows = iota((YR, lanes), 0) - 1
    along_x = tap_lookup(taps, t, x_rows - x_of + RADIUS)
    along_y = tap_lookup(taps, t, y_rows - y_of + RADIUS)
    return jnp.concatenate([along_x[x : x + 1, :] * along_y for x in range(XW)], axis=0)


def put_split(pair, rows, lanes, value):
    hi, lo = split(value)
    pair[0, rows, lanes] = hi
    pair[1, rows, lanes] = lo


def tables_kernel(
    taps, own, pos, line, edge_table, partial, force_out, parts, table, smooth, src, *pairs
):
    places = pos.shape[0] // 4
    depth = places * PZ
    terms = line.shape[1]
    lane_own = iota((8, 256), 1)
    own_x = lane_own[0:1] // YR - 1
    own_y = lane_own[0:1] % YR - 1
    own_x = jnp.where(lane_own[0:1] < XO * YR, own_x, 1000)
    lane = iota((1, 256), 1)
    in_up = lane < XO * YE
    in_down = (lane >= NE) & (lane < NE + XO * YE)
    local = jnp.where(in_up, lane, lane - NE)
    edge_x = jnp.where(in_up | in_down, local // YE - 1, 1000)
    edge_y = local % YE + jnp.where(in_up, MYD - 1, -(RADIUS + 1))
    own_pair = split(jnp.concatenate([own[...], jnp.zeros((16, depth), f32)], axis=0))
    for t in range(terms):
        kz = line_table(taps, t, depth)
        kh, kl = split(kz)
        line[0, t] = kh
        line[1, t] = kl
        q = dot3(own_pair, (kh, kl))
        put_split(smooth, slice(t * 256, t * 256 + 256), slice(None), q)
        put_split(table, slice(None), slice(t * 256, t * 256 + 256), plane_table(taps, t, own_x, own_y))
        put_split(
            edge_table, slice(None), slice(t * 256, t * 256 + 256), plane_table(taps, t, edge_x, edge_y)
        )
    partial[...] = dot3((table[0], table[1]), (smooth[0], smooth[1]))
    fill_sources(src, 0, rows_of(pos, 0, places), places)
    fill_receivers(parts, pos, places)
    force_out[...] = jnp.zeros_like(force_out)
    add_self(force_out, parts, src, pairs, places)


def planes_kernel(up, down, line, edge_table, partial, pk_lo, pk_hi, e_lo, e_hi, mid, smooth):
    terms = line.shape[1]
    block = jnp.concatenate(
        [jnp.concatenate([src[0:NE, :], src[NE : 2 * NE, :]], axis=1) for src in (up, down)], axis=0
    )
    pair = split(block)
    for t in range(terms):
        q = dot3(pair, (line[0, t], line[1, t]))
        put_split(smooth, slice(t * 256, t * 256 + 2 * NE), slice(None), q)
        for n in range(2):
            smooth[n, t * 256 + 2 * NE : t * 256 + 256, :] = jnp.zeros((256 - 2 * NE, q.shape[1]), bf16)
    total = partial[...] + dot3((edge_table[0], edge_table[1]), (smooth[0], smooth[1]))
    mid[...] = total[RADIUS * YR : (RADIUS + XO) * YR, :]
    low = total[: XO * YR, :]
    high = total[2 * RADIUS * YR :, :]
    for half in range(2):
        lanes = slice(half * 128, half * 128 + 128)
        for x in range(XO):
            rows = pl.ds(half * NS + x * YO, YO)
            pk_lo[rows, :] = low[x * YR : x * YR + YO, lanes]
            pk_hi[rows, :] = high[x * YR : x * YR + YO, lanes]
        for x in range(2):
            rows = pl.ds(half * N2 + x * YO, YO)
            e_lo[rows, :] = low[x * YR : x * YR + YO, lanes]
            e_hi[rows, :] = high[(XO - 2 + x) * YR : (XO - 2 + x) * YR + YO, lanes]
        for dst, size, pad in ((pk_lo, NS, NS - XO * YO), (pk_hi, NS, NS - XO * YO), (e_lo, N2, N2 - 2 * YO), (e_hi, N2, N2 - 2 * YO)):
            dst[(half + 1) * size - pad : (half + 1) * size, :] = jnp.zeros((pad, 128), f32)


def near_kernel(column, pos, force_in, parts, force_out, work_out, work, src, sem, *pairs, strips):
    places = pos.shape[0] // 4
    rows = 4 * places
    list_near(work_out, tables_of(column, places), places, strips)
    copy = pltpu.make_async_copy(work_out, work, sem)
    copy.start()
    force_out[...] = force_in[...]
    for n in range(3):
        fill_sources(src, n, rows_of(column, n * rows, places), places)
    copy.wait()
    add_listed(force_out, parts, src, pairs, work, places, False, 0, work[1, 0])


def sample_kernel(
    cells, frac, charge, masses, velocity, pos, force, mid, low, high, e_lo, e_hi,
    half_out, moved, long, grid, turned, store
):
    places, atoms = charge.shape
    depth = places * PZ
    for c in range(3):
        fill_spline(store, frac, c, True)
    grid[...] = jnp.zeros_like(grid)
    for x in range(XO):
        for half in range(2):
            lanes = slice(half * 128, half * 128 + 128)
            at_x = pl.ds(half * NS + x * YO, YO)
            value = mid[x * YR : x * YR + YO, lanes] + low[at_x, :] + high[at_x, :]
            if x < 2:
                value = value + e_lo[pl.ds(half * N2 + x * YO, YO), :]
            if x >= XO - 2:
                value = value + e_hi[pl.ds(half * N2 + (x - XO + 2) * YO, YO), :]
            grid[x * YR : x * YR + YO, lanes] = value
    body = jnp.transpose(grid[...])
    turned[PZ : PZ + depth, :] = body
    turned[0:PZ, :] = body[depth - PZ :, :]
    turned[PZ + depth : 2 * PZ + depth, :] = body[0:PZ, :]
    y_rows = iota((YR, 2 * atoms), 0)
    x_rows = iota((16, 2 * atoms), 0)
    z_rows = iota((4 * PZ, 2 * atoms), 0)
    for m in range(places // 2):
        vx, dx = pair_values(store, places, 0, m, 0), pair_values(store, places, 0, m, 3)
        vy, dy = pair_values(store, places, 1, m, 0), pair_values(store, places, 1, m, 3)
        vz, dz = pair_values(store, places, 2, m, 0), pair_values(store, places, 2, m, 3)
        bx, by = pair_rows(cells, 0, m), pair_rows(cells, 1, m)
        bz = pair_base_z(pair_rows(cells, 2, m), atoms)
        wx, sx = place3(x_rows, bx, vx), place3(x_rows, bx, dx)
        wy, sy = place3(y_rows, by, vy), place3(y_rows, by, dy)
        both = jnp.concatenate([place3(z_rows, bz, vz), place3(z_rows, bz, dz)], axis=1)
        bh, bl = split(both)
        th, tl = split(turned[2 * PZ * m : 2 * PZ * m + 4 * PZ, :])
        sampled = dot(
            jnp.concatenate([th, th, tl], axis=0), jnp.concatenate([bh, bl, bh], axis=0), TN
        )
        shape = (YR, 2 * atoms)
        gx, gy, gz = jnp.zeros(shape, f32), jnp.zeros(shape, f32), jnp.zeros(shape, f32)
        for x in range(XO):
            plain = sampled[x * YR : (x + 1) * YR, : 2 * atoms]
            sloped = sampled[x * YR : (x + 1) * YR, 2 * atoms :]
            gx = gx + sx[x : x + 1, :] * plain
            gy = gy + wx[x : x + 1, :] * plain
            gz = gz + wx[x : x + 1, :] * sloped
        for c, value in enumerate((gx * wy, gy * sy, gz * wy)):
            line = jnp.sum(value, axis=0, keepdims=True)
            long[c, 2 * m : 2 * m + 1, :] = line[:, :atoms]
            long[c, 2 * m + 1 : 2 * m + 2, :] = line[:, atoms:]
    inverse = time_step * (1.0 / masses[...])
    q = charge[...]
    short = folded_force(force, pos, places)
    for c in range(3):
        total = short[c] - 2.0 * q * long[c]
        half = velocity[c] + inverse * total
        half_out[c] = half
        moved[c * places : (c + 1) * places, :] = (
            pos[c * places : (c + 1) * places, :] + time_step * half
        )


def far_kernel(
    column, below, above, force_in, parts, force, work_out, work, src, sem, *pairs, strips, places
):
    rows = 4 * places
    list_across(work_out, tables_of(column, places), tables_of(below, places), places, strips)
    copy = pltpu.make_async_copy(work_out, work, sem)
    copy.start()
    for n in range(6):
        fill_sources(src, n, rows_of((below, above)[n // 3], n % 3 * rows, places), places)
    force[...] = force_in[...]
    copy.wait()
    add_listed(force, parts, src, pairs, work, places, True, 0, work[1, 0])


def moved_self_kernel(moved, pos, force_out, parts, src, *pairs):
    places = pos.shape[0] // 4
    fill_sources(src, 0, moved_rows(moved, 0, pos, 0, places), places)
    fill_receivers(parts, moved, places)
    force_out[...] = jnp.zeros_like(force_out)
    add_self(force_out, parts, src, pairs, places)


def moved_near_kernel(
    moved, below_strip, above_strip, low, high, charged, below, above, force_in, parts, work, work_across,
    force_out, src, src_across, *pairs
):
    places = moved.shape[0] // 3
    force_out[...] = force_in[...]
    for n, part in enumerate((below_strip, moved, above_strip)):
        fill_sources(src, n, moved_rows(part, 0, charged, 4 * places * n, places), places)
    for n, part, charges in ((1, low, below), (4, high, above)):
        fill_sources(src_across, n, moved_rows(part, 0, charges, 4 * places, places), places)
    add_listed(force_out, parts, src, pairs, work, places, False, 0, work[1, 0])
    add_listed(force_out, parts, src_across, pairs, work_across, places, True, 0, work_across[2, 0])


def moved_far_kernel(
    low, high, pos, below, above, force_in, parts, work, half, masses,
    shown, speed, force, src, *pairs
):
    places = pos.shape[0] // 4
    force[...] = force_in[...]
    for n in range(2):
        part, charged = ((low, below), (high, above))[n]
        for k in range(2):
            block = moved_rows(part, 3 * places * k, charged, 8 * places * k, places)
            fill_sources(src, 3 * n + 2 * k, block, places)
    add_listed(force, parts, src, pairs, work, places, True, work[2, 0], work[1, 0])
    short = folded_force(force, pos, places)
    inverse = time_step * (1.0 / masses[...])
    for c in range(3):
        before = half[c]
        after = before + inverse * short[c]
        speed[c] = after
        shown[c] = time_step * (before + after)


def call(kernel, outs, scratch, *args, flops=0, smem=(), hbm=()):
    def space(n):
        return pltpu.SMEM if n in smem else pltpu.HBM if n in hbm else pltpu.VMEM

    return pl.pallas_call(
        kernel,
        out_shape=outs,
        in_specs=[pl.BlockSpec(memory_space=space(n)) for n in range(len(args))],
        out_specs=[pl.BlockSpec(memory_space=pltpu.VMEM)] * len(outs),
        scratch_shapes=scratch,
        cost_estimate=pl.CostEstimate(flops=flops, transcendentals=0, bytes_accessed=1 << 20),
        compiler_params=pltpu.CompilerParams(vmem_limit_bytes=20 * 1024 * 1024),
    )(*args)


def shifted(x, axis, distance):
    size = lax.axis_size(axis)
    return lax.ppermute(x, axis, [(i, (i + distance) % size) for i in range(size)])


def step(
    cells, offsets, charges, masses, velocity, task_first, task_second, task_count, kernel_taps
):
    cells, offsets, velocity = cells[:, 0, 0], offsets[:, 0, 0], velocity[:, 0, 0]
    charges, masses = charges[0, 0], masses[0, 0]
    places, atoms = charges.shape
    depth = places * PZ
    strips = lax.axis_size("grp")
    slots = task_first.shape[2]
    terms = kernel_taps.shape[0]
    rows = 4 * places
    number_far = strips - 3
    shape = jax.ShapeDtypeStruct
    vm = pltpu.VMEM
    dma = pltpu.SemaphoreType.DMA

    inputs = tuple(
        pltpu.with_memory_space_constraint(x, pltpu.HBM)
        for x in (cells, offsets, charges, task_first[0], task_second[0], kernel_taps)
    )
    pack = shape((2 * NE + rows + 8, 128), f32)
    store = vm((18 * places, atoms), f32)
    own, pk_lo, pk_hi, pos, lists, taps = call(
        functools.partial(spread_kernel, strips=strips),
        [shape((XO * YR, depth), f32), pack, pack, shape((rows, 128), f32)] + [shape((8, 128), f32)] * 2,
        [vm(x.shape, x.dtype) for x in inputs] + [vm((depth + 2 * PZ, 256), f32), dma((6,)), store],
        *inputs, task_count,
        hbm=range(6), smem=(6,),
    )
    up = shifted(pk_lo, "grp", -1)
    down = shifted(pk_hi, "grp", 1)
    far = [shifted(lists, "grp", d) for d in range(2, strips - 1)]

    force_shape = shape((3 * (places + 1) * 8, 128), f32)
    part_shape = shape((24 * (places + 1), 128), f32)
    pairs = [vm((128, 512), f32)] * UNROLL

    def sources(blocks):
        return vm((blocks * places * 8, 128), f32)

    table_shape = (2, XW * YR, terms * 256)
    line, edge_table, partial, force, parts = call(
        tables_kernel,
        [
            shape((2, terms, depth, depth), bf16),
            shape(table_shape, bf16),
            shape((XW * YR, depth), f32),
            force_shape,
            part_shape,
        ],
        [vm(table_shape, bf16), vm((2, terms * 256, depth), bf16), sources(1), *pairs, *pairs],
        taps, own, pos,
        flops=10**10,
    )

    tables = -(-strips * slots // 128)
    column = call(
        functools.partial(column_kernel, number_far=number_far, strips=strips, slots=slots),
        [shape((3 * rows + 8 * tables, 128), f32)],
        [],
        up, down, pos, lists, *far,
    )[0]
    above = shifted(column, "patch", -1)
    below = shifted(column, "patch", 1)

    up, column = lax.optimization_barrier((up, column))
    pack = shape((2 * NS, 128), f32)
    edge = shape((2 * N2, 128), f32)
    to_low, to_high, edge_low, edge_high, mid = call(
        planes_kernel,
        [pack, pack, edge, edge, shape((XO * YR, depth), f32)],
        [vm((2, terms * 256, depth), bf16)],
        up, down, line, edge_table, partial,
    )
    high = shifted(to_low, "patch", -1)
    low = shifted(to_high, "patch", 1)
    e_hi = shifted(edge_low, "patch", -2)
    e_lo = shifted(edge_high, "patch", 2)

    work = (8, 2 * 128 * tables + 128)
    force, work_near = call(
        functools.partial(near_kernel, strips=strips),
        [force_shape, shape(work, i32)],
        [pltpu.SMEM(work, i32), sources(3), dma, *pairs],
        column, pos, force, parts,
        flops=10**10,
    )

    force, work_across = call(
        functools.partial(far_kernel, strips=strips, places=places),
        [force_shape, shape(work, i32)],
        [pltpu.SMEM(work, i32), sources(6), dma, *pairs],
        column, below, above, force, parts,
        flops=10**10,
    )
    half, moved = call(
        sample_kernel,
        [shape((3, places, atoms), f32), shape((3 * places, 128), f32)],
        [
            vm((3, places, atoms), f32),
            vm((XO * YR, depth), f32),
            vm((depth + 2 * PZ, XO * YR), f32),
            store,
        ],
        cells, offsets, charges, masses, velocity, pos, force, mid, low, high, e_lo, e_hi,
    )

    moved_up = shifted(moved, "grp", -1)
    moved_down = shifted(moved, "grp", 1)
    own_high = shifted(moved, "patch", -1)
    own_low = shifted(moved, "patch", 1)
    force, parts = call(
        moved_self_kernel,
        [force_shape, part_shape],
        [sources(1), *pairs, *pairs],
        moved, pos,
        flops=10**10,
    )
    beside = jnp.concatenate([moved_down, moved_up], axis=0)
    moved_high = shifted(beside, "patch", -1)
    moved_low = shifted(beside, "patch", 1)
    force = call(
        moved_near_kernel,
        [force_shape],
        [sources(3), sources(6), *pairs],
        moved, moved_down, moved_up, own_low, own_high, column, below, above, force, parts, work_near, work_across,
        smem=(10, 11), flops=10**10,
    )[0]
    shown, speed = call(
        moved_far_kernel,
        [shape((3, places, atoms), f32)] * 2,
        [vm(force_shape.shape, f32), sources(6), *pairs],
        moved_low, moved_high, pos, below, above, force, parts, work_across, half, masses,
        smem=(7,),
    )
    return shown[:, None, None], speed[:, None, None]


def solution(mesh):
    placed = (
        P(None, "patch", "grp", None, None),
        P(None, "patch", "grp", None, None),
        P("patch", "grp", None, None),
        P("patch", "grp", None, None),
        P(None, "patch", "grp", None, None),
        P("patch", "grp", None),
        P("patch", "grp", None),
        P("patch", "grp"),
        P(),
    )
    return jax.shard_map(
        step,
        mesh=mesh,
        in_specs=placed,
        out_specs=(P(None, "patch", "grp", None, None), P(None, "patch", "grp", None, None)),
        check_vma=False,
    )
```
